32 devices in a mesh: dp: 8 (over z, y), mp: 4 (over x, core).
Axes of the slice: x: 2, y: 2, z: 4, core: 2. Of those that a mesh axis runs over, the one named last changes fastest.
Arguments:
- patches: bfloat16 [16384, 768], P(('dp', 'mp')), may hold values from -6 to 6
- conditioning: bfloat16 [16384, 768], P(('dp', 'mp')), may hold values from -6 to 6
- cotangent: bfloat16 [16384, 768], P(('dp', 'mp')), may hold values from -6 to 6
- segments: int32 [64, 256], P('dp'), may hold values from 0 to 3, never falling along the last dimension, each value on 1 to 128 neighbouring positions
- routes: int32 [16384, 2], P('dp'), may hold values from 0 to 7, all different within a row; in each aligned block of 2048 rows (0 to 2047, 2048 to 4095, ...) at most 768 rows name the same one
- gate_values: float32 [16384, 2], P('dp'), may hold values from 0.2 to 0.8
- ada_weight: bfloat16 [768, 4608], replicated, may hold values from -0.21875 to 0.21875
- ada_bias: float32 [4608], replicated, may hold values from -3 to 3
- qkv_weight: bfloat16 [768, 3, 768], P(None, None, 'mp'), may hold values from -0.21875 to 0.21875
- out_weight: bfloat16 [768, 768], P('mp'), may hold values from -1.75 to 1.75
- shared_up: bfloat16 [768, 3072], P(None, 'mp'), may hold values from -0.21875 to 0.21875
- shared_down: bfloat16 [3072, 768], P('mp'), may hold values from -0.109375 to 0.109375
- expert_up: bfloat16 [8, 768, 3072], P(None, None, 'mp'), may hold values from -0.21875 to 0.21875
- expert_down: bfloat16 [8, 3072, 768], P(None, 'mp'), may hold values from -0.109375 to 0.109375
Outputs:
- output: bfloat16 [16384, 768], P(('dp', 'mp'))
- patches_grad: float32 [16384, 768], P(('dp', 'mp'))
- conditioning_grad: float32 [16384, 768], P(('dp', 'mp'))
- ada_weight_grad: float32 [768, 4608], P('dp', 'mp')
- ada_bias_grad: float32 [4608], P(('dp', 'mp'))
- qkv_weight_grad: float32 [768, 3, 768], P('dp', None, 'mp')
- out_weight_grad: float32 [768, 768], P('mp', 'dp')
- shared_up_grad: float32 [768, 3072], P('dp', 'mp')
- shared_down_grad: float32 [3072, 768], P('mp', 'dp')
- expert_up_grad: float32 [8, 768, 3072], P(None, 'dp', 'mp')
- expert_down_grad: float32 [8, 3072, 768], P(None, 'mp', 'dp')
The draws below stay inside these ranges and needn't reach their ends.
Inputs may be any that keep to these rules, and one draw needn't show every extreme that they name: Each row names two different experts. In the patches of one index of dp (2048 rows of routes) no expert is named more than 768 times, a bound that some expert reaches in some such block. `segments`: along a row the numbers never fall; an image spans 1 to 128 patches of its row, some image exactly 128.
All inputs are finite; a program needn't handle non-finite values.
Results may differ from the reference program's by a relative error of at most 0.02.
The reference program's roundings to bfloat16 on the way count: a program that leaves them out, or rounds other values in their place, can miss the bound.
Values may be sent and summed in bfloat16 or wider, within the bound.
A program may use at most 320 MiB of HBM per device.

```python
import math
from functools import partial
import jax
import jax.numpy as jnp
import numpy as np
from jax import lax

D = 768
HEADS = 12
FF = 3072
EXPERTS = 8
SEQ = 256
ROWS_DP = 8
HEAD_DIM = 64
TOK_DP = 2048
CAP = 768
ROWS = 64
TOKENS = 16384
N_DP = 8


def levels(rng, dims, shards, smallest, top_value):
    def one(dim, parts):
        heights = jax.random.uniform(jax.random.fold_in(jax.random.fold_in(rng, 6), dim), (parts,), jnp.float32, smallest / len(shards), top_value / len(shards))
        return jnp.repeat(jnp.exp(heights), dims[dim] // parts).reshape((-1,) + (1,) * (len(dims) - dim - 1))

    loudness = one(*shards[0])
    for cut in shards[1:]:
        loudness = loudness * one(*cut)
    return loudness


def profile(count, total, reach, lean):
    portions = [(1 << 20) // math.isqrt(grade ** lean) + 1 for grade in range(2, count + 1)]
    rest, given = total - reach - (count - 1), [1] * (count - 1)
    while rest > 0:
        movable = [i for i in range(count - 1) if given[i] < reach]
        mass, budget = sum([portions[i] for i in movable]), rest
        for i in movable:
            extra = min(reach - given[i], max(1, budget * portions[i] // mass), rest)
            given[i] = given[i] + extra
            rest = rest - extra
    return np.array([reach] + given)


def uneven(rng, count, total, most, skew):
    if count == 2:
        one = jax.random.randint(rng, (), max(1, total - most), min(most, total - 1) + 1)
        return jnp.stack([one, total - one])
    sizes = jnp.asarray(profile(count, total, most, skew), jnp.int32)
    couples = (count - 1) // 2
    donor, taker = sizes[1:1 + 2 * couples:2], sizes[2:2 + 2 * couples:2]
    margin = jnp.minimum(donor - 1, most - taker)
    shifted = jax.random.randint(jax.random.fold_in(rng, 1), (couples,), 0, 1 << 20) % (margin + 1)
    sizes = sizes.at[1:1 + 2 * couples:2].set(donor - shifted).at[2:2 + 2 * couples:2].set(taker + shifted)
    return sizes[jax.random.permutation(jax.random.fold_in(rng, 2), count)]


def deal_out(key, own, number, rows, count, top, reach, lean):
    ranking = jax.random.permutation(key, count)
    packed, common = shares(count, rows * top, reach, lean, True), shares(count, rows * top, reach, lean, False)
    places = jnp.arange(count)

    def named(tallies, turn):
        used = int((tallies > 0).sum())
        fixed = max(1, used // 4)
        shifted = fixed + (places - fixed + turn * (used - fixed)) % max(1, count - fixed)
        return jnp.zeros((count,), jnp.int32).at[ranking[jnp.where(places < fixed, places, shifted)]].set(jnp.asarray(tallies, jnp.int32))

    tallies = jnp.where(number % 4 == 0, named(packed, number // 4), named(common, number - number // 4 - 1))
    mixed = jax.random.permutation(jax.random.fold_in(own, 3), count)
    giver, receiver = mixed[0:count // 2 * 2:2], mixed[1:count // 2 * 2:2]
    slack = jnp.minimum(tallies[giver] - 1, reach - tallies[receiver]) // 2
    slack = jnp.where((giver == ranking[0]) | (receiver == ranking[0]) | (tallies[receiver] == 0), 0, jnp.maximum(slack, 0))
    shifted = jax.random.randint(jax.random.fold_in(own, 4), (count // 2,), 0, 1 << 20) % (slack + 1)
    tallies = tallies.at[giver].add(-shifted).at[receiver].add(shifted)
    labels = jnp.searchsorted(jnp.cumsum(tallies), jnp.arange(rows * top), side="right").astype(jnp.int32)
    grid = labels.reshape(top, rows).T
    grid = grid[jax.random.permutation(jax.random.fold_in(own, 1), rows)]
    turn = jax.random.randint(jax.random.fold_in(own, 2), (rows, 1), 0, top)
    return jnp.take_along_axis(grid, (jnp.arange(top)[None, :] + turn) % top, axis=1)


def shares(number_of, total, bound, lean, full):
    portions = [(1 << 20) // math.isqrt(standing ** lean) + 1 for standing in range(1, number_of + 1)]
    largest = bound if full else min(bound, max(-(-total // number_of), total * portions[0] // sum(portions)))
    least = 1 if total - largest >= number_of - 1 else 0
    holding, surplus = [largest] + [least] * (number_of - 1), total - largest - least * (number_of - 1)
    while surplus > 0:
        free = [i for i in range(1, number_of) if holding[i] < largest] or [i for i in range(1, number_of) if holding[i] < bound]
        mass, remaining = sum([portions[i] for i in free]), surplus
        for i in free:
            extra = min(bound - holding[i], max(1, remaining * portions[i] // mass), surplus)
            holding[i] = holding[i] + extra
            surplus = surplus - extra
    return np.array(holding)


def gaussian(rng, dims, scale, limit, split=(), held_as=jnp.bfloat16):
    array = scale * jax.random.normal(rng, dims, jnp.float32)
    if split:
        array = array * levels(rng, dims, split, -0.22, 0.18)
    return jnp.clip(array, -limit, limit).astype(held_as)


def setup_inputs(seed: int = 0) -> dict:
    key_of = jax.random.split(jax.random.key(seed), 15)
    patches = gaussian(key_of[0], (TOKENS, D), 1.0, 6.0, ((0, 32),))
    conditioning = gaussian(key_of[1], (TOKENS, D), 1.0, 6.0, ((0, 32),))
    cotangent = gaussian(key_of[2], (TOKENS, D), 1.0, 6.0, ((0, 32),))
    segments = jax.vmap(lambda own: jnp.searchsorted(jnp.cumsum(uneven(own, 4, SEQ, SEQ // 2, 1)), jnp.arange(SEQ), side="right"))(jax.random.split(key_of[3], ROWS)).reshape((ROWS, SEQ)).astype(jnp.int32)
    routes_keys = jax.random.split(jax.random.fold_in(key_of[4], 1), TOKENS // TOK_DP)
    routes_turns = jax.random.permutation(jax.random.fold_in(key_of[4], 3), TOKENS // TOK_DP)
    routes = jax.vmap(lambda own, number: deal_out(jax.random.fold_in(key_of[4], 2), own, number, TOK_DP, EXPERTS, 2, CAP, 1))(routes_keys, routes_turns).reshape((TOKENS, 2))
    gate_values = jnp.clip(0.2 + 0.6 * jax.random.uniform(key_of[5], (TOKENS, 2), jnp.float32) ** levels(key_of[5], (TOKENS, 2), ((0, 8),), -0.2, 0.2), 0.2, 0.8)
    ada_weight = gaussian(key_of[6], (D, 6 * D), D ** -0.5, 0.21875)
    ada_bias = gaussian(key_of[7], (6 * D,), 0.5, 3.0, (), jnp.float32)
    qkv_weight = gaussian(key_of[8], (D, 3, D), D ** -0.5, 0.21875, ((2, 4),))
    out_weight = gaussian(key_of[9], (D, D), (D // 64) ** -0.5, 1.75, ((0, 4),))
    shared_up = gaussian(key_of[10], (D, FF), D ** -0.5, 0.21875, ((1, 4),))
    shared_down = gaussian(key_of[11], (FF, D), FF ** -0.5, 0.109375, ((0, 4),))
    expert_up = gaussian(key_of[12], (EXPERTS, D, FF), D ** -0.5, 0.21875, ((2, 4),))
    expert_down = gaussian(key_of[13], (EXPERTS, FF, D), FF ** -0.5, 0.109375, ((1, 4),))
    return dict(patches=patches, conditioning=conditioning, cotangent=cotangent, segments=segments, routes=routes, gate_values=gate_values, ada_weight=ada_weight, ada_bias=ada_bias, qkv_weight=qkv_weight, out_weight=out_weight, shared_up=shared_up, shared_down=shared_down, expert_up=expert_up, expert_down=expert_down)


@jax.custom_vjp
def low(v):
    return lax.optimization_barrier(v.astype(jnp.bfloat16)).astype(jnp.float32)

@jax.custom_vjp
def low_back(v):
    return v

def low_keep(v):
    return (low(v), None)

def low_pass(kept, grad):
    return (grad,)

def back_keep(v):
    return (v, None)

def back_low(kept, grad):
    return (low(grad),)
low.defvjp(low_keep, low_pass)
low_back.defvjp(back_keep, back_low)
highest = lax.Precision.HIGHEST

def layer_norm(values):
    center = values - lax.optimization_barrier(jnp.mean(values, axis=-1, keepdims=True))
    spread = lax.optimization_barrier(jnp.mean(center * center, axis=-1, keepdims=True))
    return center * lax.rsqrt(spread + 1e-06)

def route_tables(routes, experts, capacity):
    tokens = routes.shape[0]
    picks = routes.shape[1]
    flat = routes.reshape(-1).astype(jnp.int32)
    onehot = (flat[:, None] == jnp.arange(experts, dtype=jnp.int32)[None, :]).astype(jnp.int32)
    before = jnp.cumsum(onehot, axis=0) - onehot
    slot = lax.optimization_barrier(jnp.sum(before * onehot, axis=1)).astype(jnp.int32)
    place = (flat * capacity + slot).astype(jnp.int32)
    order = jnp.arange(picks * tokens, dtype=jnp.int32)
    token_of = jnp.full((experts * capacity,), tokens, jnp.int32).at[place].set((order // picks).astype(jnp.int32))
    return (place.reshape(tokens, picks), token_of)

def group_forward(patches, conditioning, segments, place, token_of, gate_values, weights):
    ada_weight, ada_bias, qkv_weight, out_weight, shared_up, shared_down, expert_up, expert_down = weights
    width = patches.shape[1]
    silu_cond = low(jax.nn.silu(conditioning))
    modulation = low_back(jnp.dot(silu_cond, ada_weight, precision=highest) + ada_bias[None, :])
    shift_one, scale_one, gate_one, shift_two, scale_two, gate_two = [modulation[:, number * width:(number + 1) * width] for number in range(6)]
    normed_one = low(layer_norm(patches) * (1.0 + scale_one) + shift_one)
    qkv = low(low_back(jnp.einsum('td,dcf->tcf', normed_one, qkv_weight, precision=highest)))
    row_count, seq_len = segments.shape
    qkv = qkv.reshape(row_count, seq_len, 3, HEADS, HEAD_DIM)
    queries = qkv[:, :, 0]
    key_rows = qkv[:, :, 1]
    value_rows = qkv[:, :, 2]
    scores = low_back(jnp.einsum('rqhe,rkhe->rhqk', queries, key_rows, precision=highest) * HEAD_DIM ** (-0.5))
    same = segments[:, None, :, None] == segments[:, None, None, :]
    masked = jnp.where(same, scores, -1000000000.0)
    top = lax.optimization_barrier(jnp.max(masked, axis=-1, keepdims=True))
    expo = jnp.exp(masked - top)
    probs = expo / lax.optimization_barrier(jnp.sum(expo, axis=-1, keepdims=True))
    light = low(probs)
    attended = jnp.einsum('rhqk,rkhe->rqhe', light, value_rows, precision=highest).reshape(-1, width)
    attended = low(low_back(attended))
    attn = low_back(jnp.dot(attended, out_weight, precision=highest))
    middle = patches + gate_one * attn
    normed_two = low(layer_norm(middle) * (1.0 + scale_two) + shift_two)
    shared_hidden = low(jax.nn.gelu(low_back(jnp.dot(normed_two, shared_up, precision=highest)), approximate=True))
    shared_out = jnp.dot(shared_hidden, shared_down, precision=highest)
    padded = jnp.concatenate([normed_two, jnp.zeros((1, width), normed_two.dtype)], axis=0)
    experts = expert_up.shape[0]
    dispatched = padded[token_of].reshape(experts, -1, width)
    expert_pre = low_back(jnp.einsum('ecd,edf->ecf', dispatched, expert_up, precision=highest))
    expert_hidden = low(jax.nn.gelu(expert_pre, approximate=True))
    expert_out = low_back(jnp.einsum('ecf,efd->ecd', expert_hidden, expert_down, precision=highest)).reshape(-1, width)
    routed = lax.optimization_barrier(jnp.sum(gate_values[:, :, None] * expert_out[place], axis=1))
    mlp = low_back(shared_out + routed)
    return middle + gate_two * mlp

def reference(patches, conditioning, cotangent, segments, routes, gate_values, ada_weight, ada_bias, qkv_weight, out_weight, shared_up, shared_down, expert_up, expert_down):
    f32 = jnp.float32
    weights = tuple((w.astype(f32) for w in (ada_weight, ada_bias, qkv_weight, out_weight, shared_up, shared_down, expert_up, expert_down)))
    patches32 = patches.astype(f32)
    cond32 = conditioning.astype(f32)
    gates32 = gate_values.astype(f32).reshape(N_DP, TOK_DP, 2)
    group_routes = routes.astype(jnp.int32).reshape(N_DP, TOK_DP, 2)
    place, token_of = jax.vmap(partial(route_tables, experts=EXPERTS, capacity=CAP))(group_routes)
    group_segments = segments.astype(jnp.int32).reshape(N_DP, ROWS_DP, SEQ)

    def forward(patches_all, cond_all, weight_set):

        def one_group(group):
            group_patches, group_cond, group_segs, group_place, group_token, group_gates = group
            return jax.checkpoint(group_forward)(group_patches, group_cond, group_segs, group_place, group_token, group_gates, weight_set)
        result = lax.map(one_group, (patches_all.reshape(N_DP, TOK_DP, D), cond_all.reshape(N_DP, TOK_DP, D), group_segments, place, token_of, gates32))
        return result.reshape(TOKENS, D)
    result, backward = jax.vjp(forward, patches32, cond32, weights)
    patches_grad, conditioning_grad, weight_grads = backward(cotangent.astype(f32))
    return (result.astype(jnp.bfloat16), patches_grad, conditioning_grad, weight_grads[0], weight_grads[1], weight_grads[2], weight_grads[3], weight_grads[4], weight_grads[5], weight_grads[6], weight_grads[7])
```

```python
import functools

import jax
import jax.numpy as jnp
from jax import lax
from jax.experimental import pallas as pl
from jax.experimental.pallas import tpu as pltpu
from jax.sharding import PartitionSpec as P

HEAD_DIM = 64
BF16 = jnp.bfloat16
F32 = jnp.float32
GELU_A = 0.7978845608028654
GELU_B = 0.044715


def nn(a, b):
    return lax.dot_general(a, b, (((1,), (0,)), ((), ())), preferred_element_type=F32)


def nt(a, b):
    return lax.dot_general(a, b, (((1,), (1,)), ((), ())), preferred_element_type=F32)


def tn(a, b):
    return lax.dot_general(a, b, (((0,), (0,)), ((), ())), preferred_element_type=F32)


def cost(flops, bytes_accessed, transcendentals):
    share = 16
    return pl.CostEstimate(
        flops=flops // share, bytes_accessed=bytes_accessed // share, transcendentals=transcendentals // share
    )


def swap(value, axis, mask):
    size = lax.axis_size(axis)
    return lax.ppermute(value, axis, [(i, i ^ mask) for i in range(size)])


def halves_evenly(n_dp, rows):
    return n_dp == 8 and rows % 16 == 0


def dp_steps(n_dp):
    return [("dp", 1 << bit) for bit in range(n_dp.bit_length() - 1)]


def block_order(steps):
    order = [(0, 0)]
    for axis, mask in reversed(steps):
        order = order + [(d ^ mask, m) if axis == "dp" else (d, m ^ mask) for d, m in order]
    return order


def flip(index, mask):
    bit = 1
    while bit <= mask:
        if mask & bit:
            index = index + bit * (1 - 2 * ((index // bit) % 2))
        bit *= 2
    return index


class Chain:
    def __init__(self, keep, send, steps):
        self.keep, self.send, self.steps, self.step = keep, send, steps, 0

    def take(self, results):
        if self.step == len(self.steps):
            self.result = results.pop(0)[0]
        else:
            self.keep, self.send = results.pop(0), results.pop(0)

    def advance(self):
        got = swap(self.send, *self.steps[self.step])
        total = self.keep.astype(F32) + got.astype(F32)
        half = total.shape[0] // 2
        self.step += 1
        self.take([total[:half].astype(BF16), total[half:].astype(BF16)] if half else [total])

    def finish(self):
        while self.step < len(self.steps):
            self.advance()
        return self.result


class Exchange:
    def __init__(self, jobs):
        self.jobs = jobs
        self.operands, self.in_specs, self.out_specs, self.shapes, self.scratch = [], [], [], [], []
        self.plans = []
        for chain, count in jobs:
            blocks, tail = chain.keep.shape[0], chain.keep.shape[1:]
            steps = chain.steps[chain.step : chain.step + count]
            final = chain.step + count == len(chain.steps)
            self.plans.append((steps, final, blocks, tail))
            self.operands += [chain.keep, chain.send]
            self.in_specs += [pl.BlockSpec(memory_space=pl.ANY)] * 2
            left = blocks >> (count if not final else count - 1)
            kept = jax.ShapeDtypeStruct((left,) + tail, F32 if final else BF16)
            outs = [kept] if final else [kept, kept]
            self.shapes += outs
            self.out_specs += [pl.BlockSpec(kept.shape, lambda *_: (0, 0, 0))] * len(outs)
            self.scratch.append(pltpu.VMEM((blocks,) + tail, BF16))
            self.scratch += [pltpu.VMEM((blocks >> n,) + tail, BF16) for n in range(count)]
            self.scratch += [
                pltpu.SemaphoreType.DMA((1,)),
                pltpu.SemaphoreType.DMA((count,)),
                pltpu.SemaphoreType.DMA((count,)),
            ]

    def bind(self, ins, outs, scratch):
        self.ins, self.outs, self.buffers, self.at = [], [], [], [0] * len(self.jobs)
        for n, (steps, final, _, _) in enumerate(self.plans):
            self.ins.append(ins[2 * n : 2 * n + 2])
            number = 1 if final else 2
            self.outs.append(outs[:number])
            outs = outs[number:]
            number = len(steps) + 4
            self.buffers.append(scratch[:number])
            scratch = scratch[number:]

    @staticmethod
    def partner(axis, mask):
        return {axis: flip(lax.axis_index(axis), mask)}

    def load(self, n):
        return pltpu.make_async_copy(self.ins[n][0], self.buffers[n][0], self.buffers[n][-3].at[0])

    def copy(self, n, step):
        steps, _, blocks, _ = self.plans[n]
        work, send_sems, recv_sems = self.buffers[n][0], self.buffers[n][-2], self.buffers[n][-1]
        number = blocks >> step
        source = self.ins[n][1] if step == 0 else work.at[pl.ds(number, number)]
        return pltpu.make_async_remote_copy(
            src_ref=source,
            dst_ref=self.buffers[n][1 + step],
            send_sem=send_sems.at[step],
            recv_sem=recv_sems.at[step],
            device_id=self.partner(*steps[step]),
            device_id_type=pl.DeviceIdType.MESH,
        )

    def begin(self):
        partners = sorted({step for steps, *_ in self.plans for step in steps})
        if partners:
            barrier = pltpu.get_barrier_semaphore()
            for step in partners:
                pl.semaphore_signal(
                    barrier, inc=1, device_id=self.partner(*step), device_id_type=pl.DeviceIdType.MESH
                )
            pl.semaphore_wait(barrier, len(partners))
        for n in range(len(self.jobs)):
            self.copy(n, 0).start()
            self.load(n).start()

    def advance(self, n):
        steps, final, blocks, _ = self.plans[n]
        step = self.at[n]
        self.at[n] += 1
        work, got = self.buffers[n][0], self.buffers[n][1 + step]
        number = blocks >> step
        if step == 0:
            self.load(n).wait()
        self.copy(n, step).wait()
        half = number // 2
        ending = step == len(steps) - 1

        def add(first, count, target, shift):
            def one(i, carry):
                total = work[i].astype(F32) + got[i].astype(F32)
                target[i - shift] = total.astype(target.dtype)
                return carry

            lax.fori_loop(first, first + count, one, 0)

        if ending and final:
            add(0, number, self.outs[n][0], 0)
        elif ending:
            add(0, half, self.outs[n][0], 0)
            add(half, half, self.outs[n][1], half)
        else:
            add(half, half, work, 0)
            self.copy(n, step + 1).start()
            add(0, half, work, 0)

    def early(self):
        for n, (steps, *_) in enumerate(self.plans):
            while self.at[n] < len(steps) - 1:
                self.advance(n)

    def finish(self):
        for step in range(max([len(steps) for steps, *_ in self.plans], default=0)):
            for n, (steps, *_) in enumerate(self.plans):
                if self.at[n] == step and step < len(steps):
                    self.advance(n)

    def spread(self, results):
        results = list(results)
        for chain, count in self.jobs:
            chain.step += count
            chain.take(results)


def remote(exchange, number, vmem):
    if not exchange.jobs:
        return pltpu.CompilerParams(vmem_limit_bytes=vmem << 20)
    return pltpu.CompilerParams(vmem_limit_bytes=vmem << 20, collective_id=number, has_side_effects=True)


def run_drain(jobs, number):
    exchange = Exchange(jobs)

    def body(*refs):
        ins = len(exchange.operands)
        outs = ins + len(exchange.shapes)
        exchange.bind(refs[:ins], refs[ins:outs], refs[outs:])
        exchange.begin()
        exchange.finish()

    exchange.spread(
        pl.pallas_call(
            body,
            grid=(1,),
            in_specs=exchange.in_specs,
            out_specs=exchange.out_specs,
            out_shape=exchange.shapes,
            scratch_shapes=exchange.scratch,
            compiler_params=remote(exchange, number, 60),
            name="drain",
        )(*exchange.operands)
    )


MP_STEPS = [("mp", 1), ("mp", 2)]
MP_ORDER = [m for _, m in block_order(MP_STEPS)]


def gather_mp(own):
    far = swap(own, "mp", 2)
    return [own, far, swap(own, "mp", 1), swap(far, "mp", 1)]


def normalize(values):
    center = values - jnp.mean(values, axis=-1, keepdims=True)
    inverse = lax.rsqrt(jnp.mean(center * center, axis=-1, keepdims=True) + 1e-06)
    return center * inverse, inverse


def normalize_back(normal, inverse, grad):
    return inverse * (
        grad
        - jnp.mean(grad, axis=-1, keepdims=True)
        - normal * jnp.mean(grad * normal, axis=-1, keepdims=True)
    )


def forward_kernel(
    heads, base, shift_one, scale_one, gate_one, shift_two, scale_two, seg_col, seg_row, *refs
):
    weights, out_weights = refs[:4], refs[4:8]
    normed_out, qkv, attended, lse_out, attn_out, second_out = refs[8], refs[9:13], *refs[13:]
    span = heads * HEAD_DIM
    x = base[...].astype(F32)
    normed = (normalize(x)[0] * (1.0 + scale_one[...]) + shift_one[...]).astype(BF16)
    normed_out[...] = normed
    same = seg_col[0] == seg_row[0]
    lane = lax.broadcasted_iota(jnp.int32, (1, 128), 1)
    lse_all = jnp.zeros(lse_out.shape, F32)
    attn = jnp.zeros(x.shape, F32)
    for block in range(4):
        qkv[block][...] = nn(normed, weights[block][...]).astype(BF16)
        for head in range(heads):
            at = head * HEAD_DIM
            q = qkv[block][:, at : at + HEAD_DIM]
            k = qkv[block][:, span + at : span + at + HEAD_DIM]
            v = qkv[block][:, 2 * span + at : 2 * span + at + HEAD_DIM]
            scores = jnp.where(same, nt(q, k) * (HEAD_DIM**-0.5), -1000000000.0)
            top = jnp.max(scores, axis=-1, keepdims=True)
            expo = jnp.exp(scores - top)
            total = jnp.sum(expo, axis=-1, keepdims=True)
            light = (expo * (1.0 / total)).astype(BF16)
            start = block * span + at
            attended[:, start : start + HEAD_DIM] = nn(light, v).astype(BF16)
            lse_all = jnp.where(lane == block * heads + head, top + jnp.log(total), lse_all)
        attn += nn(attended[:, block * span : (block + 1) * span], out_weights[block][...])
    lse_out[...] = lse_all
    attn_out[...] = attn
    middle = x + gate_one[...] * attn
    second_out[...] = (normalize(middle)[0] * (1.0 + scale_two[...]) + shift_two[...]).astype(BF16)


def rows_of(owner, rows):
    return pl.multiple_of(flip(lax.axis_index("dp"), owner) * rows, 8)


def store_blocks(order, m, total, halves, rows):
    half = len(order) // 2
    for place, owner in enumerate(order):
        if owner[1] == m:
            start = 0 if rows == total.shape[0] else rows_of(owner[0], rows)
            halves[place // half][place % half, :rows, :] = total[pl.ds(start, rows), :].astype(BF16)


def row_block(seq, columns):
    return pl.BlockSpec((seq, columns), lambda i, *_: (i, 0))


def column_block(seq, width, number):
    return pl.BlockSpec((seq, width), lambda i, *_: (i, number))


def whole_block(array):
    return pl.BlockSpec(array.shape, lambda i, *_: (0,) * array.ndim, pipeline_mode=pl.Buffered(1))


def segment_blocks(seq):
    return [
        pl.BlockSpec((1, seq, 1), lambda i, *_: (i, 0, 0)),
        pl.BlockSpec((1, 1, seq), lambda i, *_: (i, 0, 0)),
    ]


def run_forward(patches, modulation, segments, qkv_parts, out_parts):
    rows, seq = segments.shape
    tokens, width = patches.shape
    columns = qkv_parts[0].shape[1]
    heads = columns // (3 * HEAD_DIM)
    work = rows * 4 * heads * seq * seq
    shapes = (
        [(width, BF16)] + [(columns, BF16)] * 4 + [(width, BF16), (128, F32), (width, F32), (width, BF16)]
    )
    return pl.pallas_call(
        functools.partial(forward_kernel, heads),
        grid=(rows,),
        in_specs=[row_block(seq, width)]
        + [column_block(seq, width, n) for n in range(5)]
        + segment_blocks(seq)
        + [whole_block(w) for w in qkv_parts + out_parts],
        out_specs=[row_block(seq, c) for c, _ in shapes],
        out_shape=[jax.ShapeDtypeStruct((tokens, c), t) for c, t in shapes],
        compiler_params=pltpu.CompilerParams(vmem_limit_bytes=48 << 20),
        cost_estimate=cost(
            flops=4 * work * HEAD_DIM + 8 * tokens * width * width,
            bytes_accessed=40 * tokens * width,
            transcendentals=work,
        ),
        name="attention_half",
    )(
        patches,
        *([modulation] * 5),
        segments[:, :, None],
        segments[:, None, :],
        *qkv_parts,
        *out_parts,
    )


def middle_back_kernel(
    base, gate_one, scale_two, attn, cotangent, kept, got, _, middle_grad, attn_grad, pieces
):
    width = base.shape[1]
    grad = kept[0].astype(F32) + got[0].astype(F32)
    branch = attn[...]
    gate = gate_one[...]
    normal, inverse = normalize(base[...].astype(F32) + gate * branch)
    total = cotangent[...].astype(F32) + normalize_back(
        normal, inverse, grad * (1.0 + scale_two[...])
    )
    middle_grad[...] = total
    attn_grad[...] = (total * gate).astype(BF16)
    pieces[:, :width] = (total * branch).astype(BF16)
    pieces[:, width : 2 * width] = grad.astype(BF16)
    pieces[:, 2 * width :] = (grad * normal).astype(BF16)


def run_middle_back(patches, modulation, attn, cotangent, kept, got, after):
    tokens, width = patches.shape
    seq = tokens // 2
    wide = row_block(seq, width)
    return pl.pallas_call(
        middle_back_kernel,
        grid=(2,),
        in_specs=[
            wide,
            column_block(seq, width, 2),
            column_block(seq, width, 4),
            wide,
            wide,
            pl.BlockSpec((1, seq, width), lambda i: (0, i, 0)),
            pl.BlockSpec((1, seq, width), lambda i: (0, i, 0)),
            pl.BlockSpec(memory_space=pl.ANY),
        ],
        out_specs=[wide, wide, row_block(seq, 3 * width)],
        out_shape=[
            jax.ShapeDtypeStruct((tokens, width), F32),
            jax.ShapeDtypeStruct((tokens, width), BF16),
            jax.ShapeDtypeStruct((tokens, 3 * width), BF16),
        ],
        compiler_params=pltpu.CompilerParams(vmem_limit_bytes=32 << 20),
        cost_estimate=cost(
            flops=40 * tokens * width, bytes_accessed=36 * tokens * width, transcendentals=0
        ),
        name="middle_back",
    )(patches, modulation, modulation, attn, cotangent, kept, got, after)


def attention_back_kernel(
    heads, exchange, order, rows, base, scale_one, middle_grad, attn_grad, normed, attended, lse, seg_col, seg_row, *refs
):
    qkv, weights, out_weights = refs[:4], refs[4:8], refs[8:12]
    number = len(exchange.operands)
    moved, refs = refs[12 : 12 + number], refs[12 + number :]
    patches_grad, pieces, halves, refs = refs[0], refs[1], refs[2:4], refs[4:]
    number = len(exchange.shapes)
    moved_out, refs = refs[:number], refs[number:]
    totals, grad_qkv, refs = refs[:4], refs[4], refs[5:]
    step, last = pl.program_id(0), pl.num_programs(0) - 1
    exchange.bind(moved, moved_out, refs)

    @pl.when(step == 0)
    def _():
        exchange.begin()

    span = heads * HEAD_DIM
    width = base.shape[1]
    factor = HEAD_DIM**-0.5
    same = seg_col[0] == seg_row[0]
    upper = attn_grad[...]
    normed_grad = jnp.zeros(base.shape, F32)
    for block in range(4):
        if block == 3:

            @pl.when(step == last)
            def _():
                exchange.early()

        grad_heads = nt(upper, out_weights[block][...]).astype(BF16)
        for head in range(heads):
            at = head * HEAD_DIM
            n = block * heads + head
            q = qkv[block][:, at : at + HEAD_DIM]
            k = qkv[block][:, span + at : span + at + HEAD_DIM]
            v = qkv[block][:, 2 * span + at : 2 * span + at + HEAD_DIM]
            g = grad_heads[:, at : at + HEAD_DIM]
            scores = jnp.where(same, nt(q, k) * factor, -1000000000.0)
            probs = jnp.exp(scores - lse[:, n : n + 1])
            grad_probs = nt(g, v)
            term = jnp.sum(probs * grad_probs, axis=-1, keepdims=True)
            grad_scores = (probs * (grad_probs - term)).astype(BF16)
            grad_qkv[:, at : at + HEAD_DIM] = (nn(grad_scores, k) * factor).astype(BF16)
            grad_qkv[:, span + at : span + at + HEAD_DIM] = (tn(grad_scores, q) * factor).astype(BF16)
            grad_qkv[:, 2 * span + at : 2 * span + at + HEAD_DIM] = tn(
                probs.astype(BF16), g
            ).astype(BF16)
        made = grad_qkv[...]
        normed_grad += nt(made, weights[block][...])
        of_qkv = tn(normed[...], made)
        of_out = tn(upper, attended[:, block * span : (block + 1) * span])

        @pl.when(step == 0)
        def _():
            totals[block][:, : 3 * span] = of_qkv
            totals[block][:, 3 * span :] = of_out

        @pl.when(step > 0)
        def _():
            totals[block][:, : 3 * span] += of_qkv
            totals[block][:, 3 * span :] += of_out

        @pl.when(step == last)
        def _():
            store_blocks(order, MP_ORDER[block], totals[block], halves, rows)

    normal, inverse = normalize(base[...].astype(F32))
    patches_grad[...] = middle_grad[...] + normalize_back(
        normal, inverse, normed_grad * (1.0 + scale_one[...])
    )
    pieces[:, :width] = normed_grad.astype(BF16)
    pieces[:, width:] = (normed_grad * normal).astype(BF16)

    @pl.when(step == last)
    def _():
        exchange.finish()


def run_attention_back(
    patches,
    modulation,
    middle_grad,
    attn_grad,
    normed,
    attended,
    lse,
    segments,
    qkv,
    qkv_parts,
    out_parts,
    order,
    rows,
    jobs,
    number,
):
    count, seq = segments.shape
    tokens, width = patches.shape
    columns = qkv[0].shape[1]
    heads = columns // (3 * HEAD_DIM)
    work = count * 4 * heads * seq * seq
    wide = row_block(seq, width)
    half = (len(order) // 2, rows, 4 * columns // 3)
    exchange = Exchange(jobs)
    results = pl.pallas_call(
        functools.partial(attention_back_kernel, heads, exchange, order, rows),
        grid_spec=pltpu.PrefetchScalarGridSpec(
            num_scalar_prefetch=0,
            grid=(count,),
            in_specs=[wide, column_block(seq, width, 1), wide, wide, wide, wide, row_block(seq, 128)]
            + segment_blocks(seq)
            + [row_block(seq, columns)] * 4
            + [whole_block(w) for w in qkv_parts + out_parts]
            + exchange.in_specs,
            out_specs=[wide, row_block(seq, 2 * width)]
            + [pl.BlockSpec(half, lambda i, *_: (0, 0, 0))] * 2
            + exchange.out_specs,
            scratch_shapes=[pltpu.VMEM((width, 4 * columns // 3), F32)] * 4
            + [pltpu.VMEM((seq, columns), BF16)]
            + exchange.scratch,
        ),
        out_shape=[
            jax.ShapeDtypeStruct((tokens, width), F32),
            jax.ShapeDtypeStruct((tokens, 2 * width), BF16),
        ]
        + [jax.ShapeDtypeStruct(half, BF16)] * 2
        + exchange.shapes,
        compiler_params=remote(exchange, number, 62),
        cost_estimate=cost(
            flops=10 * work * HEAD_DIM + 16 * tokens * width * width,
            bytes_accessed=60 * tokens * width,
            transcendentals=work,
        ),
        name="attention_back",
    )(
        patches,
        modulation,
        middle_grad,
        attn_grad,
        normed,
        attended,
        lse,
        segments[:, :, None],
        segments[:, None, :],
        *qkv,
        *qkv_parts,
        *out_parts,
        *exchange.operands,
    )
    exchange.spread(results[4:])
    return results[:4]


BIAS_ROWS = 16


def ada_kernel(orders, rows, cond, *refs):
    pieces, bias, halves, total = refs[:4], refs[4], refs[5:9], refs[9]
    for m in range(4):
        for part in range(2):
            split = pieces[m].shape[1] // 2
            total[...] = tn(cond[...], pieces[m][:, part * split : (part + 1) * split])
            store_blocks(orders[part], m, total, halves[2 * part : 2 * part + 2], rows)
    half = len(orders[0]) // 2
    for place in range(len(orders[0])):
        halves[place // half][place % half, rows:, :] = jnp.broadcast_to(
            bias[place], (BIAS_ROWS, bias.shape[2])
        ).astype(BF16)


def run_ada(silu_cond, grad_modulation, bias, orders, pieces_of, rows):
    tokens, width = silu_cond.shape
    columns = grad_modulation.shape[1] // 4
    half = len(orders[0]) // 2
    shapes = [(half, rows + BIAS_ROWS, columns // 2)] * 2 + [(half, rows, columns // 2)] * 2

    def piece(m):
        return pl.BlockSpec((tokens, columns), lambda i, p: (0, p[m]))

    return pl.pallas_call(
        lambda _, *refs: ada_kernel(orders, rows, *refs),
        grid_spec=pltpu.PrefetchScalarGridSpec(
            num_scalar_prefetch=1,
            grid=(1,),
            in_specs=[whole_block(silu_cond)] + [piece(m) for m in range(4)] + [whole_block(bias)],
            out_specs=[pl.BlockSpec(shape, lambda i, *_: (0, 0, 0)) for shape in shapes],
            scratch_shapes=[pltpu.VMEM((width, columns // 2), F32)],
        ),
        out_shape=[jax.ShapeDtypeStruct(shape, BF16) for shape in shapes],
        compiler_params=pltpu.CompilerParams(vmem_limit_bytes=60 << 20),
        cost_estimate=cost(
            flops=8 * tokens * width * columns, bytes_accessed=20 * width * columns, transcendentals=0
        ),
        name="ada_grads",
    )(pieces_of, silu_cond, *([grad_modulation] * 4), bias)


def gelu_and_slope(values):
    square = values * values
    bent = jnp.tanh(values * (GELU_A + (GELU_A * GELU_B) * square))
    half = 0.5 * (1.0 + bent)
    active = values * half
    return active, half + active * (1.0 - bent) * (GELU_A + (3.0 * GELU_A * GELU_B) * square)


def expert_kernel(columns, first, last, grad_later, exchange, orders, rows, *refs):
    count = len(columns)
    gates, tokens, grads = refs[:3]
    ups, downs, refs = refs[3 : 3 + count], refs[3 + count : 3 + 2 * count], refs[3 + 2 * count :]
    if not first:
        old_out, old_back, refs = refs[0], refs[1], refs[2:]
    number = len(exchange.operands)
    moved, refs = refs[:number], refs[number:]
    halves, refs = refs[: 2 * count], refs[2 * count :]
    out, back, refs = refs[0], refs[1], refs[2:]
    number = len(exchange.shapes)
    moved_out, refs = refs[:number], refs[number:]
    number = 0 if grad_later else 2 * count
    sums, refs = refs[:number], refs[number:]
    step, final = pl.program_id(0), pl.num_programs(0) - 1
    exchange.bind(moved, moved_out, refs)

    @pl.when(step == 0)
    def _():
        exchange.begin()

    @pl.when(step == final)
    def _():
        exchange.early()

    if not grad_later:
        start_sums(step, sums)
    x = tokens[...]
    g32 = grads[...].astype(F32)
    routed = None if first else old_out[...]
    returned = None if first else old_back[...]
    for n, column in enumerate(columns):
        gate = gates[:, column : column + 1]
        slot_grad = (gate * g32).astype(BF16)
        pre = nn(x, ups[n][0])
        grad_hidden = nt(slot_grad, downs[n][0])
        hidden, slope = gelu_and_slope(pre)
        hidden = hidden.astype(BF16)
        grad_pre = (grad_hidden * slope).astype(BF16)
        one = gate * nn(hidden, downs[n][0])
        two = nt(grad_pre, ups[n][0])
        routed = one if routed is None else routed + one
        returned = two if returned is None else returned + two
        if grad_later:
            halves[2 * n][...] = hidden
            halves[2 * n + 1][...] = grad_pre
        else:
            sums[2 * n][...] += tn(x, grad_pre)
            sums[2 * n + 1][...] += tn(slot_grad, hidden)
    out[...] = routed.astype(out.dtype)
    back[...] = returned.astype(back.dtype)
    if not grad_later:
        store_halves(step, orders, sums, halves, rows)

    @pl.when(step == final)
    def _():
        exchange.finish()


def start_sums(step, sums):
    @pl.when(step == 0)
    def _():
        for total in sums:
            total[...] = jnp.zeros_like(total)


def store_halves(step, orders, sums, halves, rows):
    @pl.when(step == pl.num_programs(0) - 1)
    def _():
        for n, order in enumerate(orders):
            half = len(order) // 2
            for place, owner in enumerate(order):
                start = place * rows if half == 1 else rows_of(owner, rows)
                for part in range(2):
                    halves[2 * n + place // half][place % half, part * rows : (part + 1) * rows, :] = sums[
                        2 * n + part
                    ][pl.ds(start, rows), :].astype(BF16)


TILE = 512


def token_tiles(columns):
    return pl.BlockSpec((TILE, columns), lambda t: (t, 0))


def run_experts(columns, weights, orders, rows, gates, tokens, grads, sums, last, grad_later, jobs, number):
    count = len(columns)
    total, width = tokens.shape
    hidden = weights[0][0].shape[2]
    steps = total // TILE
    blocks = width // rows // 2
    first = sums is None
    exchange = Exchange(jobs)

    def weight(index, shape):
        return pl.BlockSpec((1,) + shape, lambda t: (index, 0, 0), pipeline_mode=pl.Buffered(1))

    in_specs = (
        [token_tiles(gates.shape[1]), token_tiles(width), token_tiles(width)]
        + [weight(i, (width, hidden)) for _, _, i in weights]
        + [weight(i, (hidden, width)) for _, _, i in weights]
        + ([] if first else [token_tiles(width), token_tiles(width)])
    )
    given = len(in_specs)
    if grad_later:
        half, half_shape = token_tiles(hidden), (total, hidden)
    else:
        half_shape = (blocks, 2 * rows, hidden)
        half = pl.BlockSpec(half_shape, lambda t: (0, 0, 0))
    made = 2 * count
    aliases = {} if first or last else {given - 2: made, given - 1: made + 1}
    results = pl.pallas_call(
        functools.partial(expert_kernel, columns, first, last, grad_later, exchange, orders, rows),
        grid_spec=pltpu.PrefetchScalarGridSpec(
            num_scalar_prefetch=0,
            grid=(steps,),
            in_specs=in_specs + exchange.in_specs,
            out_specs=[half] * made + [token_tiles(width), token_tiles(width)] + exchange.out_specs,
            scratch_shapes=([] if grad_later else [pltpu.VMEM((width, hidden), F32)] * (2 * count))
            + exchange.scratch,
        ),
        out_shape=[jax.ShapeDtypeStruct(half_shape, BF16)] * made
        + [jax.ShapeDtypeStruct((total, width), BF16 if last else F32)] * 2
        + exchange.shapes,
        input_output_aliases=aliases,
        compiler_params=remote(exchange, number, 60),
        cost_estimate=cost(
            flops=(8 if grad_later else 12) * count * total * width * hidden,
            bytes_accessed=20 * total * width + 8 * count * width * hidden,
            transcendentals=count * total * hidden,
        ),
        name=f"experts_{count}",
    )(
        gates,
        tokens,
        grads,
        *[up for up, _, _ in weights],
        *[down for _, down, _ in weights],
        *(() if first else sums),
        *exchange.operands,
    )
    exchange.spread(results[made + 2 :])
    return results[:made], results[made : made + 2]


def expert_grads_kernel(columns, exchange, waits, orders, rows, *refs):
    count = len(columns)
    gates, tokens, grads = refs[:3]
    saved, refs = refs[3 : 3 + 2 * count], refs[3 + 2 * count :]
    number = len(exchange.operands)
    moved, refs = refs[:number], refs[number + waits :]
    halves, refs = refs[: 2 * count], refs[2 * count :]
    number = len(exchange.shapes)
    moved_out, refs = refs[:number], refs[number:]
    sums, refs = refs[: 2 * count], refs[2 * count :]
    step, final = pl.program_id(0), pl.num_programs(0) - 1
    exchange.bind(moved, moved_out, refs)

    @pl.when(step == 0)
    def _():
        exchange.begin()

    start_sums(step, sums)
    x = tokens[...]
    g32 = grads[...].astype(F32)
    for n, column in enumerate(columns):
        slot_grad = (gates[:, column : column + 1] * g32).astype(BF16)
        sums[2 * n][...] += tn(x, saved[2 * n + 1][...])
        sums[2 * n + 1][...] += tn(slot_grad, saved[2 * n][...])
    store_halves(step, orders, sums, halves, rows)

    @pl.when(step == final)
    def _():
        exchange.finish()


def run_expert_grads(columns, saved, orders, rows, gates, tokens, grads, jobs, after, number):
    count = len(columns)
    total, width = tokens.shape
    hidden = saved[0].shape[1]
    steps = total // TILE
    half_shape = (width // rows // 2, 2 * rows, hidden)
    exchange = Exchange(jobs)
    results = pl.pallas_call(
        functools.partial(expert_grads_kernel, columns, exchange, len(after), orders, rows),
        grid_spec=pltpu.PrefetchScalarGridSpec(
            num_scalar_prefetch=0,
            grid=(steps,),
            in_specs=[token_tiles(gates.shape[1]), token_tiles(width), token_tiles(width)]
            + [token_tiles(hidden)] * (2 * count)
            + exchange.in_specs
            + [pl.BlockSpec(memory_space=pl.ANY)] * len(after),
            out_specs=[pl.BlockSpec(half_shape, lambda t: (0, 0, 0))] * (2 * count)
            + exchange.out_specs,
            scratch_shapes=[pltpu.VMEM((width, hidden), F32)] * (2 * count) + exchange.scratch,
        ),
        out_shape=[jax.ShapeDtypeStruct(half_shape, BF16)] * (2 * count) + exchange.shapes,
        compiler_params=remote(exchange, number, 60),
        cost_estimate=cost(
            flops=4 * count * total * width * hidden,
            bytes_accessed=(4 + 4 * count) * total * width,
            transcendentals=0,
        ),
        name="expert_grads",
    )(gates, tokens, grads, *saved, *exchange.operands, *after)
    exchange.spread(results[2 * count :])
    return results[: 2 * count]


def local(
    patches,
    conditioning,
    cotangent,
    segments,
    routes,
    gate_values,
    ada_weight,
    ada_bias,
    qkv_weight,
    out_weight,
    shared_up,
    shared_down,
    expert_up,
    expert_down,
):
    tokens, width = patches.shape
    group = routes.shape[0]
    experts = expert_up.shape[0]
    seq = segments.shape[1]
    n_dp, n_mp = lax.axis_size("dp"), lax.axis_size("mp")
    dp, mp = lax.axis_index("dp"), lax.axis_index("mp")
    rows = width // n_dp

    qkv_parts = gather_mp(qkv_weight.reshape(width, -1))
    out_parts = gather_mp(out_weight)

    cond32 = conditioning.astype(F32)
    silu_cond = jax.nn.silu(cond32).astype(BF16)
    modulation = jnp.dot(silu_cond, ada_weight, preferred_element_type=F32) + ada_bias[None, :]
    gate_one, gate_two = modulation[:, 2 * width : 3 * width], modulation[:, 5 * width :]
    grad_out = cotangent.astype(F32)
    grad_mlp = (grad_out * gate_two).astype(BF16)

    own_rows = tokens // seq
    own_segments = lax.dynamic_slice_in_dim(segments, mp * own_rows, own_rows, axis=0)
    results = run_forward(patches, modulation, own_segments, qkv_parts, out_parts)
    normed_one, qkv, attended, lse, attn_out, normed_two = results[0], results[1:5], *results[5:]

    grad_parts = gather_mp(grad_mlp)
    all_tokens = jnp.concatenate(gather_mp(normed_two), axis=0)
    all_grads = jnp.concatenate(grad_parts, axis=0)
    number = jnp.arange(16, dtype=jnp.int32)[None, :]
    gates = jnp.sum(
        jnp.where(routes[:, :, None] == number[:, None, :], gate_values[:, :, None], 0.0), axis=1
    )
    gates = jnp.where(number == experts, 1.0, gates)
    gates = jnp.concatenate(
        [lax.dynamic_slice_in_dim(gates, (mp ^ m) * tokens, tokens, axis=0) for m in MP_ORDER],
        axis=0,
    )
    shared = (shared_up[None], shared_down[None], 0)
    weights = {e: (expert_up, expert_down, e) for e in range(experts)}
    weights[experts] = shared
    calls = [(experts,)] + [(e, e + 1) for e in range(0, experts, 2)]
    even = halves_evenly(n_dp, rows)
    step = rows if even else width // 2
    reduced, chains, wholes = {}, {}, {}

    def steps_of(column):
        steps = dp_steps(n_dp)
        return [steps[1], steps[0]] + steps[2:] if column % 2 else steps

    def orders_of(columns):
        return [[d for d, _ in block_order(steps_of(c))] if even else [0, 1] for c in columns]

    def take_halves(columns, halves):
        for n, column in enumerate(columns):
            if even:
                chains[column] = Chain(halves[2 * n], halves[2 * n + 1], steps_of(column))
            else:
                wholes[column] = halves[2 * n : 2 * n + 2]

    def jobs(**counts):
        if not even:
            return []
        return [(chains[c], int(count[1:])) for count, columns in counts.items() for c in columns]

    sums = None
    riding = [
        {},
        dict(n2=(experts,)),
        dict(n2=(0, 1), n1=(experts,)),
        dict(n2=(2, 3), n1=(0, 1)),
        dict(n1=(4, 5)),
    ]
    for number, columns in enumerate(calls):
        last = number == len(calls) - 1
        halves, sums = run_experts(
            columns,
            [weights[c] for c in columns],
            orders_of(columns),
            step,
            gates,
            all_tokens,
            all_grads,
            sums,
            last,
            last,
            jobs(**riding[number]),
            number,
        )
        if last:
            saved = halves
        else:
            take_halves(columns, halves)
    out_sum, back_sum = [s.reshape(n_mp, tokens, width) for s in sums]
    half = n_mp // 2
    from_core = swap(back_sum[half:], "mp", 1)
    near = (back_sum[:half].astype(F32) + from_core.astype(F32)).astype(BF16)
    far = swap(near[1:], "mp", 2)
    halves = run_expert_grads(
        calls[-1],
        saved,
        orders_of(calls[-1]),
        step,
        gates,
        all_tokens,
        all_grads,
        jobs(n1=(4, 5, 2, 3)),
        [from_core],
        5,
    )
    take_halves(calls[-1], halves)
    middle_grad, attn_grad, pieces_two = run_middle_back(
        patches, modulation, attn_out, cotangent, near[:1], far, halves[0]
    )
    tail_steps = [MP_STEPS] * 3
    if even:
        y, z, rest = dp_steps(n_dp)[0], dp_steps(n_dp)[1], dp_steps(n_dp)[2:]
        core, x = MP_STEPS
        tail_steps = [[core, x, y, z] + rest, [core, z, x, y] + rest, [core, y, z, x] + rest]
    tail_orders = [block_order(steps) for steps in tail_steps]

    tail_rows = rows if even else width
    results = run_attention_back(
        patches,
        modulation,
        middle_grad,
        attn_grad,
        normed_one,
        attended,
        lse,
        own_segments,
        qkv,
        qkv_parts,
        out_parts,
        tail_orders[0],
        tail_rows,
        jobs(n2=(6, 7), n1=(4, 5)),
        6,
    )
    patches_grad, pieces_one, heads_halves = results[0], results[1], results[2:4]
    heads_chain = Chain(*heads_halves, tail_steps[0])
    out_chain = Chain(out_sum[:half], out_sum[half:], MP_STEPS)
    mlp_out = out_chain.finish()
    middle = patches.astype(F32) + gate_one * attn_out
    output = (middle + gate_two * mlp_out).astype(BF16)
    grad_gate_two = (grad_out * mlp_out).astype(BF16)
    grad_modulation = jnp.concatenate([pieces_one, pieces_two, grad_gate_two], axis=1)

    bias = jnp.sum(grad_modulation.astype(F32), axis=0).reshape(n_dp, n_mp, -1)
    if even:
        bias_of = bias[
            jnp.array([d for d, _ in tail_orders[1]]) ^ dp, jnp.array([m for _, m in tail_orders[1]]) ^ mp
        ][:, None]
    else:
        bias_of = jnp.zeros((n_mp, 1, 1), F32)
    piece = grad_modulation.shape[1] // n_mp
    bias_of = jnp.pad(bias_of, ((0, 0), (0, 0), (0, piece // 2 - bias_of.shape[2])))
    ada_halves = run_ada(
        silu_cond,
        grad_modulation,
        bias_of,
        tail_orders[1:],
        (jnp.arange(4, dtype=jnp.int32) ^ mp).astype(jnp.int32),
        tail_rows,
    )
    ada_chains = [Chain(*ada_halves[:2], tail_steps[1]), Chain(*ada_halves[2:], tail_steps[2])]
    cond_grad = nt(grad_modulation, ada_weight)
    _, silu_back = jax.vjp(jax.nn.silu, cond32)
    conditioning_grad = silu_back(cond_grad)[0]

    if even:
        run_drain([(heads_chain, 5)] + [(c, 5) for c in ada_chains] + jobs(n1=(6, 7)), 7)
    heads_sum = heads_chain.finish()
    low, high = [c.finish() for c in ada_chains]
    ada_sum = jnp.concatenate([low[:tail_rows], high], axis=1)
    if even:
        for column, chain in chains.items():
            part = chain.finish()
            reduced[column] = part[:rows], part[rows:]
        bias_sum = low[rows, : bias.shape[2]]
    else:
        for column, (first, second) in wholes.items():
            whole = jnp.stack([first[0], second[0]]).reshape(2, 2, step, -1)
            whole = jnp.swapaxes(whole, 0, 1).reshape(2, width, -1)
            part = lax.psum_scatter(whole, "dp", scatter_dimension=1, tiled=True).astype(F32)
            reduced[column] = part[0], part[1]
        heads_sum, ada_sum = [
            lax.psum_scatter(a.astype(BF16), "dp", scatter_dimension=0, tiled=True).astype(F32)
            for a in (heads_sum, ada_sum)
        ]
        bias_sum = lax.psum_scatter(
            lax.psum_scatter(bias, "dp", scatter_dimension=0, tiled=True), "mp", scatter_dimension=1, tiled=True
        )
    qkv_cols = qkv[0].shape[1]
    qkv_sum = heads_sum[:, :qkv_cols].reshape(rows, 3, -1)
    out_total = heads_sum[:, qkv_cols:].T
    up_sum, down_sum = reduced[experts]
    return (
        output,
        patches_grad,
        conditioning_grad,
        ada_sum,
        bias_sum.reshape(-1),
        qkv_sum,
        out_total,
        up_sum,
        down_sum.T,
        jnp.stack([reduced[e][0] for e in range(experts)]),
        jnp.stack([reduced[e][1].T for e in range(experts)]),
    )


def solution(mesh):
    in_specs = (
        P(("dp", "mp"), None),
        P(("dp", "mp"), None),
        P(("dp", "mp"), None),
        P("dp", None),
        P("dp", None),
        P("dp", None),
        P(),
        P(),
        P(None, None, "mp"),
        P("mp", None),
        P(None, "mp"),
        P("mp", None),
        P(None, None, "mp"),
        P(None, "mp", None),
    )
    out_specs = (
        P(("dp", "mp"), None),
        P(("dp", "mp"), None),
        P(("dp", "mp"), None),
        P("dp", "mp"),
        P(("dp", "mp")),
        P("dp", None, "mp"),
        P("mp", "dp"),
        P("dp", "mp"),
        P("mp", "dp"),
        P(None, "dp", "mp"),
        P(None, "mp", "dp"),
    )
    return jax.shard_map(local, mesh=mesh, in_specs=in_specs, out_specs=out_specs, check_vma=False)
```

```python
import functools

import jax
import jax.numpy as jnp
from jax import lax
from jax.experimental import pallas as pl
from jax.experimental.pallas import tpu as pltpu
from jax.sharding import PartitionSpec as P

HEAD_DIM = 64
BF16 = jnp.bfloat16
F32 = jnp.float32
GELU_A = 0.7978845608028654
GELU_B = 0.044715


def nn(a, b):
    return lax.dot_general(a, b, (((1,), (0,)), ((), ())), preferred_element_type=F32)


def nt(a, b):
    return lax.dot_general(a, b, (((1,), (1,)), ((), ())), preferred_element_type=F32)


def tn(a, b):
    return lax.dot_general(a, b, (((0,), (0,)), ((), ())), preferred_element_type=F32)


def cost(flops, bytes_accessed, transcendentals):
    share = 16
    return pl.CostEstimate(
        flops=flops // share, bytes_accessed=bytes_accessed // share, transcendentals=transcendentals // share
    )


def swap(value, axis, mask):
    size = lax.axis_size(axis)
    return lax.ppermute(value, axis, [(i, i ^ mask) for i in range(size)])


def halves_evenly(n_dp, rows):
    return n_dp == 8 and rows % 16 == 0


def dp_steps(n_dp):
    return [("dp", 1 << bit) for bit in range(n_dp.bit_length() - 1)]


def block_order(steps):
    order = [(0, 0)]
    for axis, mask in reversed(steps):
        order = order + [(d ^ mask, m) if axis == "dp" else (d, m ^ mask) for d, m in order]
    return order


def flip(index, mask):
    bit = 1
    while bit <= mask:
        if mask & bit:
            index = index + bit * (1 - 2 * ((index // bit) % 2))
        bit *= 2
    return index


class Chain:
    def __init__(self, keep, send, steps, done=0):
        self.keep, self.send, self.steps, self.step = keep, send, steps, done
        self.shape = None if keep is None else keep.shape

    @classmethod
    def inside(cls, shape, steps):
        chain = cls(None, None, steps)
        chain.shape = shape
        return chain

    def take(self, results):
        if self.step == len(self.steps):
            self.result = results.pop(0)[0]
        else:
            self.keep, self.send = results.pop(0), results.pop(0)
            self.shape = self.keep.shape

    def advance(self):
        got = swap(self.send, *self.steps[self.step])
        total = self.keep.astype(F32) + got.astype(F32)
        half = total.shape[0] // 2
        self.step += 1
        self.take([total[:half].astype(BF16), total[half:].astype(BF16)] if half else [total])

    def finish(self):
        while self.step < len(self.steps):
            self.advance()
        return self.result


class Exchange:
    def __init__(self, jobs, sunk=False):
        self.jobs, self.sunk, self.sinks = jobs, sunk, {}
        self.operands, self.in_specs, self.out_specs, self.shapes, self.scratch = [], [], [], [], []
        self.plans = []
        for chain, count in jobs:
            blocks, tail = chain.shape[0], chain.shape[1:]
            steps = chain.steps[chain.step : chain.step + count]
            final = chain.step + count == len(chain.steps)
            self.plans.append((steps, final, blocks, chain.keep is None))
            if chain.keep is None:
                self.scratch.append(pltpu.VMEM(chain.shape, BF16))
            else:
                self.operands += [chain.keep, chain.send]
                self.in_specs += [pl.BlockSpec(memory_space=pl.ANY)] * 2
            left = blocks >> (count if not final else count - 1)
            kept = jax.ShapeDtypeStruct((left,) + tail, F32 if final else BF16)
            outs = [] if final and sunk else [kept] if final else [kept, kept]
            self.shapes += outs
            self.out_specs += [pl.BlockSpec(kept.shape, lambda *_: (0, 0, 0))] * len(outs)
            self.scratch.append(pltpu.VMEM((blocks,) + tail, BF16))
            self.scratch += [pltpu.VMEM((blocks >> n,) + tail, BF16) for n in range(count)]
            self.scratch += [
                pltpu.SemaphoreType.DMA((1,)),
                pltpu.SemaphoreType.DMA((count,)),
                pltpu.SemaphoreType.DMA((count,)),
            ]

    def bind(self, ins, outs, scratch):
        self.ins, self.outs, self.buffers, self.at = [], [], [], [0] * len(self.jobs)
        for steps, final, _, inner in self.plans:
            number = 0 if final and self.sunk else 1 if final else 2
            self.outs.append(outs[:number])
            outs = outs[number:]
            if inner:
                self.ins.append([None, scratch[0]])
                scratch = scratch[1:]
            else:
                self.ins.append(ins[:2])
                ins = ins[2:]
            number = len(steps) + 4
            self.buffers.append(scratch[:number])
            scratch = scratch[number:]

    @staticmethod
    def partner(axis, mask):
        return {axis: flip(lax.axis_index(axis), mask)}

    def load(self, n):
        return pltpu.make_async_copy(self.ins[n][0], self.buffers[n][0], self.buffers[n][-3].at[0])

    def copy(self, n, step):
        steps, _, blocks, _ = self.plans[n]
        work, send_sems, recv_sems = self.buffers[n][0], self.buffers[n][-2], self.buffers[n][-1]
        number = blocks >> step
        source = self.ins[n][1] if step == 0 else work.at[pl.ds(number, number)]
        return pltpu.make_async_remote_copy(
            src_ref=source,
            dst_ref=self.buffers[n][1 + step],
            send_sem=send_sems.at[step],
            recv_sem=recv_sems.at[step],
            device_id=self.partner(*steps[step]),
            device_id_type=pl.DeviceIdType.MESH,
        )

    def begin(self, others=()):
        partners = sorted({step for steps, *_ in self.plans for step in steps} | set(others))
        if partners:
            barrier = pltpu.get_barrier_semaphore()
            for step in partners:
                pl.semaphore_signal(
                    barrier, inc=1, device_id=self.partner(*step), device_id_type=pl.DeviceIdType.MESH
                )
            pl.semaphore_wait(barrier, len(partners))
        for n, (*_, inner) in enumerate(self.plans):
            if not inner:
                self.copy(n, 0).start()
                self.load(n).start()

    def halves(self, n):
        return self.buffers[n][0], self.ins[n][1]

    def start(self, n):
        self.copy(n, 0).start()

    def advance(self, n):
        steps, final, blocks, inner = self.plans[n]
        step = self.at[n]
        self.at[n] += 1
        work, got = self.buffers[n][0], self.buffers[n][1 + step]
        number = blocks >> step
        if step == 0 and not inner:
            self.load(n).wait()
        self.copy(n, step).wait()
        half = number // 2
        ending = step == len(steps) - 1

        def add(first, count, target, shift):
            def one(i, carry):
                total = work[i].astype(F32) + got[i].astype(F32)
                target[i - shift] = total.astype(target.dtype)
                return carry

            lax.fori_loop(first, first + count, one, 0)

        if ending and final and self.sunk:
            self.sinks[n](work[0].astype(F32) + got[0].astype(F32))
        elif ending and final:
            add(0, number, self.outs[n][0], 0)
        elif ending:
            add(0, half, self.outs[n][0], 0)
            add(half, half, self.outs[n][1], half)
        else:
            add(half, half, work, 0)
            self.copy(n, step + 1).start()
            add(0, half, work, 0)

    def left(self, n):
        return len(self.plans[n][0]) - self.at[n]

    def all_once(self):
        for n in range(len(self.jobs)):
            self.advance(n)

    def early(self, first=0, last=None):
        for n, (steps, *_) in list(enumerate(self.plans))[first:last]:
            while self.at[n] < len(steps) - 1:
                self.advance(n)

    def finish(self):
        for step in range(max([len(steps) for steps, *_ in self.plans], default=0)):
            for n, (steps, *_) in enumerate(self.plans):
                if self.at[n] == step and step < len(steps):
                    self.advance(n)

    def spread(self, results):
        results = list(results)
        for chain, count in self.jobs:
            chain.step += count
            if not (self.sunk and chain.step == len(chain.steps)):
                chain.take(results)


def remote(exchange, number, vmem, always=False):
    if not (exchange.jobs or always):
        return pltpu.CompilerParams(vmem_limit_bytes=vmem << 20)
    return pltpu.CompilerParams(vmem_limit_bytes=vmem << 20, collective_id=number, has_side_effects=True)


MP_STEPS = [("mp", 1), ("mp", 2)]
MP_ORDER = [m for _, m in block_order(MP_STEPS)]


def gather_mp(own):
    far = swap(own, "mp", 2)
    return [own, far, swap(own, "mp", 1), swap(far, "mp", 1)]


def normalize(values):
    center = values - jnp.mean(values, axis=-1, keepdims=True)
    inverse = lax.rsqrt(jnp.mean(center * center, axis=-1, keepdims=True) + 1e-06)
    return center * inverse, inverse


def normalize_back(normal, inverse, grad):
    return inverse * (
        grad
        - jnp.mean(grad, axis=-1, keepdims=True)
        - normal * jnp.mean(grad * normal, axis=-1, keepdims=True)
    )


def forward_kernel(
    heads, base, shift_one, scale_one, gate_one, shift_two, scale_two, seg_col, seg_row, *refs
):
    weights, out_weights = refs[:4], refs[4:8]
    normed_out, qkv, attended, lse_out, attn_out, second_out = refs[8], refs[9:13], *refs[13:]
    span = heads * HEAD_DIM
    x = base[...].astype(F32)
    normed = (normalize(x)[0] * (1.0 + scale_one[...]) + shift_one[...]).astype(BF16)
    normed_out[...] = normed
    same = seg_col[0] == seg_row[0]
    lane = lax.broadcasted_iota(jnp.int32, (1, 128), 1)
    lse_all = jnp.zeros(lse_out.shape, F32)
    attn = jnp.zeros(x.shape, F32)
    for block in range(4):
        qkv[block][...] = nn(normed, weights[block][...]).astype(BF16)
        for head in range(heads):
            at = head * HEAD_DIM
            q = qkv[block][:, at : at + HEAD_DIM]
            k = qkv[block][:, span + at : span + at + HEAD_DIM]
            v = qkv[block][:, 2 * span + at : 2 * span + at + HEAD_DIM]
            scores = jnp.where(same, nt(q, k) * (HEAD_DIM**-0.5), -1000000000.0)
            top = jnp.max(scores, axis=-1, keepdims=True)
            expo = jnp.exp(scores - top)
            total = jnp.sum(expo, axis=-1, keepdims=True)
            light = (expo * (1.0 / total)).astype(BF16)
            start = block * span + at
            attended[:, start : start + HEAD_DIM] = nn(light, v).astype(BF16)
            lse_all = jnp.where(lane == block * heads + head, top + jnp.log(total), lse_all)
        attn += nn(attended[:, block * span : (block + 1) * span], out_weights[block][...])
    lse_out[...] = lse_all
    attn_out[...] = attn
    middle = x + gate_one[...] * attn
    second_out[...] = (normalize(middle)[0] * (1.0 + scale_two[...]) + shift_two[...]).astype(BF16)


def rows_of(owner, rows):
    return pl.multiple_of(flip(lax.axis_index("dp"), owner) * rows, 8)


def store_blocks(order, m, total, halves, rows, columns=slice(None)):
    half = len(order) // 2
    for place, owner in enumerate(order):
        if owner[1] == m:
            start = 0 if rows == total.shape[0] else rows_of(owner[0], rows)
            halves[place // half][place % half, :rows, :] = total[pl.ds(start, rows), columns].astype(BF16)


def row_block(seq, columns):
    return pl.BlockSpec((seq, columns), lambda i, *_: (i, 0))


def column_block(seq, width, number):
    return pl.BlockSpec((seq, width), lambda i, *_: (i, number))


def whole_block(array):
    return pl.BlockSpec(array.shape, lambda i, *_: (0,) * array.ndim, pipeline_mode=pl.Buffered(1))


def segment_blocks(seq):
    return [
        pl.BlockSpec((1, seq, 1), lambda i, *_: (i, 0, 0)),
        pl.BlockSpec((1, 1, seq), lambda i, *_: (i, 0, 0)),
    ]


def run_forward(patches, modulation, segments, qkv_parts, out_parts):
    rows, seq = segments.shape
    tokens, width = patches.shape
    columns = qkv_parts[0].shape[1]
    heads = columns // (3 * HEAD_DIM)
    work = rows * 4 * heads * seq * seq
    shapes = (
        [(width, BF16)] + [(columns, BF16)] * 4 + [(width, BF16), (128, F32), (width, F32), (width, BF16)]
    )
    return pl.pallas_call(
        functools.partial(forward_kernel, heads),
        grid=(rows,),
        in_specs=[row_block(seq, width)]
        + [column_block(seq, width, n) for n in range(5)]
        + segment_blocks(seq)
        + [whole_block(w) for w in qkv_parts + out_parts],
        out_specs=[row_block(seq, c) for c, _ in shapes],
        out_shape=[jax.ShapeDtypeStruct((tokens, c), t) for c, t in shapes],
        compiler_params=pltpu.CompilerParams(vmem_limit_bytes=48 << 20),
        cost_estimate=cost(
            flops=4 * work * HEAD_DIM + 8 * tokens * width * width,
            bytes_accessed=40 * tokens * width,
            transcendentals=work,
        ),
        name="attention_half",
    )(
        patches,
        *([modulation] * 5),
        segments[:, :, None],
        segments[:, None, :],
        *qkv_parts,
        *out_parts,
    )


def attention_back_kernel(
    heads,
    exchange,
    order,
    rows,
    base,
    scale_one,
    gate_one,
    scale_two,
    attn,
    cotangent,
    summed,
    normed,
    attended,
    lse,
    seg_col,
    seg_row,
    *refs,
):
    qkv, weights, out_weights = refs[:4], refs[4:8], refs[8:12]
    number = len(exchange.operands)
    moved, refs = refs[12 : 12 + number], refs[12 + number :]
    patches_grad, pieces, halves, refs = refs[0], refs[1], refs[2:4], refs[4:]
    number = len(exchange.shapes)
    moved_out, refs = refs[:number], refs[number:]
    totals, grad_qkv, refs = refs[:4], refs[4], refs[5:]
    step, last = pl.program_id(0), pl.num_programs(0) - 1
    exchange.bind(moved, moved_out, refs)

    @pl.when(step == 0)
    def _():
        exchange.begin()

    span = heads * HEAD_DIM
    width = base.shape[1]
    factor = HEAD_DIM**-0.5
    same = seg_col[0] == seg_row[0]
    grad, branch, gate = summed[...], attn[...], gate_one[...]
    normal, inverse = normalize(base[...].astype(F32) + gate * branch)
    middle_grad = cotangent[...].astype(F32) + normalize_back(
        normal, inverse, grad * (1.0 + scale_two[...])
    )
    patches_grad[...] = middle_grad
    pieces[:, 2 * width : 3 * width] = (middle_grad * branch).astype(BF16)
    pieces[:, 3 * width : 4 * width] = grad.astype(BF16)
    pieces[:, 4 * width :] = (grad * normal).astype(BF16)
    upper = (middle_grad * gate).astype(BF16)
    normed_grad = jnp.zeros(base.shape, F32)
    for block in range(4):
        if block == 0:

            @pl.when(step == last)
            def _():
                exchange.early(0, 1)

        if block == 2:

            @pl.when(step == last)
            def _():
                exchange.early(1)

        grad_heads = nt(upper, out_weights[block][...]).astype(BF16)
        for head in range(heads):
            at = head * HEAD_DIM
            n = block * heads + head
            q = qkv[block][:, at : at + HEAD_DIM]
            k = qkv[block][:, span + at : span + at + HEAD_DIM]
            v = qkv[block][:, 2 * span + at : 2 * span + at + HEAD_DIM]
            g = grad_heads[:, at : at + HEAD_DIM]
            scores = jnp.where(same, nt(q, k) * factor, -1000000000.0)
            probs = jnp.exp(scores - lse[:, n : n + 1])
            grad_probs = nt(g, v)
            term = jnp.sum(probs * grad_probs, axis=-1, keepdims=True)
            grad_scores = (probs * (grad_probs - term)).astype(BF16)
            grad_qkv[:, at : at + HEAD_DIM] = (nn(grad_scores, k) * factor).astype(BF16)
            grad_qkv[:, span + at : span + at + HEAD_DIM] = (tn(grad_scores, q) * factor).astype(BF16)
            grad_qkv[:, 2 * span + at : 2 * span + at + HEAD_DIM] = tn(
                probs.astype(BF16), g
            ).astype(BF16)
        made = grad_qkv[...]
        normed_grad += nt(made, weights[block][...])
        of_qkv = tn(normed[...], made)
        of_out = tn(upper, attended[:, block * span : (block + 1) * span])

        @pl.when(step == 0)
        def _():
            totals[block][:, : 3 * span] = of_qkv
            totals[block][:, 3 * span :] = of_out

        @pl.when(step > 0)
        def _():
            totals[block][:, : 3 * span] += of_qkv
            totals[block][:, 3 * span :] += of_out

        @pl.when(step == last)
        def _():
            store_blocks(order, MP_ORDER[block], totals[block], halves, rows)

    normal, inverse = normalize(base[...].astype(F32))
    patches_grad[...] += normalize_back(normal, inverse, normed_grad * (1.0 + scale_one[...]))
    pieces[:, :width] = normed_grad.astype(BF16)
    pieces[:, width : 2 * width] = (normed_grad * normal).astype(BF16)

    @pl.when(step == last)
    def _():
        exchange.finish()


def run_attention_back(
    patches,
    modulation,
    attn,
    cotangent,
    summed,
    normed,
    attended,
    lse,
    segments,
    qkv,
    qkv_parts,
    out_parts,
    order,
    rows,
    jobs,
    number,
):
    count, seq = segments.shape
    tokens, width = patches.shape
    columns = qkv[0].shape[1]
    heads = columns // (3 * HEAD_DIM)
    work = count * 4 * heads * seq * seq
    wide = row_block(seq, width)
    half = (len(order) // 2, rows, 4 * columns // 3)
    exchange = Exchange(jobs)
    results = pl.pallas_call(
        functools.partial(attention_back_kernel, heads, exchange, order, rows),
        grid_spec=pltpu.PrefetchScalarGridSpec(
            num_scalar_prefetch=0,
            grid=(count,),
            in_specs=[wide]
            + [column_block(seq, width, n) for n in (1, 2, 4)]
            + [wide] * 5
            + [row_block(seq, 128)]
            + segment_blocks(seq)
            + [row_block(seq, columns)] * 4
            + [whole_block(w) for w in qkv_parts + out_parts]
            + exchange.in_specs,
            out_specs=[wide, row_block(seq, 5 * width)]
            + [pl.BlockSpec(half, lambda i, *_: (0, 0, 0))] * 2
            + exchange.out_specs,
            scratch_shapes=[pltpu.VMEM((width, 4 * columns // 3), F32)] * 4
            + [pltpu.VMEM((seq, columns), BF16)]
            + exchange.scratch,
        ),
        out_shape=[
            jax.ShapeDtypeStruct((tokens, width), F32),
            jax.ShapeDtypeStruct((tokens, 5 * width), BF16),
        ]
        + [jax.ShapeDtypeStruct(half, BF16)] * 2
        + exchange.shapes,
        compiler_params=remote(exchange, number, 62),
        cost_estimate=cost(
            flops=10 * work * HEAD_DIM + 16 * tokens * width * width,
            bytes_accessed=60 * tokens * width,
            transcendentals=work,
        ),
        name="attention_back",
    )(
        patches,
        *([modulation] * 3),
        attn,
        cotangent,
        summed,
        normed,
        attended,
        lse,
        segments[:, :, None],
        segments[:, None, :],
        *qkv,
        *qkv_parts,
        *out_parts,
        *exchange.operands,
    )
    exchange.spread(results[4:])
    return results[:4]


BIAS_ROWS = 16


def tail_kernel(
    orders,
    rows,
    exchange,
    cond,
    silu_cond,
    base,
    attn,
    gate_one,
    gate_two,
    cotangent,
    mlp,
    pieces,
    weight,
    *refs,
):
    number = len(exchange.operands)
    moved, refs = refs[:number], refs[number:]
    cond_grad, output, qkv_grad, out_grad, ada_grad, bias_grad, refs = *refs[:6], refs[6:]
    number = len(exchange.jobs) - 3
    late, refs = refs[:number], refs[number:]
    modulation_grad, weight_here, total, load_sems, refs = *refs[:4], refs[4:]
    exchange.bind(moved, (), refs)
    tokens, width = base.shape
    pieces_load = pltpu.make_async_copy(
        pieces, modulation_grad.at[:, pl.ds(0, pieces.shape[1])], load_sems.at[0]
    )
    weight_load = pltpu.make_async_copy(weight, weight_here, load_sems.at[1])
    pieces_load.start()
    weight_load.start()
    exchange.begin()
    grad_out, branch = cotangent[...].astype(F32), mlp[...]
    modulation_grad[:, 5 * width :] = (grad_out * branch).astype(BF16)
    middle = base[...].astype(F32) + gate_one[...] * attn[...]
    output[...] = (middle + gate_two[...] * branch).astype(BF16)
    pieces_load.wait()

    columns = modulation_grad.shape[1] // 4
    split = columns // 2
    heads = qkv_grad.shape[1]
    mp = lax.axis_index("mp")

    def keep_heads(value):
        qkv_grad[...] = value[:, :heads]
        out_grad[...] = value[:, heads:]

    def keep_low(value):
        ada_grad[:, :split] = value[:rows]
        bias_grad[...] = value[rows:]

    def keep_high(value):
        ada_grad[:, split:] = value

    def keep_late(target, value):
        target[...] = value

    exchange.sinks = {0: keep_low, 1: keep_high, 2: keep_heads}
    for n, target in enumerate(late):
        exchange.sinks[3 + n] = functools.partial(keep_late, target)
    bias = jnp.sum(modulation_grad[...].astype(F32), axis=0, keepdims=True).astype(BF16)
    lines = [bias[:, n * split : (n + 1) * split] for n in range(8)]
    lines = jnp.concatenate(lines + [jnp.zeros_like(lines[0])] * (BIAS_ROWS - 8), axis=0)
    for place in range(len(orders[0])):
        half = len(orders[0]) // 2
        exchange.halves(0)[place // half][place % half, rows:, :] = lines
    half = MP_ORDER[len(MP_ORDER) // 2 :]
    for m in half + [m for m in MP_ORDER if m not in half]:
        first = pl.multiple_of(flip(mp, m) * columns, 128)
        total[...] = tn(silu_cond[...], modulation_grad[:, pl.ds(first, columns)])
        for part, order in enumerate(orders):
            own = slice(part * split, (part + 1) * split)
            store_blocks(order, m, total, exchange.halves(part), rows, own)
        if m == half[0]:
            exchange.advance(2)
        if m == half[-1]:
            exchange.start(0)
            exchange.start(1)
    exchange.advance(0)
    exchange.advance(1)
    weight_load.wait()
    value = cond[...].astype(F32)
    gate = 1.0 / (1.0 + jnp.exp(-value))
    cond_grad[...] = nt(modulation_grad[...], weight_here[...]) * (gate * (1.0 + value * (1.0 - gate)))
    for n in (2, 0, 1, 2):
        exchange.advance(n) if exchange.left(n) > 1 else None
    for n in range(len(late)):
        exchange.advance(3 + n)
    for n in (0, 2, 1):
        exchange.advance(n) if exchange.left(n) > 1 else None
    exchange.finish()


def run_tail(
    conditioning, silu_cond, patches, attn, modulation, cotangent, mlp, pieces, ada_weight, orders, rows, jobs, number
):
    tokens, width = silu_cond.shape
    exchange = Exchange(jobs, True)
    anywhere = pl.BlockSpec(memory_space=pl.ANY)
    columns = ada_weight.shape[1] // 4
    heads = jobs[2][0].shape[2]
    whole = lambda columns: pl.BlockSpec((tokens, columns), lambda i: (0, 0), pipeline_mode=pl.Buffered(1))
    gate = lambda n: pl.BlockSpec((tokens, width), lambda i: (0, n), pipeline_mode=pl.Buffered(1))
    shapes = [
        jax.ShapeDtypeStruct((tokens, width), F32),
        jax.ShapeDtypeStruct((tokens, width), BF16),
        jax.ShapeDtypeStruct((rows, heads * 3 // 4), F32),
        jax.ShapeDtypeStruct((rows, heads // 4), F32),
        jax.ShapeDtypeStruct((rows, columns), F32),
        jax.ShapeDtypeStruct((BIAS_ROWS, columns // 2), F32),
    ]
    shapes += [jax.ShapeDtypeStruct(chain.shape[1:], F32) for chain, _ in jobs[3:]]
    return pl.pallas_call(
        functools.partial(tail_kernel, orders, rows, exchange),
        grid=(1,),
        in_specs=[whole(width)] * 4
        + [gate(2), gate(5)]
        + [whole(width)] * 2
        + [anywhere] * 2
        + exchange.in_specs,
        out_specs=[constant_block(shape) for shape in shapes],
        out_shape=shapes,
        scratch_shapes=[
            pltpu.VMEM((tokens, ada_weight.shape[1]), BF16),
            pltpu.VMEM(ada_weight.shape, BF16),
            pltpu.VMEM((width, columns), F32),
            pltpu.SemaphoreType.DMA((2,)),
        ]
        + exchange.scratch,
        compiler_params=remote(exchange, number, 63),
        cost_estimate=cost(
            flops=16 * tokens * width * ada_weight.shape[1], bytes_accessed=100 * width * width, transcendentals=0
        ),
        name="tail",
    )(
        conditioning,
        silu_cond,
        patches,
        attn,
        modulation,
        modulation,
        cotangent,
        mlp,
        pieces,
        ada_weight,
        *exchange.operands,
    )


def finish_kernel(moves, rows, *refs):
    parts, refs = refs[: len(moves)], refs[len(moves) :]
    half = (len(refs) - 4) // 2
    plain, outs, experts = refs[:half], refs[half : 2 * half], refs[2 * half :]
    for source, target in zip(plain, outs):
        target[...] = source[...]
    for part, (expert, first, last) in zip(parts, moves):
        for kind in range(2):
            value = part[0, kind * rows : (kind + 1) * rows, :]
            if expert is None:
                experts[2 + kind][:, first:last] = value
            else:
                experts[kind][expert, :, first:last] = value


def run_finish(moves, plain, experts, rows, width):
    def block(array, index):
        return pl.BlockSpec((1,) + array.shape[1:], lambda i: (index, 0, 0), pipeline_mode=pl.Buffered(1))

    shapes = [jax.ShapeDtypeStruct(a.shape, a.dtype) for a in plain]
    shapes += [jax.ShapeDtypeStruct((experts, rows, width), F32)] * 2
    shapes += [jax.ShapeDtypeStruct((rows, width), F32)] * 2
    return pl.pallas_call(
        functools.partial(finish_kernel, [move[2:] for move in moves], rows),
        grid=(1,),
        in_specs=[block(array, index) for array, index, *_ in moves] + [whole_block(a) for a in plain],
        out_specs=[constant_block(shape) for shape in shapes],
        out_shape=shapes,
        compiler_params=pltpu.CompilerParams(vmem_limit_bytes=60 << 20),
        name="finish",
    )(*[move[0] for move in moves], *plain)


def gelu_and_slope(values):
    square = values * values
    bent = jnp.tanh(values * (GELU_A + (GELU_A * GELU_B) * square))
    half = 0.5 * (1.0 + bent)
    active = values * half
    return active, half + active * (1.0 - bent) * (GELU_A + (3.0 * GELU_A * GELU_B) * square)


class Gather:
    def __init__(self, own, far, held, send_sems, recv_sems):
        self.own, self.far, self.held, self.send_sems, self.recv_sems = own, far, held, send_sems, recv_sems

    def copy(self, place):
        far = self.held.at[1] if self.far is None else self.far
        return pltpu.make_async_remote_copy(
            src_ref=far if place == 2 else self.own,
            dst_ref=self.held.at[place],
            send_sem=self.send_sems.at[place],
            recv_sem=self.recv_sems.at[place],
            device_id=Exchange.partner("mp", 2 if place == 1 else 1),
            device_id_type=pl.DeviceIdType.MESH,
        )

    def begin(self):
        self.held[3] = self.own[...]
        if self.far is None:
            self.copy(1).start()
            self.copy(0).start()
        else:
            self.held[1] = self.far[...]
            self.copy(0).start()
            self.copy(2).start()

    def tile(self, step):
        @pl.when(step == 1)
        def _():
            self.copy(0).wait()

        if self.far is None:

            @pl.when(step == 2)
            def _():
                self.copy(1).wait()
                self.copy(2).start()

        @pl.when(step == 3)
        def _():
            self.copy(2).wait()

        return self.held[(step + 3) % 4]


def gather_barrier():
    barrier = pltpu.get_barrier_semaphore()
    for mask in (1, 2):
        pl.semaphore_signal(
            barrier, inc=1, device_id=Exchange.partner("mp", mask), device_id_type=pl.DeviceIdType.MESH
        )
    pl.semaphore_wait(barrier, 2)


def expert_kernel(columns, gathers, first, last, grad_later, exchange, units, rows, *refs):
    count = len(columns)
    gates, tokens, grads, refs = *refs[:3], refs[3:]
    if gathers:
        grads_far, refs = refs[0], refs[1:]
    ups, downs, refs = refs[:count], refs[count : 2 * count], refs[2 * count :]
    if not first:
        old_out, old_back, refs = refs[0], refs[1], refs[2:]
    number = len(exchange.operands)
    moved, refs = refs[:number], refs[number:]
    number = 2 * count if grad_later else sum(2 * len(own) for own in units)
    halves, refs = refs[:number], refs[number:]
    number = 4 if last else 2
    made, refs = refs[:number], refs[number:]
    number = len(exchange.shapes)
    moved_out, refs = refs[:number], refs[number:]
    if gathers:
        gathered, refs = refs[:2], refs[2:]
    number = 0 if grad_later else 2 * count
    sums, refs = refs[:number], refs[number:]
    step, final = pl.program_id(0), pl.num_programs(0) - 1
    if gathers:
        gather = [Gather(tokens, None, *refs[:3]), Gather(grads, grads_far, *refs[3:6])]
        refs = refs[6:]
    exchange.bind(moved, moved_out, refs)

    @pl.when(step == 0)
    def _():
        exchange.begin()

    @pl.when(step == 2)
    def _():
        exchange.early()

    if not grad_later:
        start_sums(step, sums)
    if gathers:

        @pl.when(step == 0)
        def _():
            gather_barrier()
            for one in gather:
                one.begin()

        x, own_grads = [one.tile(step) for one in gather]
        gathered[0][...] = x
        gathered[1][...] = own_grads
    else:
        x, own_grads = tokens[...], grads[...]
    g32 = own_grads.astype(F32)
    routed = None if first else old_out[...]
    returned = None if first else old_back[...]
    for n, column in enumerate(columns):
        gate = gates[:, column : column + 1]
        slot_grad = (gate * g32).astype(BF16)
        hidden, grad_pre, one, two = expert_pass(x, slot_grad, gate, ups[n][0], downs[n][0])
        routed = one if routed is None else routed + one
        returned = two if returned is None else returned + two
        if grad_later:
            halves[2 * n][...] = hidden
            halves[2 * n + 1][...] = grad_pre
        else:
            sums[2 * n][...] += tn(x, grad_pre)
            sums[2 * n + 1][...] += tn(slot_grad, hidden)
    if last:
        for value, (kept, sent) in ((routed, made[:2]), (returned, made[2:])):

            @pl.when(step < 2)
            def _():
                kept[0] = value.astype(BF16)

            @pl.when(step >= 2)
            def _():
                sent[0] = value.astype(BF16)

    else:
        made[0][...] = routed
        made[1][...] = returned
    if not grad_later:
        store_halves(step, units, sums, halves, rows)

    @pl.when(step == final)
    def _():
        exchange.finish()


def start_sums(step, sums):
    @pl.when(step == 0)
    def _():
        for total in sums:
            total[...] = jnp.zeros_like(total)


def store_units(units, sums, targets, rows):
    for (columns, order), halves in zip(units, targets):
        half = len(order) // 2
        for place, owner in enumerate(order):
            start = place * rows if half == 1 else rows_of(owner, rows)
            for part, total in enumerate(sums):
                halves[place // half][place % half, part * rows : (part + 1) * rows, :] = total[
                    pl.ds(start, rows), columns
                ].astype(BF16)


def store_halves(step, units, sums, halves, rows):
    @pl.when(step == pl.num_programs(0) - 1)
    def _():
        start = 0
        for n, own in enumerate(units):
            pairs = [halves[start + 2 * u : start + 2 * u + 2] for u in range(len(own))]
            start += 2 * len(own)
            store_units(own, sums[2 * n : 2 * n + 2], pairs, rows)


def unit_shapes(units, rows, width):
    shapes = []
    for columns, order in units:
        number = len(range(*columns.indices(width)))
        shapes += [jax.ShapeDtypeStruct((len(order) // 2, 2 * rows, number), BF16)] * 2
    return shapes


def constant_block(shape):
    return pl.BlockSpec(shape.shape, lambda *_: (0,) * len(shape.shape))


def expert_pass(x, slot_grad, gate, up, down):
    pre = nn(x, up)
    grad_hidden = nt(slot_grad, down)
    hidden, slope = gelu_and_slope(pre)
    hidden = hidden.astype(BF16)
    grad_pre = (grad_hidden * slope).astype(BF16)
    return hidden, grad_pre, gate * nn(hidden, down), nt(grad_pre, up)


TILE = 512


def token_tiles(columns):
    return pl.BlockSpec((TILE, columns), lambda t: (t, 0))


def run_experts(
    columns, weights, units, rows, gates, tokens, grads, sums, last, grad_later, jobs, number, gathers=False
):
    count = len(columns)
    total, width = gates.shape[0], tokens.shape[1]
    hidden = weights[0][0].shape[2]
    steps = total // TILE
    first = sums is None
    exchange = Exchange(jobs)

    def weight(index, shape):
        return pl.BlockSpec((1,) + shape, lambda t: (index, 0, 0), pipeline_mode=pl.Buffered(1))

    def tiles(columns):
        return pl.BlockSpec((TILE, columns), lambda t: ((t % 2) * 2 + t // 2 if gathers else t, 0))

    in_specs = (
        [tiles(gates.shape[1])]
        + ([pl.BlockSpec((TILE, width), lambda t: (0, 0))] * 3 if gathers else [tiles(width)] * 2)
        + [weight(i, (width, hidden)) for _, _, i in weights]
        + [weight(i, (hidden, width)) for _, _, i in weights]
        + ([] if first else [token_tiles(width), token_tiles(width)])
    )
    given = len(in_specs)
    if grad_later:
        shapes = [jax.ShapeDtypeStruct((total, hidden), BF16)] * (2 * count)
        specs = [token_tiles(hidden)] * (2 * count)
    else:
        shapes = [shape for own in units for shape in unit_shapes(own, rows, hidden)]
        specs = [constant_block(shape) for shape in shapes]
    made = len(shapes)
    if last:
        block = (1, TILE, width)
        sum_specs = [
            pl.BlockSpec(block, lambda t: (jnp.minimum(t, 1), 0, 0)),
            pl.BlockSpec(block, lambda t: (jnp.maximum(t - 2, 0), 0, 0)),
        ] * 2
        sum_shapes = [jax.ShapeDtypeStruct((2, TILE, width), BF16)] * 4
    else:
        sum_specs = [tiles(width)] * 2
        sum_shapes = [jax.ShapeDtypeStruct((total, width), F32)] * 2
    gather_scratch, gather_shapes = [], []
    if gathers:
        gather_scratch = ([pltpu.VMEM((4, TILE, width), BF16)] + [pltpu.SemaphoreType.DMA((3,))] * 2) * 2
        gather_shapes = [jax.ShapeDtypeStruct((total, width), BF16)] * 2
    aliases = {} if first or last else {given - 2: made, given - 1: made + 1}
    results = pl.pallas_call(
        functools.partial(expert_kernel, columns, gathers, first, last, grad_later, exchange, units, rows),
        grid_spec=pltpu.PrefetchScalarGridSpec(
            num_scalar_prefetch=0,
            grid=(steps,),
            in_specs=in_specs + exchange.in_specs,
            out_specs=specs + sum_specs + exchange.out_specs + [tiles(width)] * (2 * gathers),
            scratch_shapes=([] if grad_later else [pltpu.VMEM((width, hidden), F32)] * (2 * count))
            + gather_scratch
            + exchange.scratch,
        ),
        out_shape=shapes + sum_shapes + exchange.shapes + gather_shapes,
        input_output_aliases=aliases,
        compiler_params=remote(exchange, number, 60, gathers),
        cost_estimate=cost(
            flops=(8 if grad_later else 12) * count * total * width * hidden,
            bytes_accessed=20 * total * width + 8 * count * width * hidden,
            transcendentals=count * total * hidden,
        ),
        name=f"experts_{count}",
    )(
        gates,
        tokens,
        *(grads if gathers else [grads]),
        *[up for up, _, _ in weights],
        *[down for _, down, _ in weights],
        *(() if first else sums),
        *exchange.operands,
    )
    number = made + len(sum_shapes)
    if gathers:
        return results[:made], results[made:number], results[number:]
    exchange.spread(results[number:])
    return results[:made], results[made:number]


SLOTS = 3


def long_kernel(count, exchange, units, unit_steps, rows, gates, tokens, grads, up, down, *refs):
    old = refs[:2]
    number = len(exchange.operands)
    moved, refs = refs[2 : 2 + number], refs[2 + number :]
    new, finals, last_final, refs = refs[:2], refs[2], refs[3], refs[4:]
    number = 2 * len(units)
    half_done, raw, refs = refs[:number], refs[number : 2 * number], refs[2 * number :]
    number = len(exchange.shapes)
    moved_out, refs = refs[:number], refs[number:]
    sums, totals, send, work, gots = refs[:2], refs[2:4], refs[4], refs[5], refs[6:9]
    send_sems, recv_sems, load_sems, store_sems, refs = *refs[9:13], refs[13:]
    exchange.bind(moved, moved_out, refs)
    e, t = pl.program_id(0), pl.program_id(1)
    tiles = 4

    def copy(chain, step, unit):
        slot = chain % SLOTS
        blocks = 4 >> step
        columns = units[unit][0]
        place = pl.ds(columns.start, columns.stop - columns.start)
        source = send if step == 0 else work
        first = 0 if step == 0 else blocks
        return pltpu.make_async_remote_copy(
            src_ref=source.at[slot, pl.ds(first, blocks), :, place],
            dst_ref=gots[step].at[slot, :, :, place],
            send_sem=send_sems.at[slot, step, unit],
            recv_sem=recv_sems.at[slot, step, unit],
            device_id=exchange.partner(*unit_steps[unit][step]),
            device_id_type=pl.DeviceIdType.MESH,
        )

    def launch(chain, step):
        for unit in range(len(units)):
            copy(chain, step, unit).start()

    def arrive(chain, step):
        for unit in range(len(units)):
            copy(chain, step, unit).wait()

    def add(chain, step):
        slot = chain % SLOTS

        def one(i, carry):
            total = work[slot, i].astype(F32) + gots[step][slot, i].astype(F32)
            work[slot, i] = total.astype(BF16)
            return carry

        lax.fori_loop(0, 4 >> step, one, 0)

    def close(chain, target):
        arrive(chain, 2)
        slot = chain % SLOTS
        target[0] = work[slot, 0].astype(F32) + gots[2][slot, 0].astype(F32)

    def loads(n, tile):
        return pltpu.make_async_copy(
            old[n].at[pl.ds(tile * TILE, TILE), :], totals[n].at[tile], load_sems.at[n, tile]
        )

    def stores(n, tile):
        return pltpu.make_async_copy(
            totals[n].at[tile], new[n].at[pl.ds(tile * TILE, TILE), :], store_sems.at[n, tile]
        )

    @pl.when((e == 0) & (t == 0))
    def _():
        for tile in range(tiles):
            for n in range(2):
                loads(n, tile).start()
        exchange.begin(sorted({step for steps in unit_steps for step in steps}))

    for tile in range(tiles):

        @pl.when((e == 0) & (t == tile))
        def _():
            for n in range(2):
                loads(n, tile).wait()

    @pl.when((e == 1) & (t == 0))
    def _():
        exchange.all_once()

    @pl.when((e == 1) & (t == 2))
    def _():
        exchange.all_once()

    @pl.when((e == 2) & (t == 0))
    def _():
        exchange.finish()

    @pl.when((e >= 2) & (t == 0))
    def _():
        arrive(e - 2, 0)
        add(e - 2, 0)
        launch(e - 2, 1)

    @pl.when((e >= 1) & (t == 0))
    def _():
        launch(e - 1, 0)

    @pl.when((e >= 3) & (t == 2))
    def _():
        close(e - 3, finals)

    @pl.when((e >= 2) & (t == 2))
    def _():
        arrive(e - 2, 1)
        add(e - 2, 1)
        launch(e - 2, 2)

    @pl.when(t == 0)
    def _():
        for total in sums:
            total[...] = jnp.zeros_like(total)

    lane = lax.broadcasted_iota(jnp.int32, (1, gates.shape[1]), 1)
    gate = jnp.sum(jnp.where(lane == e, gates[...], 0.0), axis=1, keepdims=True)
    x = tokens[...]
    slot_grad = (gate * grads[...].astype(F32)).astype(BF16)
    hidden, grad_pre, one, two = expert_pass(x, slot_grad, gate, up[0], down[0])
    totals[0][t] += one
    totals[1][t] += two
    sums[0][...] += tn(x, grad_pre)
    sums[1][...] += tn(slot_grad, hidden)

    for tile in range(tiles):

        @pl.when((e == count - 1) & (t == tile))
        def _():
            for n in range(2):
                stores(n, tile).start()

    @pl.when((t == tiles - 1) & (e < count - 1))
    def _():
        slot = e % SLOTS
        pairs = [
            (work.at[slot, :, :, pl.ds(c.start, c.stop - c.start)], send.at[slot, :, :, pl.ds(c.start, c.stop - c.start)])
            for c, _ in units
        ]
        store_units(units, sums, pairs, rows)

    @pl.when((t == tiles - 1) & (e == count - 1))
    def _():
        store_units(units, sums, [raw[2 * u : 2 * u + 2] for u in range(len(units))], rows)
        close(count - 3, last_final)
        arrive(count - 2, 0)
        add(count - 2, 0)
        slot = (count - 2) % SLOTS
        for u, (c, _) in enumerate(units):
            half_done[2 * u][...] = work[slot, 0:2, :, c]
            half_done[2 * u + 1][...] = work[slot, 2:4, :, c]
        for tile in range(tiles):
            for n in range(2):
                stores(n, tile).wait()


def run_long(count, units, unit_steps, rows, gates, tokens, grads, expert_up, expert_down, sums, jobs, number):
    total, width = tokens.shape
    hidden = expert_up.shape[2]
    exchange = Exchange(jobs)
    steps = total // TILE
    tile = lambda columns: pl.BlockSpec((TILE, columns), lambda e, t: (t, 0))
    weight = lambda shape: pl.BlockSpec((1,) + shape, lambda e, t: (e, 0, 0))
    anywhere = pl.BlockSpec(memory_space=pl.ANY)
    raw = unit_shapes(units, rows, hidden)
    half_done = [jax.ShapeDtypeStruct((s.shape[0] // 2,) + s.shape[1:], BF16) for s in raw]
    final = (1, 2 * rows, hidden)
    results = pl.pallas_call(
        functools.partial(long_kernel, count, exchange, units, unit_steps, rows),
        grid=(count, steps),
        in_specs=[
            tile(gates.shape[1]),
            tile(width),
            tile(width),
            weight((width, hidden)),
            weight((hidden, width)),
            anywhere,
            anywhere,
        ]
        + exchange.in_specs,
        out_specs=[anywhere, anywhere]
        + [pl.BlockSpec(final, lambda e, t: (jnp.maximum(e - 3, 0), 0, 0)), pl.BlockSpec(final, lambda e, t: (0, 0, 0))]
        + [constant_block(shape) for shape in half_done + raw]
        + exchange.out_specs,
        out_shape=[jax.ShapeDtypeStruct((total, width), F32)] * 2
        + [jax.ShapeDtypeStruct((count - 3,) + final[1:], F32), jax.ShapeDtypeStruct(final, F32)]
        + half_done
        + raw
        + exchange.shapes,
        scratch_shapes=[pltpu.VMEM((width, hidden), F32)] * 2
        + [pltpu.VMEM((steps, TILE, width), F32)] * 2
        + [pltpu.VMEM((SLOTS, 4, 2 * rows, hidden), BF16)] * 2
        + [pltpu.VMEM((SLOTS, 4 >> n, 2 * rows, hidden), BF16) for n in range(3)]
        + [pltpu.SemaphoreType.DMA((SLOTS, 3, len(units)))] * 2
        + [pltpu.SemaphoreType.DMA((2, steps))] * 2
        + exchange.scratch,
        compiler_params=remote(exchange, number, 62),
        cost_estimate=cost(
            flops=12 * count * total * width * hidden,
            bytes_accessed=8 * count * total * width,
            transcendentals=count * total * hidden,
        ),
        name="experts_long",
    )(gates, tokens, grads, expert_up, expert_down, *sums, *exchange.operands)
    made = len(raw)
    exchange.spread(results[4 + 2 * made :])
    finished = [(results[2], n) for n in range(count - 3)] + [(results[3], 0)]
    return results[:2], finished, results[4 : 4 + made], results[4 + made : 4 + 2 * made]


def expert_grads_kernel(columns, exchange, units, rows, *refs):
    count = len(columns)
    gates, tokens, grads = refs[:3]
    saved, refs = refs[3 : 3 + 2 * count], refs[3 + 2 * count :]
    number = len(exchange.operands)
    moved, refs = refs[:number], refs[number:]
    number = sum(2 * len(own) for own in units)
    halves, refs = refs[:number], refs[number:]
    number = len(exchange.shapes)
    moved_out, refs = refs[:number], refs[number:]
    sums, refs = refs[: 2 * count], refs[2 * count :]
    step, final = pl.program_id(0), pl.num_programs(0) - 1
    exchange.bind(moved, moved_out, refs)

    @pl.when(step == 0)
    def _():
        exchange.begin()

    @pl.when(step == 1)
    def _():
        exchange.early(0, 1)

    @pl.when(step == 2)
    def _():
        exchange.early(1)

    start_sums(step, sums)
    x = tokens[...]
    g32 = grads[...].astype(F32)
    for n, column in enumerate(columns):
        slot_grad = (gates[:, column : column + 1] * g32).astype(BF16)
        sums[2 * n][...] += tn(x, saved[2 * n + 1][...])
        sums[2 * n + 1][...] += tn(slot_grad, saved[2 * n][...])
    store_halves(step, units, sums, halves, rows)

    @pl.when(step == final)
    def _():
        exchange.finish()


def run_expert_grads(columns, saved, units, rows, gates, tokens, grads, jobs, number):
    count = len(columns)
    total, width = tokens.shape
    hidden = saved[0].shape[1]
    steps = total // TILE
    shapes = [shape for own in units for shape in unit_shapes(own, rows, hidden)]
    exchange = Exchange(jobs)
    results = pl.pallas_call(
        functools.partial(expert_grads_kernel, columns, exchange, units, rows),
        grid_spec=pltpu.PrefetchScalarGridSpec(
            num_scalar_prefetch=0,
            grid=(steps,),
            in_specs=[token_tiles(gates.shape[1]), token_tiles(width), token_tiles(width)]
            + [token_tiles(hidden)] * (2 * count)
            + exchange.in_specs,
            out_specs=[constant_block(shape) for shape in shapes] + exchange.out_specs,
            scratch_shapes=[pltpu.VMEM((width, hidden), F32)] * (2 * count) + exchange.scratch,
        ),
        out_shape=shapes + exchange.shapes,
        compiler_params=remote(exchange, number, 60),
        cost_estimate=cost(
            flops=4 * count * total * width * hidden,
            bytes_accessed=(4 + 4 * count) * total * width,
            transcendentals=0,
        ),
        name="expert_grads",
    )(gates, tokens, grads, *saved, *exchange.operands)
    exchange.spread(results[len(shapes) :])
    return results[: len(shapes)]


def local(
    patches,
    conditioning,
    cotangent,
    segments,
    routes,
    gate_values,
    ada_weight,
    ada_bias,
    qkv_weight,
    out_weight,
    shared_up,
    shared_down,
    expert_up,
    expert_down,
):
    tokens, width = patches.shape
    group = routes.shape[0]
    experts = expert_up.shape[0]
    seq = segments.shape[1]
    n_dp, n_mp = lax.axis_size("dp"), lax.axis_size("mp")
    dp, mp = lax.axis_index("dp"), lax.axis_index("mp")
    rows = width // n_dp

    qkv_parts = gather_mp(qkv_weight.reshape(width, -1))
    out_parts = gather_mp(out_weight)

    silu_cond = jax.nn.silu(conditioning.astype(F32)).astype(BF16)
    modulation = jnp.dot(silu_cond, ada_weight, preferred_element_type=F32) + ada_bias[None, :]
    gate_two = modulation[:, 5 * width :]
    grad_mlp = (cotangent.astype(F32) * gate_two).astype(BF16)
    grad_mlp, *far = lax.optimization_barrier((grad_mlp, qkv_parts[1], out_parts[1]))
    qkv_parts[1], out_parts[1] = far
    grad_far = swap(grad_mlp, "mp", 2)

    own_rows = tokens // seq
    own_segments = lax.dynamic_slice_in_dim(segments, mp * own_rows, own_rows, axis=0)
    results = run_forward(patches, modulation, own_segments, qkv_parts, out_parts)
    normed_one, qkv, attended, lse, attn_out, normed_two = results[0], results[1:5], *results[5:]

    number = jnp.arange(16, dtype=jnp.int32)[None, :]
    gates = jnp.sum(
        jnp.where(routes[:, :, None] == number[:, None, :], gate_values[:, :, None], 0.0), axis=1
    )
    gates = jnp.where(number == experts, 1.0, gates)
    gates = jnp.concatenate(
        [lax.dynamic_slice_in_dim(gates, (mp ^ m) * tokens, tokens, axis=0) for m in MP_ORDER],
        axis=0,
    )
    shared = (shared_up[None], shared_down[None], 0)
    weights = {e: (expert_up, expert_down, e) for e in range(experts)}
    weights[experts] = shared
    even = halves_evenly(n_dp, rows)
    step = rows if even else width // 2
    reduced, chains, wholes = {}, {}, {}
    if even:
        near_step, far_step, *rest = dp_steps(n_dp)
        hidden = expert_up.shape[2]
        cut = hidden * 2 // 3
        unit_steps = [[near_step, far_step] + rest, [far_step, near_step] + rest]
        parts = [(slice(0, cut), unit_steps[0]), (slice(cut, hidden), unit_steps[1])]
        kinds = {c: parts for c in weights}
        kinds[experts - 2] = [(slice(0, hidden), unit_steps[1])]
        kinds[experts - 1] = [(slice(0, hidden), unit_steps[0])]
        units = {
            c: [(columns, [d for d, _ in block_order(steps)]) for columns, steps in kind]
            for c, kind in kinds.items()
        }
    else:
        units = {c: [(slice(0, expert_up.shape[2]), [0, 1])] for c in weights}

    def take_halves(columns, halves, done=0):
        halves = list(halves)
        for column in columns:
            own = [halves.pop(0) for _ in range(2 * len(units[column]))]
            if even:
                chains[column] = [
                    Chain(own[2 * u], own[2 * u + 1], steps, done)
                    for u, (_, steps) in enumerate(kinds[column])
                ]
            else:
                wholes[column] = own

    def jobs(**counts):
        if not even:
            return []
        return [(c, int(count[1:])) for count, columns in counts.items() for x in columns for c in chains[x]]

    def call(columns, sums, last, moves, number):
        return run_experts(
            columns,
            [weights[c] for c in columns],
            [units[c] for c in columns],
            step,
            gates,
            all_tokens,
            all_grads,
            sums,
            last,
            last,
            moves,
            number,
        )

    halves, sums, (all_tokens, all_grads) = run_experts(
        (experts,),
        [weights[experts]],
        [units[experts]],
        step,
        gates,
        normed_two,
        [grad_mlp, grad_far],
        None,
        False,
        False,
        [],
        0,
        True,
    )
    take_halves((experts,), halves)
    late = (experts - 2, experts - 1)
    if even:
        sums, finished, half_done, raw = run_long(
            experts - 2,
            units[0],
            unit_steps,
            rows,
            gates,
            all_tokens,
            all_grads,
            expert_up,
            expert_down,
            sums,
            jobs(n3=(experts,)),
            1,
        )
        take_halves((experts - 4,), half_done, 1)
        take_halves((experts - 3,), raw)
    else:
        for e in range(0, experts - 2, 2):
            halves, sums = call((e, e + 1), sums, False, [], 1 + e // 2)
            take_halves((e, e + 1), halves)
    saved, sums = call(late, sums, True, jobs(n2=(experts - 4,), n1=(experts - 3,)), 4)
    out_chain, back_chain = Chain(*sums[:2], MP_STEPS), Chain(*sums[2:], MP_STEPS)
    halves = run_expert_grads(
        late,
        saved,
        [units[c] for c in late],
        step,
        gates,
        all_tokens,
        all_grads,
        [(back_chain, 2)] + jobs(n2=(experts - 3,)),
        5,
    )
    take_halves(late, halves)
    tail_steps = [MP_STEPS] * 3
    if even:
        y, z, rest = dp_steps(n_dp)[0], dp_steps(n_dp)[1], dp_steps(n_dp)[2:]
        core, x = MP_STEPS
        tail_steps = [[core, x, y, z] + rest, [core, y, x, z] + rest, [core, x, y, z] + rest]
    tail_orders = [block_order(steps) for steps in tail_steps]

    tail_rows = rows if even else width
    results = run_attention_back(
        patches,
        modulation,
        attn_out,
        cotangent,
        back_chain.result,
        normed_one,
        attended,
        lse,
        own_segments,
        qkv,
        qkv_parts,
        out_parts,
        tail_orders[0],
        tail_rows,
        [(out_chain, 2)] + jobs(n2=late),
        6,
    )
    patches_grad, pieces, heads_halves = results[0], results[1], results[2:4]
    heads_chain = Chain(*heads_halves, tail_steps[0])
    split = ada_weight.shape[1] // n_mp // 2
    half = len(tail_orders[1]) // 2
    ada_chains = [
        Chain.inside((half, tail_rows + BIAS_ROWS, split), tail_steps[1]),
        Chain.inside((half, tail_rows, split), tail_steps[2]),
    ]
    number = len(tail_steps[0])
    results = run_tail(
        conditioning,
        silu_cond,
        patches,
        attn_out,
        modulation,
        cotangent,
        out_chain.result,
        pieces,
        ada_weight,
        tail_orders[1:],
        tail_rows,
        [(c, number) for c in ada_chains] + [(heads_chain, number)] + jobs(n1=late),
        7,
    )
    conditioning_grad, output, qkv_sum, out_total, ada_sum, bias_all = results[:6]
    bias_all = bias_all[: 2 * n_mp].reshape(-1)
    if even:
        moves = [(array, index, e, 0, hidden) for e, (array, index) in enumerate(finished)]
        moves += [(array[None], 0, column, 0, hidden) for column, array in zip(late, results[6:])]
        for column, own in chains.items():
            if column not in late:
                for chain, (columns, _) in zip(own, kinds[column]):
                    place = None if column == experts else column
                    moves.append((chain.result[None], 0, place, columns.start, columns.stop))
        results = run_finish(
            moves, [output, patches_grad, conditioning_grad, ada_sum], experts, rows, hidden
        )
        output, patches_grad, conditioning_grad, ada_sum = results[:4]
        expert_up_sum, expert_down_sum, up_sum, down_sum = results[4:]
    else:
        for column, (first, second) in wholes.items():
            whole = jnp.stack([first[0], second[0]]).reshape(2, 2, step, -1)
            whole = jnp.swapaxes(whole, 0, 1).reshape(2, width, -1)
            part = lax.psum_scatter(whole, "dp", scatter_dimension=1, tiled=True).astype(F32)
            reduced[column] = part[0], part[1]
        up_sum, down_sum = reduced[experts]
        expert_up_sum, expert_down_sum = [
            jnp.stack([reduced[e][part] for e in range(experts)]) for part in range(2)
        ]
        qkv_sum, out_total, ada_sum = [
            lax.psum_scatter(a.astype(BF16), "dp", scatter_dimension=0, tiled=True).astype(F32)
            for a in (qkv_sum, out_total, ada_sum)
        ]
        bias_all = lax.psum(bias_all, "dp")
    share = bias_all.shape[0] // (n_dp * n_mp)
    return (
        output,
        patches_grad,
        conditioning_grad,
        ada_sum,
        lax.dynamic_slice_in_dim(bias_all, (dp * n_mp + mp) * share, share),
        qkv_sum.reshape(rows, 3, -1),
        out_total.T,
        up_sum,
        down_sum.T,
        expert_up_sum,
        jnp.swapaxes(expert_down_sum, 1, 2),
    )


def solution(mesh):
    in_specs = (
        P(("dp", "mp"), None),
        P(("dp", "mp"), None),
        P(("dp", "mp"), None),
        P("dp", None),
        P("dp", None),
        P("dp", None),
        P(),
        P(),
        P(None, None, "mp"),
        P("mp", None),
        P(None, "mp"),
        P("mp", None),
        P(None, None, "mp"),
        P(None, "mp", None),
    )
    out_specs = (
        P(("dp", "mp"), None),
        P(("dp", "mp"), None),
        P(("dp", "mp"), None),
        P("dp", "mp"),
        P(("dp", "mp")),
        P("dp", None, "mp"),
        P("mp", "dp"),
        P("dp", "mp"),
        P("mp", "dp"),
        P(None, "dp", "mp"),
        P(None, "mp", "dp"),
    )
    return jax.shard_map(local, mesh=mesh, in_specs=in_specs, out_specs=out_specs, check_vma=False)
```

```python
import functools

import jax
import jax.numpy as jnp
from jax import lax
from jax.experimental import pallas as pl
from jax.experimental.pallas import tpu as pltpu
from jax.sharding import PartitionSpec as P

HEAD_DIM = 64
BF16 = jnp.bfloat16
F32 = jnp.float32
GELU_A = 0.7978845608028654
GELU_B = 0.044715


def nn(a, b):
    return lax.dot_general(a, b, (((1,), (0,)), ((), ())), preferred_element_type=F32)


def nt(a, b):
    return lax.dot_general(a, b, (((1,), (1,)), ((), ())), preferred_element_type=F32)


def tn(a, b):
    return lax.dot_general(a, b, (((0,), (0,)), ((), ())), preferred_element_type=F32)


def cost(flops, bytes_accessed, transcendentals):
    share = 16
    return pl.CostEstimate(
        flops=flops // share, bytes_accessed=bytes_accessed // share, transcendentals=transcendentals // share
    )


def swap(value, axis, mask):
    size = lax.axis_size(axis)
    return lax.ppermute(value, axis, [(i, i ^ mask) for i in range(size)])


def halves_evenly(n_dp, rows):
    return n_dp == 8 and rows % 16 == 0


def dp_steps(n_dp):
    return [("dp", 1 << bit) for bit in range(n_dp.bit_length() - 1)]


def block_order(steps):
    order = [(0, 0)]
    for axis, mask in reversed(steps):
        order = order + [(d ^ mask, m) if axis == "dp" else (d, m ^ mask) for d, m in order]
    return order


def flip(index, mask):
    bit = 1
    while bit <= mask:
        if mask & bit:
            index = index + bit * (1 - 2 * ((index // bit) % 2))
        bit *= 2
    return index


class Chain:
    def __init__(self, keep, send, steps, done=0):
        self.keep, self.send, self.steps, self.step = keep, send, steps, done
        self.shape = None if keep is None else keep.shape

    @classmethod
    def inside(cls, shape, steps):
        chain = cls(None, None, steps)
        chain.shape = shape
        return chain

    def take(self, results):
        if self.step == len(self.steps):
            self.result = results.pop(0)[0]
        else:
            self.keep, self.send = results.pop(0), results.pop(0)
            self.shape = self.keep.shape

    def advance(self):
        got = swap(self.send, *self.steps[self.step])
        total = self.keep.astype(F32) + got.astype(F32)
        half = total.shape[0] // 2
        self.step += 1
        self.take([total[:half].astype(BF16), total[half:].astype(BF16)] if half else [total])

    def finish(self):
        while self.step < len(self.steps):
            self.advance()
        return self.result


class Exchange:
    def __init__(self, jobs, sunk=False):
        self.jobs, self.sunk, self.sinks = jobs, sunk, {}
        self.operands, self.in_specs, self.out_specs, self.shapes, self.scratch = [], [], [], [], []
        self.plans = []
        for chain, count in jobs:
            blocks, tail = chain.shape[0], chain.shape[1:]
            steps = chain.steps[chain.step : chain.step + count]
            final = chain.step + count == len(chain.steps)
            self.plans.append((steps, final, blocks, chain.keep is None))
            if chain.keep is None:
                self.scratch.append(pltpu.VMEM(chain.shape, BF16))
            else:
                self.operands += [chain.keep, chain.send]
                self.in_specs += [pl.BlockSpec(memory_space=pl.ANY)] * 2
            left = blocks >> (count if not final else count - 1)
            kept = jax.ShapeDtypeStruct((left,) + tail, F32 if final else BF16)
            outs = [] if final and sunk else [kept] if final else [kept, kept]
            self.shapes += outs
            self.out_specs += [pl.BlockSpec(kept.shape, lambda *_: (0, 0, 0))] * len(outs)
            self.scratch.append(pltpu.VMEM((blocks,) + tail, BF16))
            self.scratch += [pltpu.VMEM((blocks >> n,) + tail, BF16) for n in range(count)]
            self.scratch += [
                pltpu.SemaphoreType.DMA((1,)),
                pltpu.SemaphoreType.DMA((count,)),
                pltpu.SemaphoreType.DMA((count,)),
            ]

    def bind(self, ins, outs, scratch):
        self.ins, self.outs, self.buffers, self.at = [], [], [], [0] * len(self.jobs)
        for steps, final, _, inner in self.plans:
            number = 0 if final and self.sunk else 1 if final else 2
            self.outs.append(outs[:number])
            outs = outs[number:]
            if inner:
                self.ins.append([None, scratch[0]])
                scratch = scratch[1:]
            else:
                self.ins.append(ins[:2])
                ins = ins[2:]
            number = len(steps) + 4
            self.buffers.append(scratch[:number])
            scratch = scratch[number:]

    @staticmethod
    def partner(axis, mask):
        return {axis: flip(lax.axis_index(axis), mask)}

    def load(self, n):
        return pltpu.make_async_copy(self.ins[n][0], self.buffers[n][0], self.buffers[n][-3].at[0])

    def copy(self, n, step):
        steps, _, blocks, _ = self.plans[n]
        work, send_sems, recv_sems = self.buffers[n][0], self.buffers[n][-2], self.buffers[n][-1]
        number = blocks >> step
        source = self.ins[n][1] if step == 0 else work.at[pl.ds(number, number)]
        return pltpu.make_async_remote_copy(
            src_ref=source,
            dst_ref=self.buffers[n][1 + step],
            send_sem=send_sems.at[step],
            recv_sem=recv_sems.at[step],
            device_id=self.partner(*steps[step]),
            device_id_type=pl.DeviceIdType.MESH,
        )

    def begin(self, others=()):
        partners = sorted({step for steps, *_ in self.plans for step in steps} | set(others))
        if partners:
            barrier = pltpu.get_barrier_semaphore()
            for step in partners:
                pl.semaphore_signal(
                    barrier, inc=1, device_id=self.partner(*step), device_id_type=pl.DeviceIdType.MESH
                )
            pl.semaphore_wait(barrier, len(partners))
        for n, (*_, inner) in enumerate(self.plans):
            if not inner:
                self.copy(n, 0).start()
                self.load(n).start()

    def halves(self, n):
        return self.buffers[n][0], self.ins[n][1]

    def start(self, n):
        self.copy(n, 0).start()

    def advance(self, n):
        steps, final, blocks, inner = self.plans[n]
        step = self.at[n]
        self.at[n] += 1
        work, got = self.buffers[n][0], self.buffers[n][1 + step]
        number = blocks >> step
        if step == 0 and not inner:
            self.load(n).wait()
        self.copy(n, step).wait()
        half = number // 2
        ending = step == len(steps) - 1

        def add(first, count, target, shift):
            def one(i, carry):
                total = work[i].astype(F32) + got[i].astype(F32)
                target[i - shift] = total.astype(target.dtype)
                return carry

            lax.fori_loop(first, first + count, one, 0)

        if ending and final and self.sunk:
            self.sinks[n](work[0].astype(F32) + got[0].astype(F32))
        elif ending and final:
            add(0, number, self.outs[n][0], 0)
        elif ending:
            add(0, half, self.outs[n][0], 0)
            add(half, half, self.outs[n][1], half)
        else:
            add(half, half, work, 0)
            self.copy(n, step + 1).start()
            add(0, half, work, 0)

    def left(self, n):
        return len(self.plans[n][0]) - self.at[n]

    def all_once(self):
        for n in range(len(self.jobs)):
            self.advance(n)

    def early(self, first=0, last=None):
        for n, (steps, *_) in list(enumerate(self.plans))[first:last]:
            while self.at[n] < len(steps) - 1:
                self.advance(n)

    def finish(self):
        for step in range(max([len(steps) for steps, *_ in self.plans], default=0)):
            for n, (steps, *_) in enumerate(self.plans):
                if self.at[n] == step and step < len(steps):
                    self.advance(n)

    def spread(self, results):
        results = list(results)
        for chain, count in self.jobs:
            chain.step += count
            if not (self.sunk and chain.step == len(chain.steps)):
                chain.take(results)


def remote(exchange, number, vmem, always=False):
    if not (exchange.jobs or always):
        return pltpu.CompilerParams(vmem_limit_bytes=vmem << 20)
    return pltpu.CompilerParams(vmem_limit_bytes=vmem << 20, collective_id=number, has_side_effects=True)


MP_STEPS = [("mp", 1), ("mp", 2)]
MP_ORDER = [m for _, m in block_order(MP_STEPS)]


def gather_mp(own):
    far = swap(own, "mp", 2)
    return [own, far, swap(own, "mp", 1), swap(far, "mp", 1)]


def normalize(values):
    center = values - jnp.mean(values, axis=-1, keepdims=True)
    inverse = lax.rsqrt(jnp.mean(center * center, axis=-1, keepdims=True) + 1e-06)
    return center * inverse, inverse


def normalize_back(normal, inverse, grad):
    return inverse * (
        grad
        - jnp.mean(grad, axis=-1, keepdims=True)
        - normal * jnp.mean(grad * normal, axis=-1, keepdims=True)
    )


def forward_kernel(
    heads, base, shift_one, scale_one, gate_one, shift_two, scale_two, seg_col, seg_row, *refs
):
    weights, out_weights = refs[:4], refs[4:8]
    normed_out, qkv, attended, lse_out, attn_out, second_out = refs[8], refs[9:13], *refs[13:]
    span = heads * HEAD_DIM
    x = base[...].astype(F32)
    normed = (normalize(x)[0] * (1.0 + scale_one[...]) + shift_one[...]).astype(BF16)
    normed_out[...] = normed
    same = seg_col[0] == seg_row[0]
    lane = lax.broadcasted_iota(jnp.int32, (1, 128), 1)
    lse_all = jnp.zeros(lse_out.shape, F32)
    attn = jnp.zeros(x.shape, F32)
    for block in range(4):
        qkv[block][...] = nt(normed, weights[block][...]).astype(BF16)
        for head in range(heads):
            at = head * HEAD_DIM
            q = qkv[block][:, at : at + HEAD_DIM]
            k = qkv[block][:, span + at : span + at + HEAD_DIM]
            v = qkv[block][:, 2 * span + at : 2 * span + at + HEAD_DIM]
            scores = jnp.where(same, nt(q, k) * (HEAD_DIM**-0.5), -1000000000.0)
            top = jnp.max(scores, axis=-1, keepdims=True)
            expo = jnp.exp(scores - top)
            total = jnp.sum(expo, axis=-1, keepdims=True)
            light = (expo * (1.0 / total)).astype(BF16)
            start = block * span + at
            attended[:, start : start + HEAD_DIM] = nn(light, v).astype(BF16)
            lse_all = jnp.where(lane == block * heads + head, top + jnp.log(total), lse_all)
        attn += nn(attended[:, block * span : (block + 1) * span], out_weights[block][...])
    lse_out[...] = lse_all
    attn_out[...] = attn
    middle = x + gate_one[...] * attn
    second_out[...] = (normalize(middle)[0] * (1.0 + scale_two[...]) + shift_two[...]).astype(BF16)


def rows_of(owner, rows):
    return pl.multiple_of(flip(lax.axis_index("dp"), owner) * rows, 8)


def store_blocks(order, m, total, halves, rows, columns=slice(None)):
    half = len(order) // 2
    for place, owner in enumerate(order):
        if owner[1] == m:
            start = 0 if rows == total.shape[0] else rows_of(owner[0], rows)
            halves[place // half][place % half, :rows, :] = total[pl.ds(start, rows), columns].astype(BF16)


def row_block(seq, columns):
    return pl.BlockSpec((seq, columns), lambda i, *_: (i, 0))


def column_block(seq, width, number):
    return pl.BlockSpec((seq, width), lambda i, *_: (i, number))


def whole_block(array):
    return pl.BlockSpec(array.shape, lambda i, *_: (0,) * array.ndim, pipeline_mode=pl.Buffered(1))


def segment_blocks(seq):
    return [
        pl.BlockSpec((1, seq, 1), lambda i, *_: (i, 0, 0)),
        pl.BlockSpec((1, 1, seq), lambda i, *_: (i, 0, 0)),
    ]


def run_forward(patches, modulation, segments, qkv_parts, out_parts):
    rows, seq = segments.shape
    tokens, width = patches.shape
    columns = qkv_parts[0].shape[0]
    heads = columns // (3 * HEAD_DIM)
    work = rows * 4 * heads * seq * seq
    shapes = (
        [(width, BF16)] + [(columns, BF16)] * 4 + [(width, BF16), (128, F32), (width, F32), (width, BF16)]
    )
    return pl.pallas_call(
        functools.partial(forward_kernel, heads),
        grid=(rows,),
        in_specs=[row_block(seq, width)]
        + [column_block(seq, width, n) for n in range(5)]
        + segment_blocks(seq)
        + [whole_block(w) for w in qkv_parts + out_parts],
        out_specs=[row_block(seq, c) for c, _ in shapes],
        out_shape=[jax.ShapeDtypeStruct((tokens, c), t) for c, t in shapes],
        compiler_params=pltpu.CompilerParams(vmem_limit_bytes=62 << 20),
        cost_estimate=cost(
            flops=4 * work * HEAD_DIM + 8 * tokens * width * width,
            bytes_accessed=40 * tokens * width,
            transcendentals=work,
        ),
        name="attention_half",
    )(
        patches,
        *([modulation] * 5),
        segments[:, :, None],
        segments[:, None, :],
        *qkv_parts,
        *out_parts,
    )


def attention_back_kernel(
    heads,
    exchange,
    order,
    rows,
    base,
    scale_one,
    gate_one,
    scale_two,
    attn,
    cotangent,
    summed,
    normed,
    attended,
    lse,
    seg_col,
    seg_row,
    *refs,
):
    qkv, weights, out_weights = refs[:4], refs[4:8], refs[8:12]
    number = len(exchange.operands)
    moved, refs = refs[12 : 12 + number], refs[12 + number :]
    patches_grad, pieces, halves, refs = refs[0], refs[1], refs[2:4], refs[4:]
    number = len(exchange.shapes)
    moved_out, refs = refs[:number], refs[number:]
    totals, grad_qkv, refs = refs[:4], refs[4], refs[5:]
    step, last = pl.program_id(0), pl.num_programs(0) - 1
    exchange.bind(moved, moved_out, refs)

    @pl.when(step == 0)
    def _():
        exchange.begin()

    span = heads * HEAD_DIM
    width = base.shape[1]
    factor = HEAD_DIM**-0.5
    same = seg_col[0] == seg_row[0]
    grad, branch, gate = summed[...], attn[...], gate_one[...]
    normal, inverse = normalize(base[...].astype(F32) + gate * branch)
    middle_grad = cotangent[...].astype(F32) + normalize_back(
        normal, inverse, grad * (1.0 + scale_two[...])
    )
    patches_grad[...] = middle_grad
    pieces[:, 2 * width : 3 * width] = (middle_grad * branch).astype(BF16)
    pieces[:, 3 * width : 4 * width] = grad.astype(BF16)
    pieces[:, 4 * width :] = (grad * normal).astype(BF16)
    upper = (middle_grad * gate).astype(BF16)
    normed_grad = jnp.zeros(base.shape, F32)
    for block in range(4):
        if block == 0:

            @pl.when(step == last)
            def _():
                exchange.early(0, 1)

        if block == 2:

            @pl.when(step == last)
            def _():
                exchange.early(1)

        grad_heads = nt(upper, out_weights[block][...]).astype(BF16)
        for head in range(heads):
            at = head * HEAD_DIM
            n = block * heads + head
            q = qkv[block][:, at : at + HEAD_DIM]
            k = qkv[block][:, span + at : span + at + HEAD_DIM]
            v = qkv[block][:, 2 * span + at : 2 * span + at + HEAD_DIM]
            g = grad_heads[:, at : at + HEAD_DIM]
            scores = jnp.where(same, nt(q, k) * factor, -1000000000.0)
            probs = jnp.exp(scores - lse[:, n : n + 1])
            grad_probs = nt(g, v)
            term = jnp.sum(probs * grad_probs, axis=-1, keepdims=True)
            grad_scores = (probs * (grad_probs - term)).astype(BF16)
            grad_qkv[:, at : at + HEAD_DIM] = (nn(grad_scores, k) * factor).astype(BF16)
            grad_qkv[:, span + at : span + at + HEAD_DIM] = (tn(grad_scores, q) * factor).astype(BF16)
            grad_qkv[:, 2 * span + at : 2 * span + at + HEAD_DIM] = tn(
                probs.astype(BF16), g
            ).astype(BF16)
        made = grad_qkv[...]
        normed_grad += nn(made, weights[block][...])
        of_qkv = tn(normed[...], made)
        of_out = tn(upper, attended[:, block * span : (block + 1) * span])

        @pl.when(step == 0)
        def _():
            totals[block][:, : 3 * span] = of_qkv
            totals[block][:, 3 * span :] = of_out

        @pl.when(step > 0)
        def _():
            totals[block][:, : 3 * span] += of_qkv
            totals[block][:, 3 * span :] += of_out

        @pl.when(step == last)
        def _():
            store_blocks(order, MP_ORDER[block], totals[block], halves, rows)

    normal, inverse = normalize(base[...].astype(F32))
    patches_grad[...] += normalize_back(normal, inverse, normed_grad * (1.0 + scale_one[...]))
    pieces[:, :width] = normed_grad.astype(BF16)
    pieces[:, width : 2 * width] = (normed_grad * normal).astype(BF16)

    @pl.when(step == last)
    def _():
        exchange.finish()


def run_attention_back(
    patches,
    modulation,
    attn,
    cotangent,
    summed,
    normed,
    attended,
    lse,
    segments,
    qkv,
    qkv_parts,
    out_parts,
    order,
    rows,
    jobs,
    number,
):
    count, seq = segments.shape
    tokens, width = patches.shape
    columns = qkv[0].shape[1]
    heads = columns // (3 * HEAD_DIM)
    work = count * 4 * heads * seq * seq
    wide = row_block(seq, width)
    half = (len(order) // 2, rows, 4 * columns // 3)
    exchange = Exchange(jobs)
    results = pl.pallas_call(
        functools.partial(attention_back_kernel, heads, exchange, order, rows),
        grid_spec=pltpu.PrefetchScalarGridSpec(
            num_scalar_prefetch=0,
            grid=(count,),
            in_specs=[wide]
            + [column_block(seq, width, n) for n in (1, 2, 4)]
            + [wide] * 5
            + [row_block(seq, 128)]
            + segment_blocks(seq)
            + [row_block(seq, columns)] * 4
            + [whole_block(w) for w in qkv_parts + out_parts]
            + exchange.in_specs,
            out_specs=[wide, row_block(seq, 5 * width)]
            + [pl.BlockSpec(half, lambda i, *_: (0, 0, 0))] * 2
            + exchange.out_specs,
            scratch_shapes=[pltpu.VMEM((width, 4 * columns // 3), F32)] * 4
            + [pltpu.VMEM((seq, columns), BF16)]
            + exchange.scratch,
        ),
        out_shape=[
            jax.ShapeDtypeStruct((tokens, width), F32),
            jax.ShapeDtypeStruct((tokens, 5 * width), BF16),
        ]
        + [jax.ShapeDtypeStruct(half, BF16)] * 2
        + exchange.shapes,
        compiler_params=remote(exchange, number, 62),
        cost_estimate=cost(
            flops=10 * work * HEAD_DIM + 16 * tokens * width * width,
            bytes_accessed=60 * tokens * width,
            transcendentals=work,
        ),
        name="attention_back",
    )(
        patches,
        *([modulation] * 3),
        attn,
        cotangent,
        summed,
        normed,
        attended,
        lse,
        segments[:, :, None],
        segments[:, None, :],
        *qkv,
        *qkv_parts,
        *out_parts,
        *exchange.operands,
    )
    exchange.spread(results[4:])
    return results[:4]


BIAS_ROWS = 16


def tail_kernel(
    orders,
    rows,
    exchange,
    cond,
    silu_cond,
    base,
    attn,
    gate_one,
    gate_two,
    cotangent,
    mlp,
    pieces,
    weight,
    *refs,
):
    number = len(exchange.operands)
    moved, refs = refs[:number], refs[number:]
    cond_grad, output, qkv_grad, out_grad, ada_grad, bias_grad, refs = *refs[:6], refs[6:]
    number = len(exchange.jobs) - 3
    late, refs = refs[:number], refs[number:]
    modulation_grad, weight_here, total, load_sems, refs = *refs[:4], refs[4:]
    exchange.bind(moved, (), refs)
    tokens, width = base.shape
    pieces_load = pltpu.make_async_copy(
        pieces, modulation_grad.at[:, pl.ds(0, pieces.shape[1])], load_sems.at[0]
    )
    weight_load = pltpu.make_async_copy(weight, weight_here, load_sems.at[1])
    pieces_load.start()
    weight_load.start()
    exchange.begin()
    grad_out, branch = cotangent[...].astype(F32), mlp[...]
    modulation_grad[:, 5 * width :] = (grad_out * branch).astype(BF16)
    middle = base[...].astype(F32) + gate_one[...] * attn[...]
    output[...] = (middle + gate_two[...] * branch).astype(BF16)
    pieces_load.wait()

    columns = modulation_grad.shape[1] // 4
    split = columns // 2
    heads = qkv_grad.shape[1]
    mp = lax.axis_index("mp")

    def keep_heads(value):
        qkv_grad[...] = value[:, :heads]
        out_grad[...] = value[:, heads:]

    def keep_low(value):
        ada_grad[:, :split] = value[:rows]
        bias_grad[...] = value[rows:]

    def keep_high(value):
        ada_grad[:, split:] = value

    def keep_late(target, value):
        target[...] = value

    exchange.sinks = {0: keep_low, 1: keep_high, 2: keep_heads}
    for n, target in enumerate(late):
        exchange.sinks[3 + n] = functools.partial(keep_late, target)
    bias = jnp.sum(modulation_grad[...].astype(F32), axis=0, keepdims=True).astype(BF16)
    lines = [bias[:, n * split : (n + 1) * split] for n in range(8)]
    lines = jnp.concatenate(lines + [jnp.zeros_like(lines[0])] * (BIAS_ROWS - 8), axis=0)
    for place in range(len(orders[0])):
        half = len(orders[0]) // 2
        exchange.halves(0)[place // half][place % half, rows:, :] = lines
    half = MP_ORDER[len(MP_ORDER) // 2 :]
    for m in half + [m for m in MP_ORDER if m not in half]:
        first = pl.multiple_of(flip(mp, m) * columns, 128)
        total[...] = tn(silu_cond[...], modulation_grad[:, pl.ds(first, columns)])
        for part, order in enumerate(orders):
            own = slice(part * split, (part + 1) * split)
            store_blocks(order, m, total, exchange.halves(part), rows, own)
        if m == half[0]:
            exchange.advance(2)
        if m == half[-1]:
            exchange.start(0)
            exchange.start(1)
            for n in range(len(late)):
                exchange.advance(3 + n)
    exchange.advance(0)
    exchange.advance(1)
    weight_load.wait()
    value = cond[...].astype(F32)
    gate = 1.0 / (1.0 + jnp.exp(-value))
    cond_grad[...] = nt(modulation_grad[...], weight_here[...]) * (gate * (1.0 + value * (1.0 - gate)))
    for n in (2, 0, 1, 2):
        exchange.advance(n) if exchange.left(n) > 1 else None
    for n in range(len(late)):
        exchange.advance(3 + n)
    for n in (0, 2, 1):
        exchange.advance(n) if exchange.left(n) > 1 else None
    exchange.finish()


def run_tail(
    conditioning, silu_cond, patches, attn, modulation, cotangent, mlp, pieces, ada_weight, orders, rows, jobs, number
):
    tokens, width = silu_cond.shape
    exchange = Exchange(jobs, True)
    anywhere = pl.BlockSpec(memory_space=pl.ANY)
    columns = ada_weight.shape[1] // 4
    heads = jobs[2][0].shape[2]
    whole = lambda columns: pl.BlockSpec((tokens, columns), lambda i: (0, 0), pipeline_mode=pl.Buffered(1))
    gate = lambda n: pl.BlockSpec((tokens, width), lambda i: (0, n), pipeline_mode=pl.Buffered(1))
    shapes = [
        jax.ShapeDtypeStruct((tokens, width), F32),
        jax.ShapeDtypeStruct((tokens, width), BF16),
        jax.ShapeDtypeStruct((rows, heads * 3 // 4), F32),
        jax.ShapeDtypeStruct((rows, heads // 4), F32),
        jax.ShapeDtypeStruct((rows, columns), F32),
        jax.ShapeDtypeStruct((BIAS_ROWS, columns // 2), F32),
    ]
    shapes += [jax.ShapeDtypeStruct(chain.shape[1:], F32) for chain, _ in jobs[3:]]
    return pl.pallas_call(
        functools.partial(tail_kernel, orders, rows, exchange),
        grid=(1,),
        in_specs=[whole(width)] * 4
        + [gate(2), gate(5)]
        + [whole(width)] * 2
        + [anywhere] * 2
        + exchange.in_specs,
        out_specs=[constant_block(shape) for shape in shapes],
        out_shape=shapes,
        scratch_shapes=[
            pltpu.VMEM((tokens, ada_weight.shape[1]), BF16),
            pltpu.VMEM(ada_weight.shape, BF16),
            pltpu.VMEM((width, columns), F32),
            pltpu.SemaphoreType.DMA((2,)),
        ]
        + exchange.scratch,
        compiler_params=remote(exchange, number, 63),
        cost_estimate=cost(
            flops=16 * tokens * width * ada_weight.shape[1], bytes_accessed=100 * width * width, transcendentals=0
        ),
        name="tail",
    )(
        conditioning,
        silu_cond,
        patches,
        attn,
        modulation,
        modulation,
        cotangent,
        mlp,
        pieces,
        ada_weight,
        *exchange.operands,
    )


def finish_kernel(moves, rows, *refs):
    parts, refs = refs[: len(moves)], refs[len(moves) :]
    half = (len(refs) - 4) // 2
    plain, outs, experts = refs[:half], refs[half : 2 * half], refs[2 * half :]
    for source, target in zip(plain, outs):
        target[...] = source[...]
    for part, (expert, first, last) in zip(parts, moves):
        for kind in range(2):
            value = part[0, kind * rows : (kind + 1) * rows, :]
            if expert is None:
                experts[2 + kind][:, first:last] = value
            else:
                experts[kind][expert, :, first:last] = value


def run_finish(moves, plain, experts, rows, width):
    def block(array, index):
        return pl.BlockSpec((1,) + array.shape[1:], lambda i: (index, 0, 0), pipeline_mode=pl.Buffered(1))

    shapes = [jax.ShapeDtypeStruct(a.shape, a.dtype) for a in plain]
    shapes += [jax.ShapeDtypeStruct((experts, rows, width), F32)] * 2
    shapes += [jax.ShapeDtypeStruct((rows, width), F32)] * 2
    return pl.pallas_call(
        functools.partial(finish_kernel, [move[2:] for move in moves], rows),
        grid=(1,),
        in_specs=[block(array, index) for array, index, *_ in moves] + [whole_block(a) for a in plain],
        out_specs=[constant_block(shape) for shape in shapes],
        out_shape=shapes,
        compiler_params=pltpu.CompilerParams(vmem_limit_bytes=60 << 20),
        name="finish",
    )(*[move[0] for move in moves], *plain)


def gelu_and_slope(values):
    square = values * values
    bent = jnp.tanh(values * (GELU_A + (GELU_A * GELU_B) * square))
    half = 0.5 * (1.0 + bent)
    active = values * half
    return active, half + active * (1.0 - bent) * (GELU_A + (3.0 * GELU_A * GELU_B) * square)


class Gather:
    def __init__(self, own, far, held, send_sems, recv_sems):
        self.own, self.far, self.held, self.send_sems, self.recv_sems = own, far, held, send_sems, recv_sems

    def copy(self, place):
        far = self.held.at[1] if self.far is None else self.far
        return pltpu.make_async_remote_copy(
            src_ref=far if place == 2 else self.own,
            dst_ref=self.held.at[place],
            send_sem=self.send_sems.at[place],
            recv_sem=self.recv_sems.at[place],
            device_id=Exchange.partner("mp", 2 if place == 1 else 1),
            device_id_type=pl.DeviceIdType.MESH,
        )

    def begin(self):
        self.held[3] = self.own[...]
        if self.far is None:
            self.copy(1).start()
            self.copy(0).start()
        else:
            self.held[1] = self.far[...]
            self.copy(0).start()
            self.copy(2).start()

    def tile(self, step):
        @pl.when(step == 1)
        def _():
            self.copy(0).wait()

        if self.far is None:

            @pl.when(step == 2)
            def _():
                self.copy(1).wait()
                self.copy(2).start()

        @pl.when(step == 3)
        def _():
            self.copy(2).wait()

        return self.held[(step + 3) % 4]


def gather_barrier():
    barrier = pltpu.get_barrier_semaphore()
    for mask in (1, 2):
        pl.semaphore_signal(
            barrier, inc=1, device_id=Exchange.partner("mp", mask), device_id_type=pl.DeviceIdType.MESH
        )
    pl.semaphore_wait(barrier, 2)


def expert_kernel(columns, gathers, first, last, grad_later, exchange, units, rows, *refs):
    count = len(columns)
    gates, tokens, grads, refs = *refs[:3], refs[3:]
    if gathers:
        grads_far, refs = refs[0], refs[1:]
    ups, downs, refs = refs[:count], refs[count : 2 * count], refs[2 * count :]
    if not first:
        old_out, old_back, refs = refs[0], refs[1], refs[2:]
    number = len(exchange.operands)
    moved, refs = refs[:number], refs[number:]
    number = 2 * count if grad_later else sum(2 * len(own) for own in units)
    halves, refs = refs[:number], refs[number:]
    number = 4 if last else 2
    made, refs = refs[:number], refs[number:]
    number = len(exchange.shapes)
    moved_out, refs = refs[:number], refs[number:]
    if gathers:
        gathered, refs = refs[:2], refs[2:]
    number = 0 if grad_later else 2 * count
    sums, refs = refs[:number], refs[number:]
    step, final = pl.program_id(0), pl.num_programs(0) - 1
    if gathers:
        gather = [Gather(tokens, None, *refs[:3]), Gather(grads, grads_far, *refs[3:6])]
        refs = refs[6:]
    exchange.bind(moved, moved_out, refs)

    @pl.when(step == 0)
    def _():
        exchange.begin()

    @pl.when(step == 2)
    def _():
        exchange.early()

    if not grad_later:
        start_sums(step, sums)
    if gathers:

        @pl.when(step == 0)
        def _():
            gather_barrier()
            for one in gather:
                one.begin()

        x, own_grads = [one.tile(step) for one in gather]
        gathered[0][...] = x
        gathered[1][...] = own_grads
    else:
        x, own_grads = tokens[...], grads[...]
    g32 = own_grads.astype(F32)
    routed = None if first else old_out[...]
    returned = None if first else old_back[...]
    for n, column in enumerate(columns):
        gate = gates[:, column : column + 1]
        slot_grad = (gate * g32).astype(BF16)
        hidden, grad_pre, one, two = expert_pass(x, slot_grad, gate, ups[n][0], downs[n][0])
        routed = one if routed is None else routed + one
        returned = two if returned is None else returned + two
        if grad_later:
            halves[2 * n][...] = hidden
            halves[2 * n + 1][...] = grad_pre
        else:
            sums[2 * n][...] += tn(x, grad_pre)
            sums[2 * n + 1][...] += tn(slot_grad, hidden)
    if last:
        for value, (kept, sent) in ((routed, made[:2]), (returned, made[2:])):

            @pl.when(step < 2)
            def _():
                kept[0] = value.astype(BF16)

            @pl.when(step >= 2)
            def _():
                sent[0] = value.astype(BF16)

    else:
        made[0][...] = routed
        made[1][...] = returned
    if not grad_later:
        store_halves(step, units, sums, halves, rows)

    @pl.when(step == final)
    def _():
        exchange.finish()


def start_sums(step, sums):
    @pl.when(step == 0)
    def _():
        for total in sums:
            total[...] = jnp.zeros_like(total)


def store_units(units, sums, targets, rows):
    for (columns, order), halves in zip(units, targets):
        half = len(order) // 2
        for place, owner in enumerate(order):
            start = place * rows if half == 1 else rows_of(owner, rows)
            for part, total in enumerate(sums):
                halves[place // half][place % half, part * rows : (part + 1) * rows, :] = total[
                    pl.ds(start, rows), columns
                ].astype(BF16)


def store_halves(step, units, sums, halves, rows):
    @pl.when(step == pl.num_programs(0) - 1)
    def _():
        start = 0
        for n, own in enumerate(units):
            pairs = [halves[start + 2 * u : start + 2 * u + 2] for u in range(len(own))]
            start += 2 * len(own)
            store_units(own, sums[2 * n : 2 * n + 2], pairs, rows)


def unit_shapes(units, rows, width):
    shapes = []
    for columns, order in units:
        number = len(range(*columns.indices(width)))
        shapes += [jax.ShapeDtypeStruct((len(order) // 2, 2 * rows, number), BF16)] * 2
    return shapes


def constant_block(shape):
    return pl.BlockSpec(shape.shape, lambda *_: (0,) * len(shape.shape))


def expert_pass(x, slot_grad, gate, up, down):
    pre = nn(x, up)
    grad_hidden = nt(slot_grad, down)
    hidden, slope = gelu_and_slope(pre)
    hidden = hidden.astype(BF16)
    grad_pre = (grad_hidden * slope).astype(BF16)
    return hidden, grad_pre, gate * nn(hidden, down), nt(grad_pre, up)


TILE = 512


def token_tiles(columns):
    return pl.BlockSpec((TILE, columns), lambda t: (t, 0))


def run_experts(
    columns, weights, units, rows, gates, tokens, grads, sums, last, grad_later, jobs, number, gathers=False
):
    count = len(columns)
    total, width = gates.shape[0], tokens.shape[1]
    hidden = weights[0][0].shape[2]
    steps = total // TILE
    first = sums is None
    exchange = Exchange(jobs)

    def weight(index, shape):
        return pl.BlockSpec((1,) + shape, lambda t: (index, 0, 0), pipeline_mode=pl.Buffered(1))

    def tiles(columns):
        return pl.BlockSpec((TILE, columns), lambda t: ((t % 2) * 2 + t // 2 if gathers else t, 0))

    in_specs = (
        [tiles(gates.shape[1])]
        + ([pl.BlockSpec((TILE, width), lambda t: (0, 0))] * 3 if gathers else [tiles(width)] * 2)
        + [weight(i, (width, hidden)) for _, _, i in weights]
        + [weight(i, (hidden, width)) for _, _, i in weights]
        + ([] if first else [token_tiles(width), token_tiles(width)])
    )
    given = len(in_specs)
    if grad_later:
        shapes = [jax.ShapeDtypeStruct((total, hidden), BF16)] * (2 * count)
        specs = [token_tiles(hidden)] * (2 * count)
    else:
        shapes = [shape for own in units for shape in unit_shapes(own, rows, hidden)]
        specs = [constant_block(shape) for shape in shapes]
    made = len(shapes)
    if last:
        block = (1, TILE, width)
        sum_specs = [
            pl.BlockSpec(block, lambda t: (jnp.minimum(t, 1), 0, 0)),
            pl.BlockSpec(block, lambda t: (jnp.maximum(t - 2, 0), 0, 0)),
        ] * 2
        sum_shapes = [jax.ShapeDtypeStruct((2, TILE, width), BF16)] * 4
    else:
        sum_specs = [tiles(width)] * 2
        sum_shapes = [jax.ShapeDtypeStruct((total, width), F32)] * 2
    gather_scratch, gather_shapes = [], []
    if gathers:
        gather_scratch = ([pltpu.VMEM((4, TILE, width), BF16)] + [pltpu.SemaphoreType.DMA((3,))] * 2) * 2
        gather_shapes = [jax.ShapeDtypeStruct((total, width), BF16)] * 2
    aliases = {} if first or last else {given - 2: made, given - 1: made + 1}
    results = pl.pallas_call(
        functools.partial(expert_kernel, columns, gathers, first, last, grad_later, exchange, units, rows),
        grid_spec=pltpu.PrefetchScalarGridSpec(
            num_scalar_prefetch=0,
            grid=(steps,),
            in_specs=in_specs + exchange.in_specs,
            out_specs=specs + sum_specs + exchange.out_specs + [tiles(width)] * (2 * gathers),
            scratch_shapes=([] if grad_later else [pltpu.VMEM((width, hidden), F32)] * (2 * count))
            + gather_scratch
            + exchange.scratch,
        ),
        out_shape=shapes + sum_shapes + exchange.shapes + gather_shapes,
        input_output_aliases=aliases,
        compiler_params=remote(exchange, number, 60, gathers),
        cost_estimate=cost(
            flops=(8 if grad_later else 12) * count * total * width * hidden,
            bytes_accessed=20 * total * width + 8 * count * width * hidden,
            transcendentals=count * total * hidden,
        ),
        name=f"experts_{count}",
    )(
        gates,
        tokens,
        *(grads if gathers else [grads]),
        *[up for up, _, _ in weights],
        *[down for _, down, _ in weights],
        *(() if first else sums),
        *exchange.operands,
    )
    number = made + len(sum_shapes)
    if gathers:
        return results[:made], results[made:number], results[number:]
    exchange.spread(results[number:])
    return results[:made], results[made:number]


SLOTS = 3


def long_kernel(count, exchange, units, unit_steps, rows, gates, tokens, grads, up, down, *refs):
    old = refs[:2]
    number = len(exchange.operands)
    moved, refs = refs[2 : 2 + number], refs[2 + number :]
    new, finals, last_final, refs = refs[:2], refs[2], refs[3], refs[4:]
    number = 2 * len(units)
    half_done, raw, refs = refs[:number], refs[number : 2 * number], refs[2 * number :]
    number = len(exchange.shapes)
    moved_out, refs = refs[:number], refs[number:]
    sums, totals, send, work, gots = refs[:2], refs[2:4], refs[4], refs[5], refs[6:9]
    send_sems, recv_sems, load_sems, store_sems, refs = *refs[9:13], refs[13:]
    exchange.bind(moved, moved_out, refs)
    e, t = pl.program_id(0), pl.program_id(1)
    tiles = 4

    def copy(chain, step, unit):
        slot = chain % SLOTS
        blocks = 4 >> step
        columns = units[unit][0]
        place = pl.ds(columns.start, columns.stop - columns.start)
        source = send if step == 0 else work
        first = 0 if step == 0 else blocks
        return pltpu.make_async_remote_copy(
            src_ref=source.at[slot, pl.ds(first, blocks), :, place],
            dst_ref=gots[step].at[slot, :, :, place],
            send_sem=send_sems.at[slot, step, unit],
            recv_sem=recv_sems.at[slot, step, unit],
            device_id=exchange.partner(*unit_steps[unit][step]),
            device_id_type=pl.DeviceIdType.MESH,
        )

    def launch(chain, step):
        for unit in range(len(units)):
            copy(chain, step, unit).start()

    def arrive(chain, step):
        for unit in range(len(units)):
            copy(chain, step, unit).wait()

    def add(chain, step):
        slot = chain % SLOTS

        def one(i, carry):
            total = work[slot, i].astype(F32) + gots[step][slot, i].astype(F32)
            work[slot, i] = total.astype(BF16)
            return carry

        lax.fori_loop(0, 4 >> step, one, 0)

    def close(chain, target):
        arrive(chain, 2)
        slot = chain % SLOTS
        target[0] = work[slot, 0].astype(F32) + gots[2][slot, 0].astype(F32)

    def loads(n, tile):
        return pltpu.make_async_copy(
            old[n].at[pl.ds(tile * TILE, TILE), :], totals[n].at[tile], load_sems.at[n, tile]
        )

    def stores(n, tile):
        return pltpu.make_async_copy(
            totals[n].at[tile], new[n].at[pl.ds(tile * TILE, TILE), :], store_sems.at[n, tile]
        )

    @pl.when((e == 0) & (t == 0))
    def _():
        for tile in range(tiles):
            for n in range(2):
                loads(n, tile).start()
        exchange.begin(sorted({step for steps in unit_steps for step in steps}))

    for tile in range(tiles):

        @pl.when((e == 0) & (t == tile))
        def _():
            for n in range(2):
                loads(n, tile).wait()

    @pl.when((e == 1) & (t == 0))
    def _():
        exchange.all_once()

    @pl.when((e == 1) & (t == 2))
    def _():
        exchange.all_once()

    @pl.when((e == 2) & (t == 0))
    def _():
        exchange.finish()

    @pl.when((e >= 2) & (t == 0))
    def _():
        arrive(e - 2, 0)
        add(e - 2, 0)
        launch(e - 2, 1)

    @pl.when((e >= 1) & (t == 0))
    def _():
        launch(e - 1, 0)

    @pl.when((e >= 3) & (t == 2))
    def _():
        close(e - 3, finals)

    @pl.when((e >= 2) & (t == 2))
    def _():
        arrive(e - 2, 1)
        add(e - 2, 1)
        launch(e - 2, 2)

    @pl.when(t == 0)
    def _():
        for total in sums:
            total[...] = jnp.zeros_like(total)

    lane = lax.broadcasted_iota(jnp.int32, (1, gates.shape[1]), 1)
    gate = jnp.sum(jnp.where(lane == e, gates[...], 0.0), axis=1, keepdims=True)
    x = tokens[...]
    slot_grad = (gate * grads[...].astype(F32)).astype(BF16)
    hidden, grad_pre, one, two = expert_pass(x, slot_grad, gate, up[0], down[0])
    totals[0][t] += one
    totals[1][t] += two
    sums[0][...] += tn(x, grad_pre)
    sums[1][...] += tn(slot_grad, hidden)

    for tile in range(tiles):

        @pl.when((e == count - 1) & (t == tile))
        def _():
            for n in range(2):
                stores(n, tile).start()

    @pl.when((t == tiles - 1) & (e < count - 1))
    def _():
        slot = e % SLOTS
        pairs = [
            (work.at[slot, :, :, pl.ds(c.start, c.stop - c.start)], send.at[slot, :, :, pl.ds(c.start, c.stop - c.start)])
            for c, _ in units
        ]
        store_units(units, sums, pairs, rows)

    @pl.when((t == tiles - 1) & (e == count - 1))
    def _():
        store_units(units, sums, [raw[2 * u : 2 * u + 2] for u in range(len(units))], rows)
        close(count - 3, last_final)
        arrive(count - 2, 0)
        add(count - 2, 0)
        slot = (count - 2) % SLOTS
        for u, (c, _) in enumerate(units):
            half_done[2 * u][...] = work[slot, 0:2, :, c]
            half_done[2 * u + 1][...] = work[slot, 2:4, :, c]
        for tile in range(tiles):
            for n in range(2):
                stores(n, tile).wait()


def run_long(count, units, unit_steps, rows, gates, tokens, grads, expert_up, expert_down, sums, jobs, number):
    total, width = tokens.shape
    hidden = expert_up.shape[2]
    exchange = Exchange(jobs)
    steps = total // TILE
    tile = lambda columns: pl.BlockSpec((TILE, columns), lambda e, t: (t, 0))
    weight = lambda shape: pl.BlockSpec((1,) + shape, lambda e, t: (e, 0, 0))
    anywhere = pl.BlockSpec(memory_space=pl.ANY)
    raw = unit_shapes(units, rows, hidden)
    half_done = [jax.ShapeDtypeStruct((s.shape[0] // 2,) + s.shape[1:], BF16) for s in raw]
    final = (1, 2 * rows, hidden)
    results = pl.pallas_call(
        functools.partial(long_kernel, count, exchange, units, unit_steps, rows),
        grid=(count, steps),
        in_specs=[
            tile(gates.shape[1]),
            tile(width),
            tile(width),
            weight((width, hidden)),
            weight((hidden, width)),
            anywhere,
            anywhere,
        ]
        + exchange.in_specs,
        out_specs=[anywhere, anywhere]
        + [pl.BlockSpec(final, lambda e, t: (jnp.maximum(e - 3, 0), 0, 0)), pl.BlockSpec(final, lambda e, t: (0, 0, 0))]
        + [constant_block(shape) for shape in half_done + raw]
        + exchange.out_specs,
        out_shape=[jax.ShapeDtypeStruct((total, width), F32)] * 2
        + [jax.ShapeDtypeStruct((count - 3,) + final[1:], F32), jax.ShapeDtypeStruct(final, F32)]
        + half_done
        + raw
        + exchange.shapes,
        scratch_shapes=[pltpu.VMEM((width, hidden), F32)] * 2
        + [pltpu.VMEM((steps, TILE, width), F32)] * 2
        + [pltpu.VMEM((SLOTS, 4, 2 * rows, hidden), BF16)] * 2
        + [pltpu.VMEM((SLOTS, 4 >> n, 2 * rows, hidden), BF16) for n in range(3)]
        + [pltpu.SemaphoreType.DMA((SLOTS, 3, len(units)))] * 2
        + [pltpu.SemaphoreType.DMA((2, steps))] * 2
        + exchange.scratch,
        compiler_params=remote(exchange, number, 62),
        cost_estimate=cost(
            flops=12 * count * total * width * hidden,
            bytes_accessed=8 * count * total * width,
            transcendentals=count * total * hidden,
        ),
        name="experts_long",
    )(gates, tokens, grads, expert_up, expert_down, *sums, *exchange.operands)
    made = len(raw)
    exchange.spread(results[4 + 2 * made :])
    finished = [(results[2], n) for n in range(count - 3)] + [(results[3], 0)]
    return results[:2], finished, results[4 : 4 + made], results[4 + made : 4 + 2 * made]


def expert_grads_kernel(columns, exchange, units, rows, *refs):
    count = len(columns)
    gates, tokens, grads = refs[:3]
    saved, refs = refs[3 : 3 + 2 * count], refs[3 + 2 * count :]
    number = len(exchange.operands)
    moved, refs = refs[:number], refs[number:]
    number = sum(2 * len(own) for own in units)
    halves, refs = refs[:number], refs[number:]
    number = len(exchange.shapes)
    moved_out, refs = refs[:number], refs[number:]
    sums, refs = refs[: 2 * count], refs[2 * count :]
    step, final = pl.program_id(0), pl.num_programs(0) - 1
    exchange.bind(moved, moved_out, refs)

    @pl.when(step == 0)
    def _():
        exchange.begin()

    @pl.when(step == 1)
    def _():
        exchange.early(0, 1)

    @pl.when(step == 2)
    def _():
        exchange.early(1)

    start_sums(step, sums)
    x = tokens[...]
    g32 = grads[...].astype(F32)
    for n, column in enumerate(columns):
        slot_grad = (gates[:, column : column + 1] * g32).astype(BF16)
        sums[2 * n][...] += tn(x, saved[2 * n + 1][...])
        sums[2 * n + 1][...] += tn(slot_grad, saved[2 * n][...])
    store_halves(step, units, sums, halves, rows)

    @pl.when(step == final)
    def _():
        exchange.finish()


def run_expert_grads(columns, saved, units, rows, gates, tokens, grads, jobs, number):
    count = len(columns)
    total, width = tokens.shape
    hidden = saved[0].shape[1]
    steps = total // TILE
    shapes = [shape for own in units for shape in unit_shapes(own, rows, hidden)]
    exchange = Exchange(jobs)
    results = pl.pallas_call(
        functools.partial(expert_grads_kernel, columns, exchange, units, rows),
        grid_spec=pltpu.PrefetchScalarGridSpec(
            num_scalar_prefetch=0,
            grid=(steps,),
            in_specs=[token_tiles(gates.shape[1]), token_tiles(width), token_tiles(width)]
            + [token_tiles(hidden)] * (2 * count)
            + exchange.in_specs,
            out_specs=[constant_block(shape) for shape in shapes] + exchange.out_specs,
            scratch_shapes=[pltpu.VMEM((width, hidden), F32)] * (2 * count) + exchange.scratch,
        ),
        out_shape=shapes + exchange.shapes,
        compiler_params=remote(exchange, number, 60),
        cost_estimate=cost(
            flops=4 * count * total * width * hidden,
            bytes_accessed=(4 + 4 * count) * total * width,
            transcendentals=0,
        ),
        name="expert_grads",
    )(gates, tokens, grads, *saved, *exchange.operands)
    exchange.spread(results[len(shapes) :])
    return results[: len(shapes)]


def local(
    patches,
    conditioning,
    cotangent,
    segments,
    routes,
    gate_values,
    ada_weight,
    ada_bias,
    qkv_weight,
    out_weight,
    shared_up,
    shared_down,
    expert_up,
    expert_down,
):
    tokens, width = patches.shape
    group = routes.shape[0]
    experts = expert_up.shape[0]
    seq = segments.shape[1]
    n_dp, n_mp = lax.axis_size("dp"), lax.axis_size("mp")
    dp, mp = lax.axis_index("dp"), lax.axis_index("mp")
    rows = width // n_dp

    qkv_parts = gather_mp(jnp.transpose(qkv_weight, (1, 2, 0)).reshape(-1, width))
    out_parts = gather_mp(out_weight)

    silu_cond = jax.nn.silu(conditioning.astype(F32)).astype(BF16)
    modulation = jnp.dot(silu_cond, ada_weight, preferred_element_type=F32) + ada_bias[None, :]
    gate_two = modulation[:, 5 * width :]
    grad_mlp = (cotangent.astype(F32) * gate_two).astype(BF16)
    grad_mlp, *far = lax.optimization_barrier((grad_mlp, qkv_parts[1], out_parts[1]))
    qkv_parts[1], out_parts[1] = far
    grad_far = swap(grad_mlp, "mp", 2)

    own_rows = tokens // seq
    own_segments = lax.dynamic_slice_in_dim(segments, mp * own_rows, own_rows, axis=0)
    results = run_forward(patches, modulation, own_segments, qkv_parts, out_parts)
    normed_one, qkv, attended, lse, attn_out, normed_two = results[0], results[1:5], *results[5:]

    number = jnp.arange(16, dtype=jnp.int32)[None, :]
    gates = jnp.sum(
        jnp.where(routes[:, :, None] == number[:, None, :], gate_values[:, :, None], 0.0), axis=1
    )
    gates = jnp.where(number == experts, 1.0, gates)
    gates = jnp.concatenate(
        [lax.dynamic_slice_in_dim(gates, (mp ^ m) * tokens, tokens, axis=0) for m in MP_ORDER],
        axis=0,
    )
    shared = (shared_up[None], shared_down[None], 0)
    weights = {e: (expert_up, expert_down, e) for e in range(experts)}
    weights[experts] = shared
    even = halves_evenly(n_dp, rows)
    step = rows if even else width // 2
    reduced, chains, wholes = {}, {}, {}
    if even:
        near_step, far_step, *rest = dp_steps(n_dp)
        hidden = expert_up.shape[2]
        cut = hidden * 2 // 3
        unit_steps = [[near_step, far_step] + rest, [far_step, near_step] + rest]
        parts = [(slice(0, cut), unit_steps[0]), (slice(cut, hidden), unit_steps[1])]
        kinds = {c: parts for c in weights}
        kinds[experts - 2] = [(slice(0, hidden), unit_steps[1])]
        kinds[experts - 1] = [(slice(0, hidden), unit_steps[0])]
        units = {
            c: [(columns, [d for d, _ in block_order(steps)]) for columns, steps in kind]
            for c, kind in kinds.items()
        }
    else:
        units = {c: [(slice(0, expert_up.shape[2]), [0, 1])] for c in weights}

    def take_halves(columns, halves, done=0):
        halves = list(halves)
        for column in columns:
            own = [halves.pop(0) for _ in range(2 * len(units[column]))]
            if even:
                chains[column] = [
                    Chain(own[2 * u], own[2 * u + 1], steps, done)
                    for u, (_, steps) in enumerate(kinds[column])
                ]
            else:
                wholes[column] = own

    def jobs(**counts):
        if not even:
            return []
        return [(c, int(count[1:])) for count, columns in counts.items() for x in columns for c in chains[x]]

    def call(columns, sums, last, moves, number):
        return run_experts(
            columns,
            [weights[c] for c in columns],
            [units[c] for c in columns],
            step,
            gates,
            all_tokens,
            all_grads,
            sums,
            last,
            last,
            moves,
            number,
        )

    halves, sums, (all_tokens, all_grads) = run_experts(
        (experts,),
        [weights[experts]],
        [units[experts]],
        step,
        gates,
        normed_two,
        [grad_mlp, grad_far],
        None,
        False,
        False,
        [],
        0,
        True,
    )
    take_halves((experts,), halves)
    late = (experts - 2, experts - 1)
    if even:
        sums, finished, half_done, raw = run_long(
            experts - 2,
            units[0],
            unit_steps,
            rows,
            gates,
            all_tokens,
            all_grads,
            expert_up,
            expert_down,
            sums,
            jobs(n3=(experts,)),
            1,
        )
        take_halves((experts - 4,), half_done, 1)
        take_halves((experts - 3,), raw)
    else:
        for e in range(0, experts - 2, 2):
            halves, sums = call((e, e + 1), sums, False, [], 1 + e // 2)
            take_halves((e, e + 1), halves)
    saved, sums = call(late, sums, True, jobs(n2=(experts - 4,), n1=(experts - 3,)), 4)
    out_chain, back_chain = Chain(*sums[:2], MP_STEPS), Chain(*sums[2:], MP_STEPS)
    halves = run_expert_grads(
        late,
        saved,
        [units[c] for c in late],
        step,
        gates,
        all_tokens,
        all_grads,
        [(back_chain, 2)] + jobs(n2=(experts - 3,)),
        5,
    )
    take_halves(late, halves)
    tail_steps = [MP_STEPS] * 3
    if even:
        y, z, rest = dp_steps(n_dp)[0], dp_steps(n_dp)[1], dp_steps(n_dp)[2:]
        core, x = MP_STEPS
        tail_steps = [[core, x, y, z] + rest, [core, y, x, z] + rest, [core, x, y, z] + rest]
    tail_orders = [block_order(steps) for steps in tail_steps]

    tail_rows = rows if even else width
    results = run_attention_back(
        patches,
        modulation,
        attn_out,
        cotangent,
        back_chain.result,
        normed_one,
        attended,
        lse,
        own_segments,
        qkv,
        qkv_parts,
        out_parts,
        tail_orders[0],
        tail_rows,
        [(out_chain, 2)] + jobs(n1=late),
        6,
    )
    patches_grad, pieces, heads_halves = results[0], results[1], results[2:4]
    heads_chain = Chain(*heads_halves, tail_steps[0])
    split = ada_weight.shape[1] // n_mp // 2
    half = len(tail_orders[1]) // 2
    ada_chains = [
        Chain.inside((half, tail_rows + BIAS_ROWS, split), tail_steps[1]),
        Chain.inside((half, tail_rows, split), tail_steps[2]),
    ]
    number = len(tail_steps[0])
    results = run_tail(
        conditioning,
        silu_cond,
        patches,
        attn_out,
        modulation,
        cotangent,
        out_chain.result,
        pieces,
        ada_weight,
        tail_orders[1:],
        tail_rows,
        [(c, number) for c in ada_chains] + [(heads_chain, number)] + jobs(n2=late),
        7,
    )
    conditioning_grad, output, qkv_sum, out_total, ada_sum, bias_all = results[:6]
    bias_all = bias_all[: 2 * n_mp].reshape(-1)
    if even:
        moves = [(array, index, e, 0, hidden) for e, (array, index) in enumerate(finished)]
        moves += [(array[None], 0, column, 0, hidden) for column, array in zip(late, results[6:])]
        for column, own in chains.items():
            if column not in late:
                for chain, (columns, _) in zip(own, kinds[column]):
                    place = None if column == experts else column
                    moves.append((chain.result[None], 0, place, columns.start, columns.stop))
        results = run_finish(
            moves, [output, patches_grad, conditioning_grad, ada_sum], experts, rows, hidden
        )
        output, patches_grad, conditioning_grad, ada_sum = results[:4]
        expert_up_sum, expert_down_sum, up_sum, down_sum = results[4:]
    else:
        for column, (first, second) in wholes.items():
            whole = jnp.stack([first[0], second[0]]).reshape(2, 2, step, -1)
            whole = jnp.swapaxes(whole, 0, 1).reshape(2, width, -1)
            part = lax.psum_scatter(whole, "dp", scatter_dimension=1, tiled=True).astype(F32)
            reduced[column] = part[0], part[1]
        up_sum, down_sum = reduced[experts]
        expert_up_sum, expert_down_sum = [
            jnp.stack([reduced[e][part] for e in range(experts)]) for part in range(2)
        ]
        qkv_sum, out_total, ada_sum = [
            lax.psum_scatter(a.astype(BF16), "dp", scatter_dimension=0, tiled=True).astype(F32)
            for a in (qkv_sum, out_total, ada_sum)
        ]
        bias_all = lax.psum(bias_all, "dp")
    share = bias_all.shape[0] // (n_dp * n_mp)
    return (
        output,
        patches_grad,
        conditioning_grad,
        ada_sum,
        lax.dynamic_slice_in_dim(bias_all, (dp * n_mp + mp) * share, share),
        qkv_sum.reshape(rows, 3, -1),
        out_total.T,
        up_sum,
        down_sum.T,
        expert_up_sum,
        jnp.swapaxes(expert_down_sum, 1, 2),
    )


def solution(mesh):
    in_specs = (
        P(("dp", "mp"), None),
        P(("dp", "mp"), None),
        P(("dp", "mp"), None),
        P("dp", None),
        P("dp", None),
        P("dp", None),
        P(),
        P(),
        P(None, None, "mp"),
        P("mp", None),
        P(None, "mp"),
        P("mp", None),
        P(None, None, "mp"),
        P(None, "mp", None),
    )
    out_specs = (
        P(("dp", "mp"), None),
        P(("dp", "mp"), None),
        P(("dp", "mp"), None),
        P("dp", "mp"),
        P(("dp", "mp")),
        P("dp", None, "mp"),
        P("mp", "dp"),
        P("dp", "mp"),
        P("mp", "dp"),
        P(None, "dp", "mp"),
        P(None, "mp", "dp"),
    )
    return jax.shard_map(local, mesh=mesh, in_specs=in_specs, out_specs=out_specs, check_vma=False)
```

```python
import functools

import jax
import jax.numpy as jnp
from jax import lax
from jax.experimental import pallas as pl
from jax.experimental.pallas import tpu as pltpu
from jax.sharding import PartitionSpec as P

HEAD_DIM = 64
BF16 = jnp.bfloat16
F32 = jnp.float32
GELU_A = 0.7978845608028654
GELU_B = 0.044715


def nn(a, b):
    return lax.dot_general(a, b, (((1,), (0,)), ((), ())), preferred_element_type=F32)


def nt(a, b):
    return lax.dot_general(a, b, (((1,), (1,)), ((), ())), preferred_element_type=F32)


def tn(a, b):
    return lax.dot_general(a, b, (((0,), (0,)), ((), ())), preferred_element_type=F32)


def cost(flops, bytes_accessed, transcendentals):
    share = 16
    return pl.CostEstimate(
        flops=flops // share, bytes_accessed=bytes_accessed // share, transcendentals=transcendentals // share
    )


def swap(value, axis, mask):
    size = lax.axis_size(axis)
    return lax.ppermute(value, axis, [(i, i ^ mask) for i in range(size)])


def halves_evenly(n_dp, rows):
    return n_dp == 8 and rows % 16 == 0


def dp_steps(n_dp):
    return [("dp", 1 << bit) for bit in range(n_dp.bit_length() - 1)]


def block_order(steps):
    order = [(0, 0)]
    for axis, mask in reversed(steps):
        order = order + [(d ^ mask, m) if axis == "dp" else (d, m ^ mask) for d, m in order]
    return order


def flip(index, mask):
    bit = 1
    while bit <= mask:
        if mask & bit:
            index = index + bit * (1 - 2 * ((index // bit) % 2))
        bit *= 2
    return index


class Chain:
    def __init__(self, keep, send, steps, done=0):
        self.keep, self.send, self.steps, self.step = keep, send, steps, done
        self.shape = None if keep is None else keep.shape

    @classmethod
    def inside(cls, shape, steps):
        chain = cls(None, None, steps)
        chain.shape = shape
        return chain

    def take(self, results):
        if self.step == len(self.steps):
            self.result = results.pop(0)[0]
        else:
            self.keep, self.send = results.pop(0), results.pop(0)
            self.shape = self.keep.shape

    def advance(self):
        got = swap(self.send, *self.steps[self.step])
        total = self.keep.astype(F32) + got.astype(F32)
        half = total.shape[0] // 2
        self.step += 1
        self.take([total[:half].astype(BF16), total[half:].astype(BF16)] if half else [total])

    def finish(self):
        while self.step < len(self.steps):
            self.advance()
        return self.result


class Exchange:
    def __init__(self, jobs, sunk=False):
        self.jobs, self.sunk, self.sinks = jobs, sunk, {}
        self.operands, self.in_specs, self.out_specs, self.shapes, self.scratch = [], [], [], [], []
        self.plans = []
        for chain, count in jobs:
            blocks, tail = chain.shape[0], chain.shape[1:]
            steps = chain.steps[chain.step : chain.step + count]
            final = chain.step + count == len(chain.steps)
            self.plans.append((steps, final, blocks, chain.keep is None))
            if chain.keep is None:
                self.scratch.append(pltpu.VMEM(chain.shape, BF16))
            else:
                self.operands += [chain.keep, chain.send]
                self.in_specs += [pl.BlockSpec(memory_space=pl.ANY)] * 2
            left = blocks >> (count if not final else count - 1)
            kept = jax.ShapeDtypeStruct((left,) + tail, F32 if final else BF16)
            outs = [] if final and sunk else [kept] if final else [kept, kept]
            self.shapes += outs
            self.out_specs += [pl.BlockSpec(kept.shape, lambda *_: (0, 0, 0))] * len(outs)
            self.scratch.append(pltpu.VMEM((blocks,) + tail, BF16))
            self.scratch += [pltpu.VMEM((blocks >> n,) + tail, BF16) for n in range(count)]
            self.scratch += [
                pltpu.SemaphoreType.DMA((1,)),
                pltpu.SemaphoreType.DMA((count,)),
                pltpu.SemaphoreType.DMA((count,)),
            ]

    def bind(self, ins, outs, scratch):
        self.ins, self.outs, self.buffers, self.at = [], [], [], [0] * len(self.jobs)
        for steps, final, _, inner in self.plans:
            number = 0 if final and self.sunk else 1 if final else 2
            self.outs.append(outs[:number])
            outs = outs[number:]
            if inner:
                self.ins.append([None, scratch[0]])
                scratch = scratch[1:]
            else:
                self.ins.append(ins[:2])
                ins = ins[2:]
            number = len(steps) + 4
            self.buffers.append(scratch[:number])
            scratch = scratch[number:]

    @staticmethod
    def partner(axis, mask):
        return {axis: flip(lax.axis_index(axis), mask)}

    def load(self, n):
        return pltpu.make_async_copy(self.ins[n][0], self.buffers[n][0], self.buffers[n][-3].at[0])

    def copy(self, n, step):
        steps, _, blocks, _ = self.plans[n]
        work, send_sems, recv_sems = self.buffers[n][0], self.buffers[n][-2], self.buffers[n][-1]
        number = blocks >> step
        source = self.ins[n][1] if step == 0 else work.at[pl.ds(number, number)]
        return pltpu.make_async_remote_copy(
            src_ref=source,
            dst_ref=self.buffers[n][1 + step],
            send_sem=send_sems.at[step],
            recv_sem=recv_sems.at[step],
            device_id=self.partner(*steps[step]),
            device_id_type=pl.DeviceIdType.MESH,
        )

    def begin(self, others=()):
        partners = sorted({step for steps, *_ in self.plans for step in steps} | set(others))
        if partners:
            barrier = pltpu.get_barrier_semaphore()
            for step in partners:
                pl.semaphore_signal(
                    barrier, inc=1, device_id=self.partner(*step), device_id_type=pl.DeviceIdType.MESH
                )
            pl.semaphore_wait(barrier, len(partners))
        for n, (*_, inner) in enumerate(self.plans):
            if not inner:
                self.copy(n, 0).start()
                self.load(n).start()

    def halves(self, n):
        return self.buffers[n][0], self.ins[n][1]

    def start(self, n):
        self.copy(n, 0).start()

    def advance(self, n):
        steps, final, blocks, inner = self.plans[n]
        step = self.at[n]
        self.at[n] += 1
        work, got = self.buffers[n][0], self.buffers[n][1 + step]
        number = blocks >> step
        if step == 0 and not inner:
            self.load(n).wait()
        self.copy(n, step).wait()
        half = number // 2
        ending = step == len(steps) - 1

        def add(first, count, target, shift):
            def one(i, carry):
                total = work[i].astype(F32) + got[i].astype(F32)
                target[i - shift] = total.astype(target.dtype)
                return carry

            lax.fori_loop(first, first + count, one, 0)

        if ending and final and self.sunk:
            self.sinks[n](work[0].astype(F32) + got[0].astype(F32))
        elif ending and final:
            add(0, number, self.outs[n][0], 0)
        elif ending:
            add(0, half, self.outs[n][0], 0)
            add(half, half, self.outs[n][1], half)
        else:
            add(half, half, work, 0)
            self.copy(n, step + 1).start()
            add(0, half, work, 0)

    def left(self, n):
        return len(self.plans[n][0]) - self.at[n]

    def all_once(self):
        for n in range(len(self.jobs)):
            self.advance(n)

    def early(self, first=0, last=None):
        for n, (steps, *_) in list(enumerate(self.plans))[first:last]:
            while self.at[n] < len(steps) - 1:
                self.advance(n)

    def finish(self):
        for step in range(max([len(steps) for steps, *_ in self.plans], default=0)):
            for n, (steps, *_) in enumerate(self.plans):
                if self.at[n] == step and step < len(steps):
                    self.advance(n)

    def spread(self, results):
        results = list(results)
        for chain, count in self.jobs:
            chain.step += count
            if not (self.sunk and chain.step == len(chain.steps)):
                chain.take(results)


def remote(exchange, number, vmem, always=False):
    if not (exchange.jobs or always):
        return pltpu.CompilerParams(vmem_limit_bytes=vmem << 20)
    return pltpu.CompilerParams(vmem_limit_bytes=vmem << 20, collective_id=number, has_side_effects=True)


MP_STEPS = [("mp", 1), ("mp", 2)]
MP_ORDER = [m for _, m in block_order(MP_STEPS)]


def gather_mp(own):
    far = swap(own, "mp", 2)
    return [own, far, swap(own, "mp", 1), swap(far, "mp", 1)]


def normalize(values):
    center = values - jnp.mean(values, axis=-1, keepdims=True)
    inverse = lax.rsqrt(jnp.mean(center * center, axis=-1, keepdims=True) + 1e-06)
    return center * inverse, inverse


def normalize_back(normal, inverse, grad):
    return inverse * (
        grad
        - jnp.mean(grad, axis=-1, keepdims=True)
        - normal * jnp.mean(grad * normal, axis=-1, keepdims=True)
    )


def forward_kernel(
    heads, base, shift_one, scale_one, gate_one, shift_two, scale_two, seg_col, seg_row, *refs
):
    weights, out_weights = refs[:4], refs[4:8]
    normed_out, qkv, attended, lse_out, attn_out, second_out = refs[8], refs[9:13], *refs[13:]
    span = heads * HEAD_DIM
    x = base[...].astype(F32)
    normed = (normalize(x)[0] * (1.0 + scale_one[...]) + shift_one[...]).astype(BF16)
    normed_out[...] = normed
    same = seg_col[0] == seg_row[0]
    lane = lax.broadcasted_iota(jnp.int32, (1, 128), 1)
    lse_all = jnp.zeros(lse_out.shape, F32)
    attn = jnp.zeros(x.shape, F32)
    for block in range(4):
        qkv[block][...] = nt(normed, weights[block][...]).astype(BF16)
        for head in range(heads):
            at = head * HEAD_DIM
            q = qkv[block][:, at : at + HEAD_DIM]
            k = qkv[block][:, span + at : span + at + HEAD_DIM]
            v = qkv[block][:, 2 * span + at : 2 * span + at + HEAD_DIM]
            scores = jnp.where(same, nt(q, k) * (HEAD_DIM**-0.5), -1000000000.0)
            top = jnp.max(scores, axis=-1, keepdims=True)
            expo = jnp.exp(scores - top)
            total = jnp.sum(expo, axis=-1, keepdims=True)
            light = (expo * (1.0 / total)).astype(BF16)
            start = block * span + at
            attended[:, start : start + HEAD_DIM] = nn(light, v).astype(BF16)
            lse_all = jnp.where(lane == block * heads + head, top + jnp.log(total), lse_all)
        attn += nn(attended[:, block * span : (block + 1) * span], out_weights[block][...])
    lse_out[...] = lse_all
    attn_out[...] = attn
    middle = x + gate_one[...] * attn
    second_out[...] = (normalize(middle)[0] * (1.0 + scale_two[...]) + shift_two[...]).astype(BF16)


def rows_of(owner, rows):
    return pl.multiple_of(flip(lax.axis_index("dp"), owner) * rows, 8)


def store_blocks(order, m, total, halves, rows, columns=slice(None)):
    half = len(order) // 2
    for place, owner in enumerate(order):
        if owner[1] == m:
            start = 0 if rows == total.shape[0] else rows_of(owner[0], rows)
            halves[place // half][place % half, :rows, :] = total[pl.ds(start, rows), columns].astype(BF16)


def row_block(seq, columns):
    return pl.BlockSpec((seq, columns), lambda i, *_: (i, 0))


def column_block(seq, width, number):
    return pl.BlockSpec((seq, width), lambda i, *_: (i, number))


def whole_block(array):
    return pl.BlockSpec(array.shape, lambda i, *_: (0,) * array.ndim, pipeline_mode=pl.Buffered(1))


def segment_blocks(seq):
    return [
        pl.BlockSpec((1, seq, 1), lambda i, *_: (i, 0, 0)),
        pl.BlockSpec((1, 1, seq), lambda i, *_: (i, 0, 0)),
    ]


def run_forward(patches, modulation, segments, qkv_parts, out_parts):
    rows, seq = segments.shape
    tokens, width = patches.shape
    columns = qkv_parts[0].shape[0]
    heads = columns // (3 * HEAD_DIM)
    work = rows * 4 * heads * seq * seq
    shapes = (
        [(width, BF16)] + [(columns, BF16)] * 4 + [(width, BF16), (128, F32), (width, F32), (width, BF16)]
    )
    return pl.pallas_call(
        functools.partial(forward_kernel, heads),
        grid=(rows,),
        in_specs=[row_block(seq, width)]
        + [column_block(seq, width, n) for n in range(5)]
        + segment_blocks(seq)
        + [whole_block(w) for w in qkv_parts + out_parts],
        out_specs=[row_block(seq, c) for c, _ in shapes],
        out_shape=[jax.ShapeDtypeStruct((tokens, c), t) for c, t in shapes],
        compiler_params=pltpu.CompilerParams(vmem_limit_bytes=62 << 20),
        cost_estimate=cost(
            flops=4 * work * HEAD_DIM + 8 * tokens * width * width,
            bytes_accessed=40 * tokens * width,
            transcendentals=work,
        ),
        name="attention_half",
    )(
        patches,
        *([modulation] * 5),
        segments[:, :, None],
        segments[:, None, :],
        *qkv_parts,
        *out_parts,
    )


def attention_back_kernel(
    heads,
    exchange,
    order,
    rows,
    base,
    scale_one,
    gate_one,
    scale_two,
    attn,
    cotangent,
    summed,
    normed,
    attended,
    lse,
    seg_col,
    seg_row,
    *refs,
):
    qkv, weights, out_weights = refs[:4], refs[4:8], refs[8:12]
    number = len(exchange.operands)
    moved, refs = refs[12 : 12 + number], refs[12 + number :]
    patches_grad, pieces, halves, refs = refs[0], refs[1], refs[2:4], refs[4:]
    number = len(exchange.shapes)
    moved_out, refs = refs[:number], refs[number:]
    totals, grad_qkv, refs = refs[:4], refs[4], refs[5:]
    step, last = pl.program_id(0), pl.num_programs(0) - 1
    exchange.bind(moved, moved_out, refs)

    @pl.when(step == 0)
    def _():
        exchange.begin()

    span = heads * HEAD_DIM
    width = base.shape[1]
    factor = HEAD_DIM**-0.5
    same = seg_col[0] == seg_row[0]
    grad, branch, gate = summed[...], attn[...], gate_one[...]
    normal, inverse = normalize(base[...].astype(F32) + gate * branch)
    middle_grad = cotangent[...].astype(F32) + normalize_back(
        normal, inverse, grad * (1.0 + scale_two[...])
    )
    patches_grad[...] = middle_grad
    pieces[:, 2 * width : 3 * width] = (middle_grad * branch).astype(BF16)
    pieces[:, 3 * width : 4 * width] = grad.astype(BF16)
    pieces[:, 4 * width :] = (grad * normal).astype(BF16)
    upper = (middle_grad * gate).astype(BF16)
    normed_grad = jnp.zeros(base.shape, F32)
    for block in range(4):
        if block == 0:

            @pl.when(step == last)
            def _():
                exchange.early(0, 1)

        if block == 2:

            @pl.when(step == last)
            def _():
                exchange.early(1)

        grad_heads = nt(upper, out_weights[block][...]).astype(BF16)
        for head in range(heads):
            at = head * HEAD_DIM
            n = block * heads + head
            q = qkv[block][:, at : at + HEAD_DIM]
            k = qkv[block][:, span + at : span + at + HEAD_DIM]
            v = qkv[block][:, 2 * span + at : 2 * span + at + HEAD_DIM]
            g = grad_heads[:, at : at + HEAD_DIM]
            scores = jnp.where(same, nt(q, k) * factor, -1000000000.0)
            probs = jnp.exp(scores - lse[:, n : n + 1])
            grad_probs = nt(g, v)
            term = jnp.sum(probs * grad_probs, axis=-1, keepdims=True)
            grad_scores = (probs * (grad_probs - term)).astype(BF16)
            grad_qkv[:, at : at + HEAD_DIM] = (nn(grad_scores, k) * factor).astype(BF16)
            grad_qkv[:, span + at : span + at + HEAD_DIM] = (tn(grad_scores, q) * factor).astype(BF16)
            grad_qkv[:, 2 * span + at : 2 * span + at + HEAD_DIM] = tn(
                probs.astype(BF16), g
            ).astype(BF16)
        made = grad_qkv[...]
        normed_grad += nn(made, weights[block][...])
        of_qkv = tn(normed[...], made)
        of_out = tn(upper, attended[:, block * span : (block + 1) * span])

        @pl.when(step == 0)
        def _():
            totals[block][:, : 3 * span] = of_qkv
            totals[block][:, 3 * span :] = of_out

        @pl.when(step > 0)
        def _():
            totals[block][:, : 3 * span] += of_qkv
            totals[block][:, 3 * span :] += of_out

        @pl.when(step == last)
        def _():
            store_blocks(order, MP_ORDER[block], totals[block], halves, rows)

    normal, inverse = normalize(base[...].astype(F32))
    patches_grad[...] += normalize_back(normal, inverse, normed_grad * (1.0 + scale_one[...]))
    pieces[:, :width] = normed_grad.astype(BF16)
    pieces[:, width : 2 * width] = (normed_grad * normal).astype(BF16)

    @pl.when(step == last)
    def _():
        exchange.finish()


def run_attention_back(
    patches,
    modulation,
    attn,
    cotangent,
    summed,
    normed,
    attended,
    lse,
    segments,
    qkv,
    qkv_parts,
    out_parts,
    order,
    rows,
    jobs,
    number,
):
    count, seq = segments.shape
    tokens, width = patches.shape
    columns = qkv[0].shape[1]
    heads = columns // (3 * HEAD_DIM)
    work = count * 4 * heads * seq * seq
    wide = row_block(seq, width)
    half = (len(order) // 2, rows, 4 * columns // 3)
    exchange = Exchange(jobs)
    results = pl.pallas_call(
        functools.partial(attention_back_kernel, heads, exchange, order, rows),
        grid_spec=pltpu.PrefetchScalarGridSpec(
            num_scalar_prefetch=0,
            grid=(count,),
            in_specs=[wide]
            + [column_block(seq, width, n) for n in (1, 2, 4)]
            + [wide] * 5
            + [row_block(seq, 128)]
            + segment_blocks(seq)
            + [row_block(seq, columns)] * 4
            + [whole_block(w) for w in qkv_parts + out_parts]
            + exchange.in_specs,
            out_specs=[wide, row_block(seq, 5 * width)]
            + [pl.BlockSpec(half, lambda i, *_: (0, 0, 0))] * 2
            + exchange.out_specs,
            scratch_shapes=[pltpu.VMEM((width, 4 * columns // 3), F32)] * 4
            + [pltpu.VMEM((seq, columns), BF16)]
            + exchange.scratch,
        ),
        out_shape=[
            jax.ShapeDtypeStruct((tokens, width), F32),
            jax.ShapeDtypeStruct((tokens, 5 * width), BF16),
        ]
        + [jax.ShapeDtypeStruct(half, BF16)] * 2
        + exchange.shapes,
        compiler_params=remote(exchange, number, 62),
        cost_estimate=cost(
            flops=10 * work * HEAD_DIM + 16 * tokens * width * width,
            bytes_accessed=60 * tokens * width,
            transcendentals=work,
        ),
        name="attention_back",
    )(
        patches,
        *([modulation] * 3),
        attn,
        cotangent,
        summed,
        normed,
        attended,
        lse,
        segments[:, :, None],
        segments[:, None, :],
        *qkv,
        *qkv_parts,
        *out_parts,
        *exchange.operands,
    )
    exchange.spread(results[4:])
    return results[:4]


BIAS_ROWS = 16


def tail_kernel(
    orders,
    rows,
    exchange,
    cond,
    silu_cond,
    base,
    attn,
    gate_one,
    gate_two,
    cotangent,
    mlp,
    pieces,
    weight,
    *refs,
):
    number = len(exchange.operands)
    moved, refs = refs[:number], refs[number:]
    cond_grad, output, qkv_grad, out_grad, ada_grad, bias_grad, refs = *refs[:6], refs[6:]
    number = len(exchange.jobs) - 3
    late, refs = refs[:number], refs[number:]
    modulation_grad, weight_here, total, load_sems, refs = *refs[:4], refs[4:]
    exchange.bind(moved, (), refs)
    tokens, width = base.shape
    pieces_load = pltpu.make_async_copy(
        pieces, modulation_grad.at[:, pl.ds(0, pieces.shape[1])], load_sems.at[0]
    )
    weight_load = pltpu.make_async_copy(weight, weight_here, load_sems.at[1])
    pieces_load.start()
    weight_load.start()
    exchange.begin()
    grad_out, branch = cotangent[...].astype(F32), mlp[...]
    modulation_grad[:, 5 * width :] = (grad_out * branch).astype(BF16)
    middle = base[...].astype(F32) + gate_one[...] * attn[...]
    output[...] = (middle + gate_two[...] * branch).astype(BF16)
    pieces_load.wait()

    columns = modulation_grad.shape[1] // 4
    split = columns // 2
    heads = qkv_grad.shape[1]
    mp = lax.axis_index("mp")

    def keep_heads(value):
        qkv_grad[...] = value[:, :heads]
        out_grad[...] = value[:, heads:]

    def keep_low(value):
        ada_grad[:, :split] = value[:rows]
        bias_grad[...] = value[rows:]

    def keep_high(value):
        ada_grad[:, split:] = value

    def keep_late(target, value):
        target[...] = value

    exchange.sinks = {0: keep_low, 1: keep_high, 2: keep_heads}
    for n, target in enumerate(late):
        exchange.sinks[3 + n] = functools.partial(keep_late, target)
    bias = jnp.sum(modulation_grad[...].astype(F32), axis=0, keepdims=True).astype(BF16)
    lines = [bias[:, n * split : (n + 1) * split] for n in range(8)]
    lines = jnp.concatenate(lines + [jnp.zeros_like(lines[0])] * (BIAS_ROWS - 8), axis=0)
    for place in range(len(orders[0])):
        half = len(orders[0]) // 2
        exchange.halves(0)[place // half][place % half, rows:, :] = lines
    half = MP_ORDER[len(MP_ORDER) // 2 :]
    for m in half + [m for m in MP_ORDER if m not in half]:
        first = pl.multiple_of(flip(mp, m) * columns, 128)
        total[...] = tn(silu_cond[...], modulation_grad[:, pl.ds(first, columns)])
        for part, order in enumerate(orders):
            own = slice(part * split, (part + 1) * split)
            store_blocks(order, m, total, exchange.halves(part), rows, own)
        if m == half[0]:
            exchange.advance(2)
        if m == half[-1]:
            exchange.start(0)
            exchange.start(1)
            for n in range(len(late)):
                exchange.advance(3 + n)
    exchange.advance(0)
    exchange.advance(1)
    weight_load.wait()
    value = cond[...].astype(F32)
    gate = 1.0 / (1.0 + jnp.exp(-value))
    cond_grad[...] = nt(modulation_grad[...], weight_here[...]) * (gate * (1.0 + value * (1.0 - gate)))
    for n in [2] + [3 + n for n in range(len(late))] + [0, 1, 0, 2, 1, 2, 0, 1]:
        if n > 2 or exchange.left(n) > 1:
            exchange.advance(n)
    exchange.finish()


def run_tail(
    conditioning, silu_cond, patches, attn, modulation, cotangent, mlp, pieces, ada_weight, orders, rows, jobs, number
):
    tokens, width = silu_cond.shape
    exchange = Exchange(jobs, True)
    anywhere = pl.BlockSpec(memory_space=pl.ANY)
    columns = ada_weight.shape[1] // 4
    heads = jobs[2][0].shape[2]
    whole = lambda columns: pl.BlockSpec((tokens, columns), lambda i: (0, 0), pipeline_mode=pl.Buffered(1))
    gate = lambda n: pl.BlockSpec((tokens, width), lambda i: (0, n), pipeline_mode=pl.Buffered(1))
    shapes = [
        jax.ShapeDtypeStruct((tokens, width), F32),
        jax.ShapeDtypeStruct((tokens, width), BF16),
        jax.ShapeDtypeStruct((rows, heads * 3 // 4), F32),
        jax.ShapeDtypeStruct((rows, heads // 4), F32),
        jax.ShapeDtypeStruct((rows, columns), F32),
        jax.ShapeDtypeStruct((BIAS_ROWS, columns // 2), F32),
    ]
    shapes += [jax.ShapeDtypeStruct(chain.shape[1:], F32) for chain, _ in jobs[3:]]
    return pl.pallas_call(
        functools.partial(tail_kernel, orders, rows, exchange),
        grid=(1,),
        in_specs=[whole(width)] * 4
        + [gate(2), gate(5)]
        + [whole(width)] * 2
        + [anywhere] * 2
        + exchange.in_specs,
        out_specs=[constant_block(shape) for shape in shapes],
        out_shape=shapes,
        scratch_shapes=[
            pltpu.VMEM((tokens, ada_weight.shape[1]), BF16),
            pltpu.VMEM(ada_weight.shape, BF16),
            pltpu.VMEM((width, columns), F32),
            pltpu.SemaphoreType.DMA((2,)),
        ]
        + exchange.scratch,
        compiler_params=remote(exchange, number, 63),
        cost_estimate=cost(
            flops=16 * tokens * width * ada_weight.shape[1], bytes_accessed=100 * width * width, transcendentals=0
        ),
        name="tail",
    )(
        conditioning,
        silu_cond,
        patches,
        attn,
        modulation,
        modulation,
        cotangent,
        mlp,
        pieces,
        ada_weight,
        *exchange.operands,
    )


def finish_kernel(moves, rows, *refs):
    parts, refs = refs[: len(moves)], refs[len(moves) :]
    half = (len(refs) - 4) // 2
    plain, outs, experts = refs[:half], refs[half : 2 * half], refs[2 * half :]
    for source, target in zip(plain, outs):
        target[...] = source[...]
    for part, (expert, first, last) in zip(parts, moves):
        for kind in range(2):
            value = part[0, kind * rows : (kind + 1) * rows, :]
            if expert is None:
                experts[2 + kind][:, first:last] = value
            else:
                experts[kind][expert, :, first:last] = value


def run_finish(moves, plain, experts, rows, width):
    def block(array, index):
        return pl.BlockSpec((1,) + array.shape[1:], lambda i: (index, 0, 0), pipeline_mode=pl.Buffered(1))

    shapes = [jax.ShapeDtypeStruct(a.shape, a.dtype) for a in plain]
    shapes += [jax.ShapeDtypeStruct((experts, rows, width), F32)] * 2
    shapes += [jax.ShapeDtypeStruct((rows, width), F32)] * 2
    return pl.pallas_call(
        functools.partial(finish_kernel, [move[2:] for move in moves], rows),
        grid=(1,),
        in_specs=[block(array, index) for array, index, *_ in moves] + [whole_block(a) for a in plain],
        out_specs=[constant_block(shape) for shape in shapes],
        out_shape=shapes,
        compiler_params=pltpu.CompilerParams(vmem_limit_bytes=60 << 20),
        name="finish",
    )(*[move[0] for move in moves], *plain)


def gelu_and_slope(values):
    square = values * values
    bent = jnp.tanh(values * (GELU_A + (GELU_A * GELU_B) * square))
    half = 0.5 * (1.0 + bent)
    active = values * half
    return active, half + active * (1.0 - bent) * (GELU_A + (3.0 * GELU_A * GELU_B) * square)


class Gather:
    def __init__(self, own, far, held, send_sems, recv_sems):
        self.own, self.far, self.held, self.send_sems, self.recv_sems = own, far, held, send_sems, recv_sems

    def copy(self, place):
        far = self.held.at[1] if self.far is None else self.far
        return pltpu.make_async_remote_copy(
            src_ref=far if place == 2 else self.own,
            dst_ref=self.held.at[place],
            send_sem=self.send_sems.at[place],
            recv_sem=self.recv_sems.at[place],
            device_id=Exchange.partner("mp", 2 if place == 1 else 1),
            device_id_type=pl.DeviceIdType.MESH,
        )

    def begin(self):
        self.held[3] = self.own[...]
        if self.far is None:
            self.copy(1).start()
            self.copy(0).start()
        else:
            self.held[1] = self.far[...]
            self.copy(0).start()
            self.copy(2).start()

    def tile(self, step):
        @pl.when(step == 1)
        def _():
            self.copy(0).wait()

        if self.far is None:

            @pl.when(step == 2)
            def _():
                self.copy(1).wait()
                self.copy(2).start()

        @pl.when(step == 3)
        def _():
            self.copy(2).wait()

        return self.held[(step + 3) % 4]


def gather_barrier():
    barrier = pltpu.get_barrier_semaphore()
    for mask in (1, 2):
        pl.semaphore_signal(
            barrier, inc=1, device_id=Exchange.partner("mp", mask), device_id_type=pl.DeviceIdType.MESH
        )
    pl.semaphore_wait(barrier, 2)


def expert_kernel(columns, gathers, first, last, grad_later, exchange, units, rows, *refs):
    count = len(columns)
    gates, tokens, grads, refs = *refs[:3], refs[3:]
    if gathers:
        grads_far, refs = refs[0], refs[1:]
    ups, downs, refs = refs[:count], refs[count : 2 * count], refs[2 * count :]
    if not first:
        old_out, old_back, refs = refs[0], refs[1], refs[2:]
    number = len(exchange.operands)
    moved, refs = refs[:number], refs[number:]
    number = 2 * count if grad_later else sum(2 * len(own) for own in units)
    halves, refs = refs[:number], refs[number:]
    number = 4 if last else 2
    made, refs = refs[:number], refs[number:]
    number = len(exchange.shapes)
    moved_out, refs = refs[:number], refs[number:]
    if gathers:
        gathered, refs = refs[:2], refs[2:]
    number = 0 if grad_later else 2 * count
    sums, refs = refs[:number], refs[number:]
    step, final = pl.program_id(0), pl.num_programs(0) - 1
    if gathers:
        gather = [Gather(tokens, None, *refs[:3]), Gather(grads, grads_far, *refs[3:6])]
        refs = refs[6:]
    exchange.bind(moved, moved_out, refs)

    @pl.when(step == 0)
    def _():
        exchange.begin()

    @pl.when(step == 2)
    def _():
        exchange.early()

    if not grad_later:
        start_sums(step, sums)
    if gathers:

        @pl.when(step == 0)
        def _():
            gather_barrier()
            for one in gather:
                one.begin()

        x, own_grads = [one.tile(step) for one in gather]
        gathered[0][...] = x
        gathered[1][...] = own_grads
    else:
        x, own_grads = tokens[...], grads[...]
    g32 = own_grads.astype(F32)
    routed = None if first else old_out[...]
    returned = None if first else old_back[...]
    for n, column in enumerate(columns):
        gate = gates[:, column : column + 1]
        slot_grad = (gate * g32).astype(BF16)
        hidden, grad_pre, one, two = expert_pass(x, slot_grad, gate, ups[n][0], downs[n][0])
        routed = one if routed is None else routed + one
        returned = two if returned is None else returned + two
        if grad_later:
            halves[2 * n][...] = hidden
            halves[2 * n + 1][...] = grad_pre
        else:
            sums[2 * n][...] += tn(x, grad_pre)
            sums[2 * n + 1][...] += tn(slot_grad, hidden)
    if last:
        for value, (kept, sent) in ((routed, made[:2]), (returned, made[2:])):

            @pl.when(step < 2)
            def _():
                kept[0] = value.astype(BF16)

            @pl.when(step >= 2)
            def _():
                sent[0] = value.astype(BF16)

    else:
        made[0][...] = routed
        made[1][...] = returned
    if not grad_later:
        store_halves(step, units, sums, halves, rows)

    @pl.when(step == final)
    def _():
        exchange.finish()


def start_sums(step, sums):
    @pl.when(step == 0)
    def _():
        for total in sums:
            total[...] = jnp.zeros_like(total)


def store_units(units, sums, targets, rows):
    for (columns, order), halves in zip(units, targets):
        half = len(order) // 2
        for place, owner in enumerate(order):
            start = place * rows if half == 1 else rows_of(owner, rows)
            for part, total in enumerate(sums):
                halves[place // half][place % half, part * rows : (part + 1) * rows, :] = total[
                    pl.ds(start, rows), columns
                ].astype(BF16)


def store_halves(step, units, sums, halves, rows):
    @pl.when(step == pl.num_programs(0) - 1)
    def _():
        start = 0
        for n, own in enumerate(units):
            pairs = [halves[start + 2 * u : start + 2 * u + 2] for u in range(len(own))]
            start += 2 * len(own)
            store_units(own, sums[2 * n : 2 * n + 2], pairs, rows)


def unit_shapes(units, rows, width):
    shapes = []
    for columns, order in units:
        number = len(range(*columns.indices(width)))
        shapes += [jax.ShapeDtypeStruct((len(order) // 2, 2 * rows, number), BF16)] * 2
    return shapes


def constant_block(shape):
    return pl.BlockSpec(shape.shape, lambda *_: (0,) * len(shape.shape))


def expert_pass(x, slot_grad, gate, up, down):
    pre = nn(x, up)
    grad_hidden = nt(slot_grad, down)
    hidden, slope = gelu_and_slope(pre)
    hidden = hidden.astype(BF16)
    grad_pre = (grad_hidden * slope).astype(BF16)
    return hidden, grad_pre, gate * nn(hidden, down), nt(grad_pre, up)


TILE = 512


def token_tiles(columns):
    return pl.BlockSpec((TILE, columns), lambda t: (t, 0))


def run_experts(
    columns, weights, units, rows, gates, tokens, grads, sums, last, grad_later, jobs, number, gathers=False
):
    count = len(columns)
    total, width = gates.shape[0], tokens.shape[1]
    hidden = weights[0][0].shape[2]
    steps = total // TILE
    first = sums is None
    exchange = Exchange(jobs)

    def weight(index, shape):
        return pl.BlockSpec((1,) + shape, lambda t: (index, 0, 0), pipeline_mode=pl.Buffered(1))

    def tiles(columns):
        return pl.BlockSpec((TILE, columns), lambda t: ((t % 2) * 2 + t // 2 if gathers else t, 0))

    in_specs = (
        [tiles(gates.shape[1])]
        + ([pl.BlockSpec((TILE, width), lambda t: (0, 0))] * 3 if gathers else [tiles(width)] * 2)
        + [weight(i, (width, hidden)) for _, _, i in weights]
        + [weight(i, (hidden, width)) for _, _, i in weights]
        + ([] if first else [token_tiles(width), token_tiles(width)])
    )
    given = len(in_specs)
    if grad_later:
        shapes = [jax.ShapeDtypeStruct((total, hidden), BF16)] * (2 * count)
        specs = [token_tiles(hidden)] * (2 * count)
    else:
        shapes = [shape for own in units for shape in unit_shapes(own, rows, hidden)]
        specs = [constant_block(shape) for shape in shapes]
    made = len(shapes)
    if last:
        block = (1, TILE, width)
        sum_specs = [
            pl.BlockSpec(block, lambda t: (jnp.minimum(t, 1), 0, 0)),
            pl.BlockSpec(block, lambda t: (jnp.maximum(t - 2, 0), 0, 0)),
        ] * 2
        sum_shapes = [jax.ShapeDtypeStruct((2, TILE, width), BF16)] * 4
    else:
        sum_specs = [tiles(width)] * 2
        sum_shapes = [jax.ShapeDtypeStruct((total, width), F32)] * 2
    gather_scratch, gather_shapes = [], []
    if gathers:
        gather_scratch = ([pltpu.VMEM((4, TILE, width), BF16)] + [pltpu.SemaphoreType.DMA((3,))] * 2) * 2
        gather_shapes = [jax.ShapeDtypeStruct((total, width), BF16)] * 2
    aliases = {} if first or last else {given - 2: made, given - 1: made + 1}
    results = pl.pallas_call(
        functools.partial(expert_kernel, columns, gathers, first, last, grad_later, exchange, units, rows),
        grid_spec=pltpu.PrefetchScalarGridSpec(
            num_scalar_prefetch=0,
            grid=(steps,),
            in_specs=in_specs + exchange.in_specs,
            out_specs=specs + sum_specs + exchange.out_specs + [tiles(width)] * (2 * gathers),
            scratch_shapes=([] if grad_later else [pltpu.VMEM((width, hidden), F32)] * (2 * count))
            + gather_scratch
            + exchange.scratch,
        ),
        out_shape=shapes + sum_shapes + exchange.shapes + gather_shapes,
        input_output_aliases=aliases,
        compiler_params=remote(exchange, number, 60, gathers),
        cost_estimate=cost(
            flops=(8 if grad_later else 12) * count * total * width * hidden,
            bytes_accessed=20 * total * width + 8 * count * width * hidden,
            transcendentals=count * total * hidden,
        ),
        name=f"experts_{count}",
    )(
        gates,
        tokens,
        *(grads if gathers else [grads]),
        *[up for up, _, _ in weights],
        *[down for _, down, _ in weights],
        *(() if first else sums),
        *exchange.operands,
    )
    number = made + len(sum_shapes)
    if gathers:
        return results[:made], results[made:number], results[number:]
    exchange.spread(results[number:])
    return results[:made], results[made:number]


SLOTS = 3


def long_kernel(count, exchange, units, unit_steps, rows, gates, tokens, grads, up, down, *refs):
    old = refs[:2]
    number = len(exchange.operands)
    moved, refs = refs[2 : 2 + number], refs[2 + number :]
    new, finals, last_final, refs = refs[:2], refs[2], refs[3], refs[4:]
    number = 2 * len(units)
    half_done, raw, refs = refs[:number], refs[number : 2 * number], refs[2 * number :]
    number = len(exchange.shapes)
    moved_out, refs = refs[:number], refs[number:]
    sums, totals, send, work, gots = refs[:2], refs[2:4], refs[4], refs[5], refs[6:9]
    send_sems, recv_sems, load_sems, store_sems, refs = *refs[9:13], refs[13:]
    exchange.bind(moved, moved_out, refs)
    e, t = pl.program_id(0), pl.program_id(1)
    tiles = 4

    def copy(chain, step, unit):
        slot = chain % SLOTS
        blocks = 4 >> step
        columns = units[unit][0]
        place = pl.ds(columns.start, columns.stop - columns.start)
        source = send if step == 0 else work
        first = 0 if step == 0 else blocks
        return pltpu.make_async_remote_copy(
            src_ref=source.at[slot, pl.ds(first, blocks), :, place],
            dst_ref=gots[step].at[slot, :, :, place],
            send_sem=send_sems.at[slot, step, unit],
            recv_sem=recv_sems.at[slot, step, unit],
            device_id=exchange.partner(*unit_steps[unit][step]),
            device_id_type=pl.DeviceIdType.MESH,
        )

    def launch(chain, step):
        for unit in range(len(units)):
            copy(chain, step, unit).start()

    def arrive(chain, step):
        for unit in range(len(units)):
            copy(chain, step, unit).wait()

    def add(chain, step):
        slot = chain % SLOTS

        def one(i, carry):
            total = work[slot, i].astype(F32) + gots[step][slot, i].astype(F32)
            work[slot, i] = total.astype(BF16)
            return carry

        lax.fori_loop(0, 4 >> step, one, 0)

    def close(chain, target):
        arrive(chain, 2)
        slot = chain % SLOTS
        target[0] = work[slot, 0].astype(F32) + gots[2][slot, 0].astype(F32)

    def loads(n, tile):
        return pltpu.make_async_copy(
            old[n].at[pl.ds(tile * TILE, TILE), :], totals[n].at[tile], load_sems.at[n, tile]
        )

    def stores(n, tile):
        return pltpu.make_async_copy(
            totals[n].at[tile], new[n].at[pl.ds(tile * TILE, TILE), :], store_sems.at[n, tile]
        )

    @pl.when((e == 0) & (t == 0))
    def _():
        for tile in range(tiles):
            for n in range(2):
                loads(n, tile).start()
        exchange.begin(sorted({step for steps in unit_steps for step in steps}))

    for tile in range(tiles):

        @pl.when((e == 0) & (t == tile))
        def _():
            for n in range(2):
                loads(n, tile).wait()

    @pl.when((e == 1) & (t == 0))
    def _():
        exchange.all_once()

    @pl.when((e == 1) & (t == 2))
    def _():
        exchange.all_once()

    @pl.when((e == 2) & (t == 0))
    def _():
        exchange.finish()

    @pl.when((e >= 2) & (t == 0))
    def _():
        arrive(e - 2, 0)
        add(e - 2, 0)
        launch(e - 2, 1)

    @pl.when((e >= 1) & (t == 0))
    def _():
        launch(e - 1, 0)

    @pl.when((e >= 3) & (t == 2))
    def _():
        close(e - 3, finals)

    @pl.when((e >= 2) & (t == 2))
    def _():
        arrive(e - 2, 1)
        add(e - 2, 1)
        launch(e - 2, 2)

    @pl.when(t == 0)
    def _():
        for total in sums:
            total[...] = jnp.zeros_like(total)

    lane = lax.broadcasted_iota(jnp.int32, (1, gates.shape[1]), 1)
    gate = jnp.sum(jnp.where(lane == e, gates[...], 0.0), axis=1, keepdims=True)
    x = tokens[...]
    slot_grad = (gate * grads[...].astype(F32)).astype(BF16)
    hidden, grad_pre, one, two = expert_pass(x, slot_grad, gate, up[0], down[0])
    totals[0][t] += one
    totals[1][t] += two
    sums[0][...] += tn(x, grad_pre)
    sums[1][...] += tn(slot_grad, hidden)

    for tile in range(tiles):

        @pl.when((e == count - 1) & (t == tile))
        def _():
            for n in range(2):
                stores(n, tile).start()

    @pl.when((t == tiles - 1) & (e < count - 1))
    def _():
        slot = e % SLOTS
        pairs = [
            (work.at[slot, :, :, pl.ds(c.start, c.stop - c.start)], send.at[slot, :, :, pl.ds(c.start, c.stop - c.start)])
            for c, _ in units
        ]
        store_units(units, sums, pairs, rows)

    @pl.when((t == tiles - 1) & (e == count - 1))
    def _():
        store_units(units, sums, [raw[2 * u : 2 * u + 2] for u in range(len(units))], rows)
        close(count - 3, last_final)
        arrive(count - 2, 0)
        add(count - 2, 0)
        slot = (count - 2) % SLOTS
        for u, (c, _) in enumerate(units):
            half_done[2 * u][...] = work[slot, 0:2, :, c]
            half_done[2 * u + 1][...] = work[slot, 2:4, :, c]
        for tile in range(tiles):
            for n in range(2):
                stores(n, tile).wait()


def run_long(count, units, unit_steps, rows, gates, tokens, grads, expert_up, expert_down, sums, jobs, number):
    total, width = tokens.shape
    hidden = expert_up.shape[2]
    exchange = Exchange(jobs)
    steps = total // TILE
    tile = lambda columns: pl.BlockSpec((TILE, columns), lambda e, t: (t, 0))
    weight = lambda shape: pl.BlockSpec((1,) + shape, lambda e, t: (e, 0, 0))
    anywhere = pl.BlockSpec(memory_space=pl.ANY)
    raw = unit_shapes(units, rows, hidden)
    half_done = [jax.ShapeDtypeStruct((s.shape[0] // 2,) + s.shape[1:], BF16) for s in raw]
    final = (1, 2 * rows, hidden)
    results = pl.pallas_call(
        functools.partial(long_kernel, count, exchange, units, unit_steps, rows),
        grid=(count, steps),
        in_specs=[
            tile(gates.shape[1]),
            tile(width),
            tile(width),
            weight((width, hidden)),
            weight((hidden, width)),
            anywhere,
            anywhere,
        ]
        + exchange.in_specs,
        out_specs=[anywhere, anywhere]
        + [pl.BlockSpec(final, lambda e, t: (jnp.maximum(e - 3, 0), 0, 0)), pl.BlockSpec(final, lambda e, t: (0, 0, 0))]
        + [constant_block(shape) for shape in half_done + raw]
        + exchange.out_specs,
        out_shape=[jax.ShapeDtypeStruct((total, width), F32)] * 2
        + [jax.ShapeDtypeStruct((count - 3,) + final[1:], F32), jax.ShapeDtypeStruct(final, F32)]
        + half_done
        + raw
        + exchange.shapes,
        scratch_shapes=[pltpu.VMEM((width, hidden), F32)] * 2
        + [pltpu.VMEM((steps, TILE, width), F32)] * 2
        + [pltpu.VMEM((SLOTS, 4, 2 * rows, hidden), BF16)] * 2
        + [pltpu.VMEM((SLOTS, 4 >> n, 2 * rows, hidden), BF16) for n in range(3)]
        + [pltpu.SemaphoreType.DMA((SLOTS, 3, len(units)))] * 2
        + [pltpu.SemaphoreType.DMA((2, steps))] * 2
        + exchange.scratch,
        compiler_params=remote(exchange, number, 62),
        cost_estimate=cost(
            flops=12 * count * total * width * hidden,
            bytes_accessed=8 * count * total * width,
            transcendentals=count * total * hidden,
        ),
        name="experts_long",
    )(gates, tokens, grads, expert_up, expert_down, *sums, *exchange.operands)
    made = len(raw)
    exchange.spread(results[4 + 2 * made :])
    finished = [(results[2], n) for n in range(count - 3)] + [(results[3], 0)]
    return results[:2], finished, results[4 : 4 + made], results[4 + made : 4 + 2 * made]


def expert_grads_kernel(columns, exchange, units, rows, *refs):
    count = len(columns)
    gates, tokens, grads = refs[:3]
    saved, refs = refs[3 : 3 + 2 * count], refs[3 + 2 * count :]
    number = len(exchange.operands)
    moved, refs = refs[:number], refs[number:]
    number = sum(2 * len(own) for own in units)
    halves, refs = refs[:number], refs[number:]
    number = len(exchange.shapes)
    moved_out, refs = refs[:number], refs[number:]
    sums, refs = refs[: 2 * count], refs[2 * count :]
    step, final = pl.program_id(0), pl.num_programs(0) - 1
    exchange.bind(moved, moved_out, refs)

    @pl.when(step == 0)
    def _():
        exchange.begin()

    @pl.when(step == 1)
    def _():
        exchange.early(0, 1)

    @pl.when(step == 2)
    def _():
        exchange.early(1)

    start_sums(step, sums)
    x = tokens[...]
    g32 = grads[...].astype(F32)
    for n, column in enumerate(columns):
        slot_grad = (gates[:, column : column + 1] * g32).astype(BF16)
        sums[2 * n][...] += tn(x, saved[2 * n + 1][...])
        sums[2 * n + 1][...] += tn(slot_grad, saved[2 * n][...])
    store_halves(step, units, sums, halves, rows)

    @pl.when(step == final)
    def _():
        exchange.finish()


def run_expert_grads(columns, saved, units, rows, gates, tokens, grads, jobs, number):
    count = len(columns)
    total, width = tokens.shape
    hidden = saved[0].shape[1]
    steps = total // TILE
    shapes = [shape for own in units for shape in unit_shapes(own, rows, hidden)]
    exchange = Exchange(jobs)
    results = pl.pallas_call(
        functools.partial(expert_grads_kernel, columns, exchange, units, rows),
        grid_spec=pltpu.PrefetchScalarGridSpec(
            num_scalar_prefetch=0,
            grid=(steps,),
            in_specs=[token_tiles(gates.shape[1]), token_tiles(width), token_tiles(width)]
            + [token_tiles(hidden)] * (2 * count)
            + exchange.in_specs,
            out_specs=[constant_block(shape) for shape in shapes] + exchange.out_specs,
            scratch_shapes=[pltpu.VMEM((width, hidden), F32)] * (2 * count) + exchange.scratch,
        ),
        out_shape=shapes + exchange.shapes,
        compiler_params=remote(exchange, number, 60),
        cost_estimate=cost(
            flops=4 * count * total * width * hidden,
            bytes_accessed=(4 + 4 * count) * total * width,
            transcendentals=0,
        ),
        name="expert_grads",
    )(gates, tokens, grads, *saved, *exchange.operands)
    exchange.spread(results[len(shapes) :])
    return results[: len(shapes)]


def local(
    patches,
    conditioning,
    cotangent,
    segments,
    routes,
    gate_values,
    ada_weight,
    ada_bias,
    qkv_weight,
    out_weight,
    shared_up,
    shared_down,
    expert_up,
    expert_down,
):
    tokens, width = patches.shape
    group = routes.shape[0]
    experts = expert_up.shape[0]
    seq = segments.shape[1]
    n_dp, n_mp = lax.axis_size("dp"), lax.axis_size("mp")
    dp, mp = lax.axis_index("dp"), lax.axis_index("mp")
    rows = width // n_dp

    qkv_parts = gather_mp(jnp.transpose(qkv_weight, (1, 2, 0)).reshape(-1, width))
    out_parts = gather_mp(out_weight)

    silu_cond = jax.nn.silu(conditioning.astype(F32)).astype(BF16)
    modulation = jnp.dot(silu_cond, ada_weight, preferred_element_type=F32) + ada_bias[None, :]
    gate_two = modulation[:, 5 * width :]
    grad_mlp = (cotangent.astype(F32) * gate_two).astype(BF16)
    own_rows = tokens // seq
    own_segments = lax.dynamic_slice_in_dim(segments, mp * own_rows, own_rows, axis=0)
    number = jnp.arange(16, dtype=jnp.int32)[None, :]
    gates = jnp.sum(
        jnp.where(routes[:, :, None] == number[:, None, :], gate_values[:, :, None], 0.0), axis=1
    )
    gates = jnp.where(number == experts, 1.0, gates)
    gates = jnp.concatenate(
        [lax.dynamic_slice_in_dim(gates, (mp ^ m) * tokens, tokens, axis=0) for m in MP_ORDER],
        axis=0,
    )
    grad_mlp, qkv_parts[1], out_parts[1], gates, own_segments, silu_cond = lax.optimization_barrier(
        (grad_mlp, qkv_parts[1], out_parts[1], gates, own_segments, silu_cond)
    )
    grad_far = swap(grad_mlp, "mp", 2)

    results = run_forward(patches, modulation, own_segments, qkv_parts, out_parts)
    normed_one, qkv, attended, lse, attn_out, normed_two = results[0], results[1:5], *results[5:]

    shared = (shared_up[None], shared_down[None], 0)
    weights = {e: (expert_up, expert_down, e) for e in range(experts)}
    weights[experts] = shared
    even = halves_evenly(n_dp, rows)
    step = rows if even else width // 2
    reduced, chains, wholes = {}, {}, {}
    if even:
        near_step, far_step, *rest = dp_steps(n_dp)
        hidden = expert_up.shape[2]
        cut = hidden * 2 // 3
        unit_steps = [[near_step, far_step] + rest, [far_step, near_step] + rest]
        parts = [(slice(0, cut), unit_steps[0]), (slice(cut, hidden), unit_steps[1])]
        kinds = {c: parts for c in weights}
        kinds[experts - 2] = [(slice(0, hidden), unit_steps[1])]
        kinds[experts - 1] = [(slice(0, hidden), unit_steps[0])]
        units = {
            c: [(columns, [d for d, _ in block_order(steps)]) for columns, steps in kind]
            for c, kind in kinds.items()
        }
    else:
        units = {c: [(slice(0, expert_up.shape[2]), [0, 1])] for c in weights}

    def take_halves(columns, halves, done=0):
        halves = list(halves)
        for column in columns:
            own = [halves.pop(0) for _ in range(2 * len(units[column]))]
            if even:
                chains[column] = [
                    Chain(own[2 * u], own[2 * u + 1], steps, done)
                    for u, (_, steps) in enumerate(kinds[column])
                ]
            else:
                wholes[column] = own

    def jobs(**counts):
        if not even:
            return []
        return [(c, int(count[1:])) for count, columns in counts.items() for x in columns for c in chains[x]]

    def call(columns, sums, last, moves, number):
        return run_experts(
            columns,
            [weights[c] for c in columns],
            [units[c] for c in columns],
            step,
            gates,
            all_tokens,
            all_grads,
            sums,
            last,
            last,
            moves,
            number,
        )

    halves, sums, (all_tokens, all_grads) = run_experts(
        (experts,),
        [weights[experts]],
        [units[experts]],
        step,
        gates,
        normed_two,
        [grad_mlp, grad_far],
        None,
        False,
        False,
        [],
        0,
        True,
    )
    take_halves((experts,), halves)
    late = (experts - 2, experts - 1)
    if even:
        sums, finished, half_done, raw = run_long(
            experts - 2,
            units[0],
            unit_steps,
            rows,
            gates,
            all_tokens,
            all_grads,
            expert_up,
            expert_down,
            sums,
            jobs(n3=(experts,)),
            1,
        )
        take_halves((experts - 4,), half_done, 1)
        take_halves((experts - 3,), raw)
    else:
        for e in range(0, experts - 2, 2):
            halves, sums = call((e, e + 1), sums, False, [], 1 + e // 2)
            take_halves((e, e + 1), halves)
    saved, sums = call(late, sums, True, jobs(n2=(experts - 4,), n1=(experts - 3,)), 4)
    out_chain, back_chain = Chain(*sums[:2], MP_STEPS), Chain(*sums[2:], MP_STEPS)
    halves = run_expert_grads(
        late,
        saved,
        [units[c] for c in late],
        step,
        gates,
        all_tokens,
        all_grads,
        [(back_chain, 2)] + jobs(n2=(experts - 3,)),
        5,
    )
    take_halves(late, halves)
    tail_steps = [MP_STEPS] * 3
    if even:
        y, z, rest = dp_steps(n_dp)[0], dp_steps(n_dp)[1], dp_steps(n_dp)[2:]
        core, x = MP_STEPS
        tail_steps = [[core, x, y, z] + rest, [core, y, x, z] + rest, [core, z, x, y] + rest]
    tail_orders = [block_order(steps) for steps in tail_steps]

    tail_rows = rows if even else width
    results = run_attention_back(
        patches,
        modulation,
        attn_out,
        cotangent,
        back_chain.result,
        normed_one,
        attended,
        lse,
        own_segments,
        qkv,
        qkv_parts,
        out_parts,
        tail_orders[0],
        tail_rows,
        [(out_chain, 2)] + jobs(n1=late),
        6,
    )
    patches_grad, pieces, heads_halves = results[0], results[1], results[2:4]
    heads_chain = Chain(*heads_halves, tail_steps[0])
    split = ada_weight.shape[1] // n_mp // 2
    half = len(tail_orders[1]) // 2
    ada_chains = [
        Chain.inside((half, tail_rows + BIAS_ROWS, split), tail_steps[1]),
        Chain.inside((half, tail_rows, split), tail_steps[2]),
    ]
    number = len(tail_steps[0])
    results = run_tail(
        conditioning,
        silu_cond,
        patches,
        attn_out,
        modulation,
        cotangent,
        out_chain.result,
        pieces,
        ada_weight,
        tail_orders[1:],
        tail_rows,
        [(c, number) for c in ada_chains] + [(heads_chain, number)] + jobs(n2=late),
        7,
    )
    conditioning_grad, output, qkv_sum, out_total, ada_sum, bias_all = results[:6]
    bias_all = bias_all[: 2 * n_mp].reshape(-1)
    if even:
        moves = [(array, index, e, 0, hidden) for e, (array, index) in enumerate(finished)]
        moves += [(array[None], 0, column, 0, hidden) for column, array in zip(late, results[6:])]
        for column, own in chains.items():
            if column not in late:
                for chain, (columns, _) in zip(own, kinds[column]):
                    place = None if column == experts else column
                    moves.append((chain.result[None], 0, place, columns.start, columns.stop))
        results = run_finish(
            moves, [output, patches_grad, conditioning_grad, ada_sum], experts, rows, hidden
        )
        output, patches_grad, conditioning_grad, ada_sum = results[:4]
        expert_up_sum, expert_down_sum, up_sum, down_sum = results[4:]
    else:
        for column, (first, second) in wholes.items():
            whole = jnp.stack([first[0], second[0]]).reshape(2, 2, step, -1)
            whole = jnp.swapaxes(whole, 0, 1).reshape(2, width, -1)
            part = lax.psum_scatter(whole, "dp", scatter_dimension=1, tiled=True).astype(F32)
            reduced[column] = part[0], part[1]
        up_sum, down_sum = reduced[experts]
        expert_up_sum, expert_down_sum = [
            jnp.stack([reduced[e][part] for e in range(experts)]) for part in range(2)
        ]
        qkv_sum, out_total, ada_sum = [
            lax.psum_scatter(a.astype(BF16), "dp", scatter_dimension=0, tiled=True).astype(F32)
            for a in (qkv_sum, out_total, ada_sum)
        ]
        bias_all = lax.psum(bias_all, "dp")
    share = bias_all.shape[0] // (n_dp * n_mp)
    return (
        output,
        patches_grad,
        conditioning_grad,
        ada_sum,
        lax.dynamic_slice_in_dim(bias_all, (dp * n_mp + mp) * share, share),
        qkv_sum.reshape(rows, 3, -1),
        out_total.T,
        up_sum,
        down_sum.T,
        expert_up_sum,
        jnp.swapaxes(expert_down_sum, 1, 2),
    )


def solution(mesh):
    in_specs = (
        P(("dp", "mp"), None),
        P(("dp", "mp"), None),
        P(("dp", "mp"), None),
        P("dp", None),
        P("dp", None),
        P("dp", None),
        P(),
        P(),
        P(None, None, "mp"),
        P("mp", None),
        P(None, "mp"),
        P("mp", None),
        P(None, None, "mp"),
        P(None, "mp", None),
    )
    out_specs = (
        P(("dp", "mp"), None),
        P(("dp", "mp"), None),
        P(("dp", "mp"), None),
        P("dp", "mp"),
        P(("dp", "mp")),
        P("dp", None, "mp"),
        P("mp", "dp"),
        P("dp", "mp"),
        P("mp", "dp"),
        P(None, "dp", "mp"),
        P(None, "mp", "dp"),
    )
    return jax.shard_map(local, mesh=mesh, in_specs=in_specs, out_specs=out_specs, check_vma=False)
```

```python
import functools

import jax
import jax.numpy as jnp
from jax import lax
from jax.experimental import pallas as pl
from jax.experimental.pallas import tpu as pltpu
from jax.sharding import PartitionSpec as P

HEAD_DIM = 64
BF16 = jnp.bfloat16
F32 = jnp.float32
GELU_A = 0.7978845608028654
GELU_B = 0.044715


def nn(a, b):
    return lax.dot_general(a, b, (((1,), (0,)), ((), ())), preferred_element_type=F32)


def nt(a, b):
    return lax.dot_general(a, b, (((1,), (1,)), ((), ())), preferred_element_type=F32)


def tn(a, b):
    return lax.dot_general(a, b, (((0,), (0,)), ((), ())), preferred_element_type=F32)


def cost(flops, bytes_accessed, transcendentals):
    share = 16
    return pl.CostEstimate(
        flops=flops // share, bytes_accessed=bytes_accessed // share, transcendentals=transcendentals // share
    )


def swap(value, axis, mask):
    size = lax.axis_size(axis)
    return lax.ppermute(value, axis, [(i, i ^ mask) for i in range(size)])


def halves_evenly(n_dp, rows):
    return n_dp == 8 and rows % 16 == 0


def dp_steps(n_dp):
    return [("dp", 1 << bit) for bit in range(n_dp.bit_length() - 1)]


def block_order(steps):
    order = [(0, 0)]
    for axis, mask in reversed(steps):
        order = order + [(d ^ mask, m) if axis == "dp" else (d, m ^ mask) for d, m in order]
    return order


def flip(index, mask):
    bit = 1
    while bit <= mask:
        if mask & bit:
            index = index + bit * (1 - 2 * ((index // bit) % 2))
        bit *= 2
    return index


class Chain:
    def __init__(self, keep, send, steps, done=0):
        self.keep, self.send, self.steps, self.step = keep, send, steps, done
        self.shape = None if keep is None else keep.shape

    @classmethod
    def inside(cls, shape, steps):
        chain = cls(None, None, steps)
        chain.shape = shape
        return chain

    def take(self, results):
        if self.step == len(self.steps):
            self.result = results.pop(0)[0]
        else:
            self.keep, self.send = results.pop(0), results.pop(0)
            self.shape = self.keep.shape

    def advance(self):
        got = swap(self.send, *self.steps[self.step])
        total = self.keep.astype(F32) + got.astype(F32)
        half = total.shape[0] // 2
        self.step += 1
        self.take([total[:half].astype(BF16), total[half:].astype(BF16)] if half else [total])

    def finish(self):
        while self.step < len(self.steps):
            self.advance()
        return self.result


class Exchange:
    def __init__(self, jobs, sunk=False):
        self.jobs, self.sunk, self.sinks = jobs, sunk, {}
        self.operands, self.in_specs, self.out_specs, self.shapes, self.scratch = [], [], [], [], []
        self.plans = []
        for chain, count in jobs:
            blocks, tail = chain.shape[0], chain.shape[1:]
            steps = chain.steps[chain.step : chain.step + count]
            final = chain.step + count == len(chain.steps)
            self.plans.append((steps, final, blocks, chain.keep is None))
            if chain.keep is None:
                self.scratch.append(pltpu.VMEM(chain.shape, BF16))
            else:
                self.operands += [chain.keep, chain.send]
                self.in_specs += [pl.BlockSpec(memory_space=pl.ANY)] * 2
            left = blocks >> (count if not final else count - 1)
            kept = jax.ShapeDtypeStruct((left,) + tail, F32 if final else BF16)
            outs = [] if final and sunk else [kept] if final else [kept, kept]
            self.shapes += outs
            self.out_specs += [pl.BlockSpec(kept.shape, lambda *_: (0, 0, 0))] * len(outs)
            self.scratch.append(pltpu.VMEM((blocks,) + tail, BF16))
            self.scratch += [pltpu.VMEM((blocks >> n,) + tail, BF16) for n in range(count)]
            self.scratch += [
                pltpu.SemaphoreType.DMA((1,)),
                pltpu.SemaphoreType.DMA((count,)),
                pltpu.SemaphoreType.DMA((count,)),
            ]

    def bind(self, ins, outs, scratch):
        self.ins, self.outs, self.buffers, self.at = [], [], [], [0] * len(self.jobs)
        for steps, final, _, inner in self.plans:
            number = 0 if final and self.sunk else 1 if final else 2
            self.outs.append(outs[:number])
            outs = outs[number:]
            if inner:
                self.ins.append([None, scratch[0]])
                scratch = scratch[1:]
            else:
                self.ins.append(ins[:2])
                ins = ins[2:]
            number = len(steps) + 4
            self.buffers.append(scratch[:number])
            scratch = scratch[number:]

    @staticmethod
    def partner(axis, mask):
        return {axis: flip(lax.axis_index(axis), mask)}

    def load(self, n):
        return pltpu.make_async_copy(self.ins[n][0], self.buffers[n][0], self.buffers[n][-3].at[0])

    def copy(self, n, step):
        steps, _, blocks, _ = self.plans[n]
        work, send_sems, recv_sems = self.buffers[n][0], self.buffers[n][-2], self.buffers[n][-1]
        number = blocks >> step
        source = self.ins[n][1] if step == 0 else work.at[pl.ds(number, number)]
        return pltpu.make_async_remote_copy(
            src_ref=source,
            dst_ref=self.buffers[n][1 + step],
            send_sem=send_sems.at[step],
            recv_sem=recv_sems.at[step],
            device_id=self.partner(*steps[step]),
            device_id_type=pl.DeviceIdType.MESH,
        )

    def begin(self, others=()):
        partners = sorted({step for steps, *_ in self.plans for step in steps} | set(others))
        if partners:
            barrier = pltpu.get_barrier_semaphore()
            for step in partners:
                pl.semaphore_signal(
                    barrier, inc=1, device_id=self.partner(*step), device_id_type=pl.DeviceIdType.MESH
                )
            pl.semaphore_wait(barrier, len(partners))
        for n, (*_, inner) in enumerate(self.plans):
            if not inner:
                self.copy(n, 0).start()
                self.load(n).start()

    def halves(self, n):
        return self.buffers[n][0], self.ins[n][1]

    def start(self, n):
        self.copy(n, 0).start()

    def advance(self, n):
        steps, final, blocks, inner = self.plans[n]
        step = self.at[n]
        self.at[n] += 1
        work, got = self.buffers[n][0], self.buffers[n][1 + step]
        number = blocks >> step
        if step == 0 and not inner:
            self.load(n).wait()
        self.copy(n, step).wait()
        half = number // 2
        ending = step == len(steps) - 1

        def add(first, count, target, shift):
            def one(i, carry):
                total = work[i].astype(F32) + got[i].astype(F32)
                target[i - shift] = total.astype(target.dtype)
                return carry

            lax.fori_loop(first, first + count, one, 0)

        if ending and final and self.sunk:
            self.sinks[n](work[0].astype(F32) + got[0].astype(F32))
        elif ending and final:
            add(0, number, self.outs[n][0], 0)
        elif ending:
            add(0, half, self.outs[n][0], 0)
            add(half, half, self.outs[n][1], half)
        else:
            add(half, half, work, 0)
            self.copy(n, step + 1).start()
            add(0, half, work, 0)

    def left(self, n):
        return len(self.plans[n][0]) - self.at[n]

    def all_once(self):
        for n in range(len(self.jobs)):
            self.advance(n)

    def early(self, first=0, last=None):
        for n, (steps, *_) in list(enumerate(self.plans))[first:last]:
            while self.at[n] < len(steps) - 1:
                self.advance(n)

    def finish(self):
        for step in range(max([len(steps) for steps, *_ in self.plans], default=0)):
            for n, (steps, *_) in enumerate(self.plans):
                if self.at[n] == step and step < len(steps):
                    self.advance(n)

    def spread(self, results):
        results = list(results)
        for chain, count in self.jobs:
            chain.step += count
            if not (self.sunk and chain.step == len(chain.steps)):
                chain.take(results)


def remote(exchange, number, vmem, always=False):
    if not (exchange.jobs or always):
        return pltpu.CompilerParams(vmem_limit_bytes=vmem << 20)
    return pltpu.CompilerParams(vmem_limit_bytes=vmem << 20, collective_id=number, has_side_effects=True)


MP_STEPS = [("mp", 1), ("mp", 2)]
MP_ORDER = [m for _, m in block_order(MP_STEPS)]


def gather_mp(own):
    far = swap(own, "mp", 2)
    return [own, far, swap(own, "mp", 1), swap(far, "mp", 1)]


def normalize(values):
    center = values - jnp.mean(values, axis=-1, keepdims=True)
    inverse = lax.rsqrt(jnp.mean(center * center, axis=-1, keepdims=True) + 1e-06)
    return center * inverse, inverse


def normalize_back(normal, inverse, grad):
    return inverse * (
        grad
        - jnp.mean(grad, axis=-1, keepdims=True)
        - normal * jnp.mean(grad * normal, axis=-1, keepdims=True)
    )


def forward_kernel(
    heads, base, shift_one, scale_one, gate_one, shift_two, scale_two, seg_col, seg_row, *refs
):
    weights, out_weights = refs[:4], refs[4:8]
    normed_out, qkv, attended, lse_out, attn_out, second_out = refs[8], refs[9:13], *refs[13:]
    span = heads * HEAD_DIM
    x = base[...].astype(F32)
    normed = (normalize(x)[0] * (1.0 + scale_one[...]) + shift_one[...]).astype(BF16)
    normed_out[...] = normed
    same = seg_col[0] == seg_row[0]
    lane = lax.broadcasted_iota(jnp.int32, (1, 128), 1)
    lse_all = jnp.zeros(lse_out.shape, F32)
    attn = jnp.zeros(x.shape, F32)
    for block in range(4):
        qkv[block][...] = nt(normed, weights[block][...]).astype(BF16)
        for head in range(heads):
            at = head * HEAD_DIM
            q = qkv[block][:, at : at + HEAD_DIM]
            k = qkv[block][:, span + at : span + at + HEAD_DIM]
            v = qkv[block][:, 2 * span + at : 2 * span + at + HEAD_DIM]
            scores = jnp.where(same, nt(q, k) * (HEAD_DIM**-0.5), -1000000000.0)
            top = jnp.max(scores, axis=-1, keepdims=True)
            expo = jnp.exp(scores - top)
            total = jnp.sum(expo, axis=-1, keepdims=True)
            light = (expo * (1.0 / total)).astype(BF16)
            start = block * span + at
            attended[:, start : start + HEAD_DIM] = nn(light, v).astype(BF16)
            lse_all = jnp.where(lane == block * heads + head, top + jnp.log(total), lse_all)
        attn += nn(attended[:, block * span : (block + 1) * span], out_weights[block][...])
    lse_out[...] = lse_all
    attn_out[...] = attn
    middle = x + gate_one[...] * attn
    second_out[...] = (normalize(middle)[0] * (1.0 + scale_two[...]) + shift_two[...]).astype(BF16)


def rows_of(owner, rows):
    return pl.multiple_of(flip(lax.axis_index("dp"), owner) * rows, 8)


def store_blocks(order, m, total, halves, rows, columns=slice(None)):
    half = len(order) // 2
    for place, owner in enumerate(order):
        if owner[1] == m:
            start = 0 if rows == total.shape[0] else rows_of(owner[0], rows)
            halves[place // half][place % half, :rows, :] = total[pl.ds(start, rows), columns].astype(BF16)


def row_block(seq, columns):
    return pl.BlockSpec((seq, columns), lambda i, *_: (i, 0))


def column_block(seq, width, number):
    return pl.BlockSpec((seq, width), lambda i, *_: (i, number))


def whole_block(array):
    return pl.BlockSpec(array.shape, lambda i, *_: (0,) * array.ndim, pipeline_mode=pl.Buffered(1))


def segment_blocks(seq):
    return [
        pl.BlockSpec((1, seq, 1), lambda i, *_: (i, 0, 0)),
        pl.BlockSpec((1, 1, seq), lambda i, *_: (i, 0, 0)),
    ]


def run_forward(patches, modulation, segments, qkv_parts, out_parts):
    rows, seq = segments.shape
    tokens, width = patches.shape
    columns = qkv_parts[0].shape[0]
    heads = columns // (3 * HEAD_DIM)
    work = rows * 4 * heads * seq * seq
    shapes = (
        [(width, BF16)] + [(columns, BF16)] * 4 + [(width, BF16), (128, F32), (width, F32), (width, BF16)]
    )
    return pl.pallas_call(
        functools.partial(forward_kernel, heads),
        grid=(rows,),
        in_specs=[row_block(seq, width)]
        + [column_block(seq, width, n) for n in range(5)]
        + segment_blocks(seq)
        + [whole_block(w) for w in qkv_parts + out_parts],
        out_specs=[row_block(seq, c) for c, _ in shapes],
        out_shape=[jax.ShapeDtypeStruct((tokens, c), t) for c, t in shapes],
        compiler_params=pltpu.CompilerParams(vmem_limit_bytes=62 << 20),
        cost_estimate=cost(
            flops=4 * work * HEAD_DIM + 8 * tokens * width * width,
            bytes_accessed=40 * tokens * width,
            transcendentals=work,
        ),
        name="attention_half",
    )(
        patches,
        *([modulation] * 5),
        segments[:, :, None],
        segments[:, None, :],
        *qkv_parts,
        *out_parts,
    )


def attention_back_kernel(
    heads,
    exchange,
    order,
    rows,
    base,
    scale_one,
    gate_one,
    scale_two,
    attn,
    cotangent,
    summed,
    normed,
    attended,
    lse,
    seg_col,
    seg_row,
    *refs,
):
    qkv, weights, out_weights = refs[:4], refs[4:8], refs[8:12]
    number = len(exchange.operands)
    moved, refs = refs[12 : 12 + number], refs[12 + number :]
    patches_grad, pieces, halves, refs = refs[0], refs[1], refs[2:4], refs[4:]
    number = len(exchange.shapes)
    moved_out, refs = refs[:number], refs[number:]
    totals, grad_qkv, refs = refs[:4], refs[4], refs[5:]
    step, last = pl.program_id(0), pl.num_programs(0) - 1
    exchange.bind(moved, moved_out, refs)

    @pl.when(step == 0)
    def _():
        exchange.begin()

    span = heads * HEAD_DIM
    width = base.shape[1]
    factor = HEAD_DIM**-0.5
    same = seg_col[0] == seg_row[0]
    grad, branch, gate = summed[...], attn[...], gate_one[...]
    normal, inverse = normalize(base[...].astype(F32) + gate * branch)
    middle_grad = cotangent[...].astype(F32) + normalize_back(
        normal, inverse, grad * (1.0 + scale_two[...])
    )
    patches_grad[...] = middle_grad
    pieces[:, 2 * width : 3 * width] = (middle_grad * branch).astype(BF16)
    pieces[:, 3 * width : 4 * width] = grad.astype(BF16)
    pieces[:, 4 * width :] = (grad * normal).astype(BF16)
    upper = (middle_grad * gate).astype(BF16)
    normed_grad = jnp.zeros(base.shape, F32)
    for block in range(4):
        if block == 0:

            @pl.when(step == last)
            def _():
                exchange.early(0, 1)

        if block == 2:

            @pl.when(step == last)
            def _():
                exchange.early(1)

        grad_heads = nt(upper, out_weights[block][...]).astype(BF16)
        for head in range(heads):
            at = head * HEAD_DIM
            n = block * heads + head
            q = qkv[block][:, at : at + HEAD_DIM]
            k = qkv[block][:, span + at : span + at + HEAD_DIM]
            v = qkv[block][:, 2 * span + at : 2 * span + at + HEAD_DIM]
            g = grad_heads[:, at : at + HEAD_DIM]
            scores = jnp.where(same, nt(q, k) * factor, -1000000000.0)
            probs = jnp.exp(scores - lse[:, n : n + 1])
            grad_probs = nt(g, v)
            term = jnp.sum(probs * grad_probs, axis=-1, keepdims=True)
            grad_scores = (probs * (grad_probs - term)).astype(BF16)
            grad_qkv[:, at : at + HEAD_DIM] = (nn(grad_scores, k) * factor).astype(BF16)
            grad_qkv[:, span + at : span + at + HEAD_DIM] = (tn(grad_scores, q) * factor).astype(BF16)
            grad_qkv[:, 2 * span + at : 2 * span + at + HEAD_DIM] = tn(
                probs.astype(BF16), g
            ).astype(BF16)
        made = grad_qkv[...]
        normed_grad += nn(made, weights[block][...])
        of_qkv = tn(normed[...], made)
        of_out = tn(upper, attended[:, block * span : (block + 1) * span])

        @pl.when(step == 0)
        def _():
            totals[block][:, : 3 * span] = of_qkv
            totals[block][:, 3 * span :] = of_out

        @pl.when(step > 0)
        def _():
            totals[block][:, : 3 * span] += of_qkv
            totals[block][:, 3 * span :] += of_out

        @pl.when(step == last)
        def _():
            store_blocks(order, MP_ORDER[block], totals[block], halves, rows)

    normal, inverse = normalize(base[...].astype(F32))
    patches_grad[...] += normalize_back(normal, inverse, normed_grad * (1.0 + scale_one[...]))
    pieces[:, :width] = normed_grad.astype(BF16)
    pieces[:, width : 2 * width] = (normed_grad * normal).astype(BF16)

    @pl.when(step == last)
    def _():
        exchange.finish()


def run_attention_back(
    patches,
    modulation,
    attn,
    cotangent,
    summed,
    normed,
    attended,
    lse,
    segments,
    qkv,
    qkv_parts,
    out_parts,
    order,
    rows,
    jobs,
    number,
):
    count, seq = segments.shape
    tokens, width = patches.shape
    columns = qkv[0].shape[1]
    heads = columns // (3 * HEAD_DIM)
    work = count * 4 * heads * seq * seq
    wide = row_block(seq, width)
    half = (len(order) // 2, rows, 4 * columns // 3)
    exchange = Exchange(jobs)
    results = pl.pallas_call(
        functools.partial(attention_back_kernel, heads, exchange, order, rows),
        grid_spec=pltpu.PrefetchScalarGridSpec(
            num_scalar_prefetch=0,
            grid=(count,),
            in_specs=[wide]
            + [column_block(seq, width, n) for n in (1, 2, 4)]
            + [wide] * 5
            + [row_block(seq, 128)]
            + segment_blocks(seq)
            + [row_block(seq, columns)] * 4
            + [whole_block(w) for w in qkv_parts + out_parts]
            + exchange.in_specs,
            out_specs=[wide, row_block(seq, 5 * width)]
            + [pl.BlockSpec(half, lambda i, *_: (0, 0, 0))] * 2
            + exchange.out_specs,
            scratch_shapes=[pltpu.VMEM((width, 4 * columns // 3), F32)] * 4
            + [pltpu.VMEM((seq, columns), BF16)]
            + exchange.scratch,
        ),
        out_shape=[
            jax.ShapeDtypeStruct((tokens, width), F32),
            jax.ShapeDtypeStruct((tokens, 5 * width), BF16),
        ]
        + [jax.ShapeDtypeStruct(half, BF16)] * 2
        + exchange.shapes,
        compiler_params=remote(exchange, number, 62),
        cost_estimate=cost(
            flops=10 * work * HEAD_DIM + 16 * tokens * width * width,
            bytes_accessed=60 * tokens * width,
            transcendentals=work,
        ),
        name="attention_back",
    )(
        patches,
        *([modulation] * 3),
        attn,
        cotangent,
        summed,
        normed,
        attended,
        lse,
        segments[:, :, None],
        segments[:, None, :],
        *qkv,
        *qkv_parts,
        *out_parts,
        *exchange.operands,
    )
    exchange.spread(results[4:])
    return results[:4]


BIAS_ROWS = 16


def tail_kernel(
    orders,
    rows,
    exchange,
    cond,
    silu_cond,
    base,
    attn,
    gate_one,
    gate_two,
    cotangent,
    mlp,
    pieces,
    weight,
    *refs,
):
    number = len(exchange.operands)
    moved, refs = refs[:number], refs[number:]
    cond_grad, output, qkv_grad, out_grad, ada_grad, bias_grad, refs = *refs[:6], refs[6:]
    number = len(exchange.jobs) - 3
    late, refs = refs[:number], refs[number:]
    modulation_grad, weight_here, total, load_sems, refs = *refs[:4], refs[4:]
    exchange.bind(moved, (), refs)
    tokens, width = base.shape
    pieces_load = pltpu.make_async_copy(
        pieces, modulation_grad.at[:, pl.ds(0, pieces.shape[1])], load_sems.at[0]
    )
    weight_load = pltpu.make_async_copy(weight, weight_here, load_sems.at[1])
    pieces_load.start()
    weight_load.start()
    exchange.begin()
    grad_out, branch = cotangent[...].astype(F32), mlp[...]
    modulation_grad[:, 5 * width :] = (grad_out * branch).astype(BF16)
    middle = base[...].astype(F32) + gate_one[...] * attn[...]
    output[...] = (middle + gate_two[...] * branch).astype(BF16)
    pieces_load.wait()

    columns = modulation_grad.shape[1] // 4
    split = columns // 2
    heads = qkv_grad.shape[1]
    mp = lax.axis_index("mp")

    def keep_heads(value):
        qkv_grad[...] = value[:, :heads]
        out_grad[...] = value[:, heads:]

    def keep_low(value):
        ada_grad[:, :split] = value[:rows]
        bias_grad[...] = value[rows:]

    def keep_high(value):
        ada_grad[:, split:] = value

    def keep_late(target, value):
        target[...] = value

    exchange.sinks = {0: keep_low, 1: keep_high, 2: keep_heads}
    for n, target in enumerate(late):
        exchange.sinks[3 + n] = functools.partial(keep_late, target)
    bias = jnp.sum(modulation_grad[...].astype(F32), axis=0, keepdims=True).astype(BF16)
    lines = [bias[:, n * split : (n + 1) * split] for n in range(8)]
    lines = jnp.concatenate(lines + [jnp.zeros_like(lines[0])] * (BIAS_ROWS - 8), axis=0)
    for place in range(len(orders[0])):
        half = len(orders[0]) // 2
        exchange.halves(0)[place // half][place % half, rows:, :] = lines
    half = MP_ORDER[len(MP_ORDER) // 2 :]
    for m in half + [m for m in MP_ORDER if m not in half]:
        first = pl.multiple_of(flip(mp, m) * columns, 128)
        total[...] = tn(silu_cond[...], modulation_grad[:, pl.ds(first, columns)])
        for part, order in enumerate(orders):
            own = slice(part * split, (part + 1) * split)
            store_blocks(order, m, total, exchange.halves(part), rows, own)
        if m == half[0]:
            exchange.advance(2)
        if m == half[-1]:
            exchange.start(0)
            exchange.start(1)
            for n in range(len(late)):
                exchange.advance(3 + n)
    exchange.advance(0)
    exchange.advance(1)
    weight_load.wait()
    value = cond[...].astype(F32)
    gate = 1.0 / (1.0 + jnp.exp(-value))
    cond_grad[...] = nt(modulation_grad[...], weight_here[...]) * (gate * (1.0 + value * (1.0 - gate)))
    for n in [2] + [3 + n for n in range(len(late))] + [0, 1, 0, 2, 1, 2, 0, 1]:
        if n > 2 or exchange.left(n) > 1:
            exchange.advance(n)
    exchange.finish()


def run_tail(
    conditioning, silu_cond, patches, attn, modulation, cotangent, mlp, pieces, ada_weight, orders, rows, jobs, number
):
    tokens, width = silu_cond.shape
    exchange = Exchange(jobs, True)
    anywhere = pl.BlockSpec(memory_space=pl.ANY)
    columns = ada_weight.shape[1] // 4
    heads = jobs[2][0].shape[2]
    whole = lambda columns: pl.BlockSpec((tokens, columns), lambda i: (0, 0), pipeline_mode=pl.Buffered(1))
    gate = lambda n: pl.BlockSpec((tokens, width), lambda i: (0, n), pipeline_mode=pl.Buffered(1))
    shapes = [
        jax.ShapeDtypeStruct((tokens, width), F32),
        jax.ShapeDtypeStruct((tokens, width), BF16),
        jax.ShapeDtypeStruct((rows, heads * 3 // 4), F32),
        jax.ShapeDtypeStruct((rows, heads // 4), F32),
        jax.ShapeDtypeStruct((rows, columns), F32),
        jax.ShapeDtypeStruct((BIAS_ROWS, columns // 2), F32),
    ]
    shapes += [jax.ShapeDtypeStruct(chain.shape[1:], F32) for chain, _ in jobs[3:]]
    return pl.pallas_call(
        functools.partial(tail_kernel, orders, rows, exchange),
        grid=(1,),
        in_specs=[whole(width)] * 4
        + [gate(2), gate(5)]
        + [whole(width)] * 2
        + [anywhere] * 2
        + exchange.in_specs,
        out_specs=[constant_block(shape) for shape in shapes],
        out_shape=shapes,
        scratch_shapes=[
            pltpu.VMEM((tokens, ada_weight.shape[1]), BF16),
            pltpu.VMEM(ada_weight.shape, BF16),
            pltpu.VMEM((width, columns), F32),
            pltpu.SemaphoreType.DMA((2,)),
        ]
        + exchange.scratch,
        compiler_params=remote(exchange, number, 63),
        cost_estimate=cost(
            flops=16 * tokens * width * ada_weight.shape[1], bytes_accessed=100 * width * width, transcendentals=0
        ),
        name="tail",
    )(
        conditioning,
        silu_cond,
        patches,
        attn,
        modulation,
        modulation,
        cotangent,
        mlp,
        pieces,
        ada_weight,
        *exchange.operands,
    )


def finish_kernel(moves, rows, *refs):
    parts, refs = refs[: len(moves)], refs[len(moves) :]
    half = (len(refs) - 4) // 2
    plain, outs, experts = refs[:half], refs[half : 2 * half], refs[2 * half :]
    for source, target in zip(plain, outs):
        target[...] = source[...]
    for part, (expert, first, last) in zip(parts, moves):
        for kind in range(2):
            value = part[0, kind * rows : (kind + 1) * rows, :]
            if expert is None:
                experts[2 + kind][:, first:last] = value
            else:
                experts[kind][expert, :, first:last] = value


def run_finish(moves, plain, experts, rows, width):
    def block(array, index):
        return pl.BlockSpec((1,) + array.shape[1:], lambda i: (index, 0, 0), pipeline_mode=pl.Buffered(1))

    shapes = [jax.ShapeDtypeStruct(a.shape, a.dtype) for a in plain]
    shapes += [jax.ShapeDtypeStruct((experts, rows, width), F32)] * 2
    shapes += [jax.ShapeDtypeStruct((rows, width), F32)] * 2
    return pl.pallas_call(
        functools.partial(finish_kernel, [move[2:] for move in moves], rows),
        grid=(1,),
        in_specs=[block(array, index) for array, index, *_ in moves] + [whole_block(a) for a in plain],
        out_specs=[constant_block(shape) for shape in shapes],
        out_shape=shapes,
        compiler_params=pltpu.CompilerParams(vmem_limit_bytes=60 << 20),
        name="finish",
    )(*[move[0] for move in moves], *plain)


def gelu_and_slope(values):
    square = values * values
    bent = jnp.tanh(values * (GELU_A + (GELU_A * GELU_B) * square))
    half = 0.5 * (1.0 + bent)
    active = values * half
    return active, half + active * (1.0 - bent) * (GELU_A + (3.0 * GELU_A * GELU_B) * square)


class Gather:
    def __init__(self, own, far, held, send_sems, recv_sems):
        self.own, self.far, self.held, self.send_sems, self.recv_sems = own, far, held, send_sems, recv_sems

    def copy(self, place):
        far = self.held.at[1] if self.far is None else self.far
        return pltpu.make_async_remote_copy(
            src_ref=far if place == 2 else self.own,
            dst_ref=self.held.at[place],
            send_sem=self.send_sems.at[place],
            recv_sem=self.recv_sems.at[place],
            device_id=Exchange.partner("mp", 2 if place == 1 else 1),
            device_id_type=pl.DeviceIdType.MESH,
        )

    def begin(self):
        self.held[3] = self.own[...]
        if self.far is None:
            self.copy(1).start()
            self.copy(0).start()
        else:
            self.held[1] = self.far[...]
            self.copy(0).start()
            self.copy(2).start()

    def tile(self, step):
        @pl.when(step == 1)
        def _():
            self.copy(0).wait()

        if self.far is None:

            @pl.when(step == 2)
            def _():
                self.copy(1).wait()
                self.copy(2).start()

        @pl.when(step == 3)
        def _():
            self.copy(2).wait()

        return self.held[(step + 3) % 4]


def gather_barrier():
    barrier = pltpu.get_barrier_semaphore()
    for mask in (1, 2):
        pl.semaphore_signal(
            barrier, inc=1, device_id=Exchange.partner("mp", mask), device_id_type=pl.DeviceIdType.MESH
        )
    pl.semaphore_wait(barrier, 2)


def expert_kernel(columns, gathers, first, last, grad_later, exchange, units, rows, *refs):
    count = len(columns)
    gates, tokens, grads, refs = *refs[:3], refs[3:]
    if gathers:
        grads_far, refs = refs[0], refs[1:]
    ups, downs, refs = refs[:count], refs[count : 2 * count], refs[2 * count :]
    if not first:
        old_out, old_back, refs = refs[0], refs[1], refs[2:]
    number = len(exchange.operands)
    moved, refs = refs[:number], refs[number:]
    number = 2 * count if grad_later else sum(2 * len(own) for own in units)
    halves, refs = refs[:number], refs[number:]
    number = 4 if last else 2
    made, refs = refs[:number], refs[number:]
    number = len(exchange.shapes)
    moved_out, refs = refs[:number], refs[number:]
    if gathers:
        gathered, refs = refs[:2], refs[2:]
    number = 0 if grad_later else 2 * count
    sums, refs = refs[:number], refs[number:]
    step, final = pl.program_id(0), pl.num_programs(0) - 1
    if gathers:
        gather = [Gather(tokens, None, *refs[:3]), Gather(grads, grads_far, *refs[3:6])]
        refs = refs[6:]
    exchange.bind(moved, moved_out, refs)

    @pl.when(step == 0)
    def _():
        exchange.begin()

    @pl.when(step == 2)
    def _():
        exchange.early()

    if not grad_later:
        start_sums(step, sums)
    if gathers:

        @pl.when(step == 0)
        def _():
            gather_barrier()
            for one in gather:
                one.begin()

        x, own_grads = [one.tile(step) for one in gather]
        gathered[0][...] = x
        gathered[1][...] = own_grads
    else:
        x, own_grads = tokens[...], grads[...]
    g32 = own_grads.astype(F32)
    routed = None if first else old_out[...]
    returned = None if first else old_back[...]
    for n, column in enumerate(columns):
        gate = gates[:, column : column + 1]
        slot_grad = (gate * g32).astype(BF16)
        hidden, grad_pre, one, two = expert_pass(x, slot_grad, gate, ups[n][0], downs[n][0])
        routed = one if routed is None else routed + one
        returned = two if returned is None else returned + two
        if grad_later:
            halves[2 * n][...] = hidden
            halves[2 * n + 1][...] = grad_pre
        else:
            sums[2 * n][...] += tn(x, grad_pre)
            sums[2 * n + 1][...] += tn(slot_grad, hidden)
    if last:
        for value, (kept, sent) in ((routed, made[:2]), (returned, made[2:])):

            @pl.when(step < 2)
            def _():
                kept[0] = value.astype(BF16)

            @pl.when(step >= 2)
            def _():
                sent[0] = value.astype(BF16)

    else:
        made[0][...] = routed
        made[1][...] = returned
    if not grad_later:
        store_halves(step, units, sums, halves, rows)

    @pl.when(step == final)
    def _():
        exchange.finish()


def start_sums(step, sums):
    @pl.when(step == 0)
    def _():
        for total in sums:
            total[...] = jnp.zeros_like(total)


def store_units(units, sums, targets, rows):
    for (columns, order), halves in zip(units, targets):
        half = len(order) // 2
        for place, owner in enumerate(order):
            start = place * rows if half == 1 else rows_of(owner, rows)
            for part, total in enumerate(sums):
                halves[place // half][place % half, part * rows : (part + 1) * rows, :] = total[
                    pl.ds(start, rows), columns
                ].astype(BF16)


def store_halves(step, units, sums, halves, rows):
    @pl.when(step == pl.num_programs(0) - 1)
    def _():
        start = 0
        for n, own in enumerate(units):
            pairs = [halves[start + 2 * u : start + 2 * u + 2] for u in range(len(own))]
            start += 2 * len(own)
            store_units(own, sums[2 * n : 2 * n + 2], pairs, rows)


def unit_shapes(units, rows, width):
    shapes = []
    for columns, order in units:
        number = len(range(*columns.indices(width)))
        shapes += [jax.ShapeDtypeStruct((len(order) // 2, 2 * rows, number), BF16)] * 2
    return shapes


def constant_block(shape):
    return pl.BlockSpec(shape.shape, lambda *_: (0,) * len(shape.shape))


def expert_pass(x, slot_grad, gate, up, down):
    pre = nn(x, up)
    grad_hidden = nt(slot_grad, down)
    hidden, slope = gelu_and_slope(pre)
    hidden = hidden.astype(BF16)
    grad_pre = (grad_hidden * slope).astype(BF16)
    return hidden, grad_pre, gate * nn(hidden, down), nt(grad_pre, up)


TILE = 512


def token_tiles(columns):
    return pl.BlockSpec((TILE, columns), lambda t: (t, 0))


def run_experts(
    columns, weights, units, rows, gates, tokens, grads, sums, last, grad_later, jobs, number, gathers=False
):
    count = len(columns)
    total, width = gates.shape[0], tokens.shape[1]
    hidden = weights[0][0].shape[2]
    steps = total // TILE
    first = sums is None
    exchange = Exchange(jobs)

    def weight(index, shape):
        return pl.BlockSpec((1,) + shape, lambda t: (index, 0, 0), pipeline_mode=pl.Buffered(1))

    def tiles(columns):
        return pl.BlockSpec((TILE, columns), lambda t: ((t % 2) * 2 + t // 2 if gathers else t, 0))

    in_specs = (
        [tiles(gates.shape[1])]
        + ([pl.BlockSpec((TILE, width), lambda t: (0, 0))] * 3 if gathers else [tiles(width)] * 2)
        + [weight(i, (width, hidden)) for _, _, i in weights]
        + [weight(i, (hidden, width)) for _, _, i in weights]
        + ([] if first else [token_tiles(width), token_tiles(width)])
    )
    given = len(in_specs)
    if grad_later:
        shapes = [jax.ShapeDtypeStruct((total, hidden), BF16)] * (2 * count)
        specs = [token_tiles(hidden)] * (2 * count)
    else:
        shapes = [shape for own in units for shape in unit_shapes(own, rows, hidden)]
        specs = [constant_block(shape) for shape in shapes]
    made = len(shapes)
    if last:
        block = (1, TILE, width)
        sum_specs = [
            pl.BlockSpec(block, lambda t: (jnp.minimum(t, 1), 0, 0)),
            pl.BlockSpec(block, lambda t: (jnp.maximum(t - 2, 0), 0, 0)),
        ] * 2
        sum_shapes = [jax.ShapeDtypeStruct((2, TILE, width), BF16)] * 4
    else:
        sum_specs = [tiles(width)] * 2
        sum_shapes = [jax.ShapeDtypeStruct((total, width), F32)] * 2
    gather_scratch, gather_shapes = [], []
    if gathers:
        gather_scratch = ([pltpu.VMEM((4, TILE, width), BF16)] + [pltpu.SemaphoreType.DMA((3,))] * 2) * 2
        gather_shapes = [jax.ShapeDtypeStruct((total, width), BF16)] * 2
    aliases = {} if first or last else {given - 2: made, given - 1: made + 1}
    results = pl.pallas_call(
        functools.partial(expert_kernel, columns, gathers, first, last, grad_later, exchange, units, rows),
        grid_spec=pltpu.PrefetchScalarGridSpec(
            num_scalar_prefetch=0,
            grid=(steps,),
            in_specs=in_specs + exchange.in_specs,
            out_specs=specs + sum_specs + exchange.out_specs + [tiles(width)] * (2 * gathers),
            scratch_shapes=([] if grad_later else [pltpu.VMEM((width, hidden), F32)] * (2 * count))
            + gather_scratch
            + exchange.scratch,
        ),
        out_shape=shapes + sum_shapes + exchange.shapes + gather_shapes,
        input_output_aliases=aliases,
        compiler_params=remote(exchange, number, 60, gathers),
        cost_estimate=cost(
            flops=(8 if grad_later else 12) * count * total * width * hidden,
            bytes_accessed=20 * total * width + 8 * count * width * hidden,
            transcendentals=count * total * hidden,
        ),
        name=f"experts_{count}",
    )(
        gates,
        tokens,
        *(grads if gathers else [grads]),
        *[up for up, _, _ in weights],
        *[down for _, down, _ in weights],
        *(() if first else sums),
        *exchange.operands,
    )
    number = made + len(sum_shapes)
    if gathers:
        return results[:made], results[made:number], results[number:]
    exchange.spread(results[number:])
    return results[:made], results[made:number]


SLOTS = 3


def long_kernel(count, exchange, units, unit_steps, rows, gates, tokens, grads, up, down, *refs):
    old = refs[:2]
    number = len(exchange.operands)
    moved, refs = refs[2 : 2 + number], refs[2 + number :]
    new, finals, last_final, refs = refs[:2], refs[2], refs[3], refs[4:]
    number = 2 * len(units)
    half_done, raw, refs = refs[:number], refs[number : 2 * number], refs[2 * number :]
    number = len(exchange.shapes)
    moved_out, refs = refs[:number], refs[number:]
    sums, totals, send, work, gots = refs[:2], refs[2:4], refs[4], refs[5], refs[6:9]
    send_sems, recv_sems, load_sems, store_sems, refs = *refs[9:13], refs[13:]
    exchange.bind(moved, moved_out, refs)
    e, t = pl.program_id(0), pl.program_id(1)
    tiles = 4

    def copy(chain, step, unit):
        slot = chain % SLOTS
        blocks = 4 >> step
        columns = units[unit][0]
        place = pl.ds(columns.start, columns.stop - columns.start)
        source = send if step == 0 else work
        first = 0 if step == 0 else blocks
        return pltpu.make_async_remote_copy(
            src_ref=source.at[slot, pl.ds(first, blocks), :, place],
            dst_ref=gots[step].at[slot, :, :, place],
            send_sem=send_sems.at[slot, step, unit],
            recv_sem=recv_sems.at[slot, step, unit],
            device_id=exchange.partner(*unit_steps[unit][step]),
            device_id_type=pl.DeviceIdType.MESH,
        )

    def launch(chain, step):
        for unit in range(len(units)):
            copy(chain, step, unit).start()

    def arrive(chain, step):
        for unit in range(len(units)):
            copy(chain, step, unit).wait()

    def add(chain, step):
        slot = chain % SLOTS

        def one(i, carry):
            total = work[slot, i].astype(F32) + gots[step][slot, i].astype(F32)
            work[slot, i] = total.astype(BF16)
            return carry

        lax.fori_loop(0, 4 >> step, one, 0)

    def close(chain, target):
        arrive(chain, 2)
        slot = chain % SLOTS
        target[0] = work[slot, 0].astype(F32) + gots[2][slot, 0].astype(F32)

    def loads(n, tile):
        return pltpu.make_async_copy(
            old[n].at[pl.ds(tile * TILE, TILE), :], totals[n].at[tile], load_sems.at[n, tile]
        )

    def stores(n, tile):
        return pltpu.make_async_copy(
            totals[n].at[tile], new[n].at[pl.ds(tile * TILE, TILE), :], store_sems.at[n, tile]
        )

    @pl.when((e == 0) & (t == 0))
    def _():
        for tile in range(tiles):
            for n in range(2):
                loads(n, tile).start()
        exchange.begin(sorted({step for steps in unit_steps for step in steps}))

    for tile in range(tiles):

        @pl.when((e == 0) & (t == tile))
        def _():
            for n in range(2):
                loads(n, tile).wait()

    @pl.when((e == 1) & (t == 0))
    def _():
        exchange.all_once()

    @pl.when((e == 1) & (t == 2))
    def _():
        exchange.all_once()

    @pl.when((e == 2) & (t == 0))
    def _():
        exchange.finish()

    @pl.when((e >= 2) & (t == 0))
    def _():
        arrive(e - 2, 0)
        add(e - 2, 0)
        launch(e - 2, 1)

    @pl.when((e >= 1) & (t == 0))
    def _():
        launch(e - 1, 0)

    @pl.when((e >= 3) & (t == 2))
    def _():
        close(e - 3, finals)

    @pl.when((e >= 2) & (t == 2))
    def _():
        arrive(e - 2, 1)
        add(e - 2, 1)
        launch(e - 2, 2)

    @pl.when(t == 0)
    def _():
        for total in sums:
            total[...] = jnp.zeros_like(total)

    lane = lax.broadcasted_iota(jnp.int32, (1, gates.shape[1]), 1)
    gate = jnp.sum(jnp.where(lane == e, gates[...], 0.0), axis=1, keepdims=True)
    x = tokens[...]
    slot_grad = (gate * grads[...].astype(F32)).astype(BF16)
    hidden, grad_pre, one, two = expert_pass(x, slot_grad, gate, up[0], down[0])
    totals[0][t] += one
    totals[1][t] += two
    sums[0][...] += tn(x, grad_pre)
    sums[1][...] += tn(slot_grad, hidden)

    for tile in range(tiles):

        @pl.when((e == count - 1) & (t == tile))
        def _():
            for n in range(2):
                stores(n, tile).start()

    @pl.when((t == tiles - 1) & (e < count - 1))
    def _():
        slot = e % SLOTS
        pairs = [
            (work.at[slot, :, :, pl.ds(c.start, c.stop - c.start)], send.at[slot, :, :, pl.ds(c.start, c.stop - c.start)])
            for c, _ in units
        ]
        store_units(units, sums, pairs, rows)

    @pl.when((t == tiles - 1) & (e == count - 1))
    def _():
        store_units(units, sums, [raw[2 * u : 2 * u + 2] for u in range(len(units))], rows)
        close(count - 3, last_final)
        arrive(count - 2, 0)
        add(count - 2, 0)
        slot = (count - 2) % SLOTS
        for u, (c, _) in enumerate(units):
            half_done[2 * u][...] = work[slot, 0:2, :, c]
            half_done[2 * u + 1][...] = work[slot, 2:4, :, c]
        for tile in range(tiles):
            for n in range(2):
                stores(n, tile).wait()


def run_long(count, units, unit_steps, rows, gates, tokens, grads, expert_up, expert_down, sums, jobs, number):
    total, width = tokens.shape
    hidden = expert_up.shape[2]
    exchange = Exchange(jobs)
    steps = total // TILE
    tile = lambda columns: pl.BlockSpec((TILE, columns), lambda e, t: (t, 0))
    weight = lambda shape: pl.BlockSpec((1,) + shape, lambda e, t: (e, 0, 0))
    anywhere = pl.BlockSpec(memory_space=pl.ANY)
    raw = unit_shapes(units, rows, hidden)
    half_done = [jax.ShapeDtypeStruct((s.shape[0] // 2,) + s.shape[1:], BF16) for s in raw]
    final = (1, 2 * rows, hidden)
    results = pl.pallas_call(
        functools.partial(long_kernel, count, exchange, units, unit_steps, rows),
        grid=(count, steps),
        in_specs=[
            tile(gates.shape[1]),
            tile(width),
            tile(width),
            weight((width, hidden)),
            weight((hidden, width)),
            anywhere,
            anywhere,
        ]
        + exchange.in_specs,
        out_specs=[anywhere, anywhere]
        + [pl.BlockSpec(final, lambda e, t: (jnp.maximum(e - 3, 0), 0, 0)), pl.BlockSpec(final, lambda e, t: (0, 0, 0))]
        + [constant_block(shape) for shape in half_done + raw]
        + exchange.out_specs,
        out_shape=[jax.ShapeDtypeStruct((total, width), F32)] * 2
        + [jax.ShapeDtypeStruct((count - 3,) + final[1:], F32), jax.ShapeDtypeStruct(final, F32)]
        + half_done
        + raw
        + exchange.shapes,
        scratch_shapes=[pltpu.VMEM((width, hidden), F32)] * 2
        + [pltpu.VMEM((steps, TILE, width), F32)] * 2
        + [pltpu.VMEM((SLOTS, 4, 2 * rows, hidden), BF16)] * 2
        + [pltpu.VMEM((SLOTS, 4 >> n, 2 * rows, hidden), BF16) for n in range(3)]
        + [pltpu.SemaphoreType.DMA((SLOTS, 3, len(units)))] * 2
        + [pltpu.SemaphoreType.DMA((2, steps))] * 2
        + exchange.scratch,
        compiler_params=remote(exchange, number, 62),
        cost_estimate=cost(
            flops=12 * count * total * width * hidden,
            bytes_accessed=8 * count * total * width,
            transcendentals=count * total * hidden,
        ),
        name="experts_long",
    )(gates, tokens, grads, expert_up, expert_down, *sums, *exchange.operands)
    made = len(raw)
    exchange.spread(results[4 + 2 * made :])
    finished = [(results[2], n) for n in range(count - 3)] + [(results[3], 0)]
    return results[:2], finished, results[4 : 4 + made], results[4 + made : 4 + 2 * made]


def expert_grads_kernel(columns, exchange, units, rows, *refs):
    count = len(columns)
    gates, tokens, grads = refs[:3]
    saved, refs = refs[3 : 3 + 2 * count], refs[3 + 2 * count :]
    number = len(exchange.operands)
    moved, refs = refs[:number], refs[number:]
    number = sum(2 * len(own) for own in units)
    halves, refs = refs[:number], refs[number:]
    number = len(exchange.shapes)
    moved_out, refs = refs[:number], refs[number:]
    sums, refs = refs[: 2 * count], refs[2 * count :]
    step, final = pl.program_id(0), pl.num_programs(0) - 1
    exchange.bind(moved, moved_out, refs)

    @pl.when(step == 0)
    def _():
        exchange.begin()

    @pl.when(step == 1)
    def _():
        exchange.early(0, 1)

    @pl.when(step == 2)
    def _():
        exchange.early(1)

    start_sums(step, sums)
    x = tokens[...]
    g32 = grads[...].astype(F32)
    for n, column in enumerate(columns):
        slot_grad = (gates[:, column : column + 1] * g32).astype(BF16)
        sums[2 * n][...] += tn(x, saved[2 * n + 1][...])
        sums[2 * n + 1][...] += tn(slot_grad, saved[2 * n][...])
    store_halves(step, units, sums, halves, rows)

    @pl.when(step == final)
    def _():
        exchange.finish()


def run_expert_grads(columns, saved, units, rows, gates, tokens, grads, jobs, number):
    count = len(columns)
    total, width = tokens.shape
    hidden = saved[0].shape[1]
    steps = total // TILE
    shapes = [shape for own in units for shape in unit_shapes(own, rows, hidden)]
    exchange = Exchange(jobs)
    results = pl.pallas_call(
        functools.partial(expert_grads_kernel, columns, exchange, units, rows),
        grid_spec=pltpu.PrefetchScalarGridSpec(
            num_scalar_prefetch=0,
            grid=(steps,),
            in_specs=[token_tiles(gates.shape[1]), token_tiles(width), token_tiles(width)]
            + [token_tiles(hidden)] * (2 * count)
            + exchange.in_specs,
            out_specs=[constant_block(shape) for shape in shapes] + exchange.out_specs,
            scratch_shapes=[pltpu.VMEM((width, hidden), F32)] * (2 * count) + exchange.scratch,
        ),
        out_shape=shapes + exchange.shapes,
        compiler_params=remote(exchange, number, 60),
        cost_estimate=cost(
            flops=4 * count * total * width * hidden,
            bytes_accessed=(4 + 4 * count) * total * width,
            transcendentals=0,
        ),
        name="expert_grads",
    )(gates, tokens, grads, *saved, *exchange.operands)
    exchange.spread(results[len(shapes) :])
    return results[: len(shapes)]


def local(
    patches,
    conditioning,
    cotangent,
    segments,
    routes,
    gate_values,
    ada_weight,
    ada_bias,
    qkv_weight,
    out_weight,
    shared_up,
    shared_down,
    expert_up,
    expert_down,
):
    tokens, width = patches.shape
    group = routes.shape[0]
    experts = expert_up.shape[0]
    seq = segments.shape[1]
    n_dp, n_mp = lax.axis_size("dp"), lax.axis_size("mp")
    dp, mp = lax.axis_index("dp"), lax.axis_index("mp")
    rows = width // n_dp

    qkv_parts = gather_mp(jnp.transpose(qkv_weight, (1, 2, 0)).reshape(-1, width))
    out_parts = gather_mp(out_weight)

    silu_cond = jax.nn.silu(conditioning.astype(F32)).astype(BF16)
    modulation = jnp.dot(silu_cond, ada_weight, preferred_element_type=F32) + ada_bias[None, :]
    gate_two = modulation[:, 5 * width :]
    grad_mlp = (cotangent.astype(F32) * gate_two).astype(BF16)
    own_rows = tokens // seq
    own_segments = lax.dynamic_slice_in_dim(segments, mp * own_rows, own_rows, axis=0)
    number = jnp.arange(16, dtype=jnp.int32)[None, :]
    gates = jnp.sum(
        jnp.where(routes[:, :, None] == number[:, None, :], gate_values[:, :, None], 0.0), axis=1
    )
    gates = jnp.where(number == experts, 1.0, gates)
    gates = jnp.concatenate(
        [lax.dynamic_slice_in_dim(gates, (mp ^ m) * tokens, tokens, axis=0) for m in MP_ORDER],
        axis=0,
    )
    grad_mlp, qkv_parts[1], out_parts[1], gates, own_segments, silu_cond = lax.optimization_barrier(
        (grad_mlp, qkv_parts[1], out_parts[1], gates, own_segments, silu_cond)
    )
    grad_far = swap(grad_mlp, "mp", 2)

    results = run_forward(patches, modulation, own_segments, qkv_parts, out_parts)
    normed_one, qkv, attended, lse, attn_out, normed_two = results[0], results[1:5], *results[5:]

    shared = (shared_up[None], shared_down[None], 0)
    weights = {e: (expert_up, expert_down, e) for e in range(experts)}
    weights[experts] = shared
    even = halves_evenly(n_dp, rows)
    step = rows if even else width // 2
    reduced, chains, wholes = {}, {}, {}
    if even:
        near_step, far_step, *rest = dp_steps(n_dp)
        hidden = expert_up.shape[2]
        cut = hidden * 2 // 3
        unit_steps = [[near_step, far_step] + rest, [far_step, near_step] + rest]
        parts = [(slice(0, cut), unit_steps[0]), (slice(cut, hidden), unit_steps[1])]
        kinds = {c: parts for c in weights}
        kinds[experts - 2] = [(slice(0, hidden), unit_steps[1])]
        kinds[experts - 1] = [(slice(0, hidden), unit_steps[0])]
        units = {
            c: [(columns, [d for d, _ in block_order(steps)]) for columns, steps in kind]
            for c, kind in kinds.items()
        }
    else:
        units = {c: [(slice(0, expert_up.shape[2]), [0, 1])] for c in weights}

    def take_halves(columns, halves, done=0):
        halves = list(halves)
        for column in columns:
            own = [halves.pop(0) for _ in range(2 * len(units[column]))]
            if even:
                chains[column] = [
                    Chain(own[2 * u], own[2 * u + 1], steps, done)
                    for u, (_, steps) in enumerate(kinds[column])
                ]
            else:
                wholes[column] = own

    def jobs(**counts):
        if not even:
            return []
        return [(c, int(count[1:])) for count, columns in counts.items() for x in columns for c in chains[x]]

    def call(columns, sums, last, moves, number):
        return run_experts(
            columns,
            [weights[c] for c in columns],
            [units[c] for c in columns],
            step,
            gates,
            all_tokens,
            all_grads,
            sums,
            last,
            last,
            moves,
            number,
        )

    halves, sums, (all_tokens, all_grads) = run_experts(
        (experts,),
        [weights[experts]],
        [units[experts]],
        step,
        gates,
        normed_two,
        [grad_mlp, grad_far],
        None,
        False,
        False,
        [],
        0,
        True,
    )
    take_halves((experts,), halves)
    late = (experts - 2, experts - 1)
    if even:
        sums, finished, half_done, raw = run_long(
            experts - 2,
            units[0],
            unit_steps,
            rows,
            gates,
            all_tokens,
            all_grads,
            expert_up,
            expert_down,
            sums,
            jobs(n3=(experts,)),
            1,
        )
        take_halves((experts - 4,), half_done, 1)
        take_halves((experts - 3,), raw)
    else:
        for e in range(0, experts - 2, 2):
            halves, sums = call((e, e + 1), sums, False, [], 1 + e // 2)
            take_halves((e, e + 1), halves)
    saved, sums = call(late, sums, True, jobs(n1=(experts - 4, experts - 3)), 4)
    out_chain, back_chain = Chain(*sums[:2], MP_STEPS), Chain(*sums[2:], MP_STEPS)
    halves = run_expert_grads(
        late,
        saved,
        [units[c] for c in late],
        step,
        gates,
        all_tokens,
        all_grads,
        [(back_chain, 2)] + jobs(n1=(experts - 4, experts - 3)),
        5,
    )
    take_halves(late, halves)
    tail_steps = [MP_STEPS] * 3
    if even:
        y, z, rest = dp_steps(n_dp)[0], dp_steps(n_dp)[1], dp_steps(n_dp)[2:]
        core, x = MP_STEPS
        tail_steps = [[core, x, y, z] + rest, [core, y, x, z] + rest, [core, z, x, y] + rest]
    tail_orders = [block_order(steps) for steps in tail_steps]

    tail_rows = rows if even else width
    results = run_attention_back(
        patches,
        modulation,
        attn_out,
        cotangent,
        back_chain.result,
        normed_one,
        attended,
        lse,
        own_segments,
        qkv,
        qkv_parts,
        out_parts,
        tail_orders[0],
        tail_rows,
        [(out_chain, 2)] + jobs(n1=late + (experts - 3,)),
        6,
    )
    patches_grad, pieces, heads_halves = results[0], results[1], results[2:4]
    heads_chain = Chain(*heads_halves, tail_steps[0])
    split = ada_weight.shape[1] // n_mp // 2
    half = len(tail_orders[1]) // 2
    ada_chains = [
        Chain.inside((half, tail_rows + BIAS_ROWS, split), tail_steps[1]),
        Chain.inside((half, tail_rows, split), tail_steps[2]),
    ]
    number = len(tail_steps[0])
    results = run_tail(
        conditioning,
        silu_cond,
        patches,
        attn_out,
        modulation,
        cotangent,
        out_chain.result,
        pieces,
        ada_weight,
        tail_orders[1:],
        tail_rows,
        [(c, number) for c in ada_chains] + [(heads_chain, number)] + jobs(n2=late),
        7,
    )
    conditioning_grad, output, qkv_sum, out_total, ada_sum, bias_all = results[:6]
    bias_all = bias_all[: 2 * n_mp].reshape(-1)
    if even:
        moves = [(array, index, e, 0, hidden) for e, (array, index) in enumerate(finished)]
        moves += [(array[None], 0, column, 0, hidden) for column, array in zip(late, results[6:])]
        for column, own in chains.items():
            if column not in late:
                for chain, (columns, _) in zip(own, kinds[column]):
                    place = None if column == experts else column
                    moves.append((chain.result[None], 0, place, columns.start, columns.stop))
        results = run_finish(
            moves, [output, patches_grad, conditioning_grad, ada_sum], experts, rows, hidden
        )
        output, patches_grad, conditioning_grad, ada_sum = results[:4]
        expert_up_sum, expert_down_sum, up_sum, down_sum = results[4:]
    else:
        for column, (first, second) in wholes.items():
            whole = jnp.stack([first[0], second[0]]).reshape(2, 2, step, -1)
            whole = jnp.swapaxes(whole, 0, 1).reshape(2, width, -1)
            part = lax.psum_scatter(whole, "dp", scatter_dimension=1, tiled=True).astype(F32)
            reduced[column] = part[0], part[1]
        up_sum, down_sum = reduced[experts]
        expert_up_sum, expert_down_sum = [
            jnp.stack([reduced[e][part] for e in range(experts)]) for part in range(2)
        ]
        qkv_sum, out_total, ada_sum = [
            lax.psum_scatter(a.astype(BF16), "dp", scatter_dimension=0, tiled=True).astype(F32)
            for a in (qkv_sum, out_total, ada_sum)
        ]
        bias_all = lax.psum(bias_all, "dp")
    share = bias_all.shape[0] // (n_dp * n_mp)
    return (
        output,
        patches_grad,
        conditioning_grad,
        ada_sum,
        lax.dynamic_slice_in_dim(bias_all, (dp * n_mp + mp) * share, share),
        qkv_sum.reshape(rows, 3, -1),
        out_total.T,
        up_sum,
        down_sum.T,
        expert_up_sum,
        jnp.swapaxes(expert_down_sum, 1, 2),
    )


def solution(mesh):
    in_specs = (
        P(("dp", "mp"), None),
        P(("dp", "mp"), None),
        P(("dp", "mp"), None),
        P("dp", None),
        P("dp", None),
        P("dp", None),
        P(),
        P(),
        P(None, None, "mp"),
        P("mp", None),
        P(None, "mp"),
        P("mp", None),
        P(None, None, "mp"),
        P(None, "mp", None),
    )
    out_specs = (
        P(("dp", "mp"), None),
        P(("dp", "mp"), None),
        P(("dp", "mp"), None),
        P("dp", "mp"),
        P(("dp", "mp")),
        P("dp", None, "mp"),
        P("mp", "dp"),
        P("dp", "mp"),
        P("mp", "dp"),
        P(None, "dp", "mp"),
        P(None, "mp", "dp"),
    )
    return jax.shard_map(local, mesh=mesh, in_specs=in_specs, out_specs=out_specs, check_vma=False)
```

```python
import functools

import jax
import jax.numpy as jnp
from jax import lax
from jax.experimental import pallas as pl
from jax.experimental.pallas import tpu as pltpu
from jax.sharding import PartitionSpec as P

HEAD_DIM = 64
BF16 = jnp.bfloat16
F32 = jnp.float32
GELU_A = 0.7978845608028654
GELU_B = 0.044715


def nn(a, b):
    return lax.dot_general(a, b, (((1,), (0,)), ((), ())), preferred_element_type=F32)


def nt(a, b):
    return lax.dot_general(a, b, (((1,), (1,)), ((), ())), preferred_element_type=F32)


def tn(a, b):
    return lax.dot_general(a, b, (((0,), (0,)), ((), ())), preferred_element_type=F32)


def cost(flops, bytes_accessed, transcendentals):
    share = 16
    return pl.CostEstimate(
        flops=flops // share, bytes_accessed=bytes_accessed // share, transcendentals=transcendentals // share
    )


def swap(value, axis, mask):
    size = lax.axis_size(axis)
    return lax.ppermute(value, axis, [(i, i ^ mask) for i in range(size)])


def halves_evenly(n_dp, rows):
    return n_dp == 8 and rows % 16 == 0


def dp_steps(n_dp):
    return [("dp", 1 << bit) for bit in range(n_dp.bit_length() - 1)]


def block_order(steps):
    order = [(0, 0)]
    for axis, mask in reversed(steps):
        order = order + [(d ^ mask, m) if axis == "dp" else (d, m ^ mask) for d, m in order]
    return order


def flip(index, mask):
    bit = 1
    while bit <= mask:
        if mask & bit:
            index = index + bit * (1 - 2 * ((index // bit) % 2))
        bit *= 2
    return index


class Chain:
    def __init__(self, keep, send, steps, done=0):
        self.keep, self.send, self.steps, self.step = keep, send, steps, done
        self.shape = None if keep is None else keep.shape

    @classmethod
    def inside(cls, shape, steps):
        chain = cls(None, None, steps)
        chain.shape = shape
        return chain

    def take(self, results):
        if self.step == len(self.steps):
            self.result = results.pop(0)[0]
        else:
            self.keep, self.send = results.pop(0), results.pop(0)
            self.shape = self.keep.shape

    def advance(self):
        got = swap(self.send, *self.steps[self.step])
        total = self.keep.astype(F32) + got.astype(F32)
        half = total.shape[0] // 2
        self.step += 1
        self.take([total[:half].astype(BF16), total[half:].astype(BF16)] if half else [total])

    def finish(self):
        while self.step < len(self.steps):
            self.advance()
        return self.result


class Exchange:
    def __init__(self, jobs, sunk=False):
        self.jobs, self.sunk, self.sinks = jobs, sunk, {}
        self.operands, self.in_specs, self.out_specs, self.shapes, self.scratch = [], [], [], [], []
        self.plans = []
        for chain, count in jobs:
            blocks, tail = chain.shape[0], chain.shape[1:]
            steps = chain.steps[chain.step : chain.step + count]
            final = chain.step + count == len(chain.steps)
            self.plans.append((steps, final, blocks, chain.keep is None))
            if chain.keep is None:
                self.scratch.append(pltpu.VMEM(chain.shape, BF16))
            else:
                self.operands += [chain.keep, chain.send]
                self.in_specs += [pl.BlockSpec(memory_space=pl.ANY)] * 2
            left = blocks >> (count if not final else count - 1)
            kept = jax.ShapeDtypeStruct((left,) + tail, F32 if final else BF16)
            outs = [] if final and sunk else [kept] if final else [kept, kept]
            self.shapes += outs
            self.out_specs += [pl.BlockSpec(kept.shape, lambda *_: (0, 0, 0))] * len(outs)
            self.scratch.append(pltpu.VMEM((blocks,) + tail, BF16))
            self.scratch += [pltpu.VMEM((blocks >> n,) + tail, BF16) for n in range(count)]
            self.scratch += [
                pltpu.SemaphoreType.DMA((1,)),
                pltpu.SemaphoreType.DMA((count,)),
                pltpu.SemaphoreType.DMA((count,)),
            ]

    def bind(self, ins, outs, scratch):
        self.ins, self.outs, self.buffers, self.at = [], [], [], [0] * len(self.jobs)
        for steps, final, _, inner in self.plans:
            number = 0 if final and self.sunk else 1 if final else 2
            self.outs.append(outs[:number])
            outs = outs[number:]
            if inner:
                self.ins.append([None, scratch[0]])
                scratch = scratch[1:]
            else:
                self.ins.append(ins[:2])
                ins = ins[2:]
            number = len(steps) + 4
            self.buffers.append(scratch[:number])
            scratch = scratch[number:]

    @staticmethod
    def partner(axis, mask):
        return {axis: flip(lax.axis_index(axis), mask)}

    def load(self, n):
        return pltpu.make_async_copy(self.ins[n][0], self.buffers[n][0], self.buffers[n][-3].at[0])

    def copy(self, n, step):
        steps, _, blocks, _ = self.plans[n]
        work, send_sems, recv_sems = self.buffers[n][0], self.buffers[n][-2], self.buffers[n][-1]
        number = blocks >> step
        source = self.ins[n][1] if step == 0 else work.at[pl.ds(number, number)]
        return pltpu.make_async_remote_copy(
            src_ref=source,
            dst_ref=self.buffers[n][1 + step],
            send_sem=send_sems.at[step],
            recv_sem=recv_sems.at[step],
            device_id=self.partner(*steps[step]),
            device_id_type=pl.DeviceIdType.MESH,
        )

    def begin(self, others=()):
        partners = sorted({step for steps, *_ in self.plans for step in steps} | set(others))
        if partners:
            barrier = pltpu.get_barrier_semaphore()
            for step in partners:
                pl.semaphore_signal(
                    barrier, inc=1, device_id=self.partner(*step), device_id_type=pl.DeviceIdType.MESH
                )
            pl.semaphore_wait(barrier, len(partners))
        for n, (*_, inner) in enumerate(self.plans):
            if not inner:
                self.copy(n, 0).start()
                self.load(n).start()

    def halves(self, n):
        return self.buffers[n][0], self.ins[n][1]

    def start(self, n):
        self.copy(n, 0).start()

    def advance(self, n):
        steps, final, blocks, inner = self.plans[n]
        step = self.at[n]
        self.at[n] += 1
        work, got = self.buffers[n][0], self.buffers[n][1 + step]
        number = blocks >> step
        if step == 0 and not inner:
            self.load(n).wait()
        self.copy(n, step).wait()
        half = number // 2
        ending = step == len(steps) - 1

        def add(first, count, target, shift):
            def one(i, carry):
                total = work[i].astype(F32) + got[i].astype(F32)
                target[i - shift] = total.astype(target.dtype)
                return carry

            lax.fori_loop(first, first + count, one, 0)

        if ending and final and self.sunk:
            self.sinks[n](work[0].astype(F32) + got[0].astype(F32))
        elif ending and final:
            add(0, number, self.outs[n][0], 0)
        elif ending:
            add(0, half, self.outs[n][0], 0)
            add(half, half, self.outs[n][1], half)
        else:
            add(half, half, work, 0)
            self.copy(n, step + 1).start()
            add(0, half, work, 0)

    def left(self, n):
        return len(self.plans[n][0]) - self.at[n]

    def all_once(self):
        for n in range(len(self.jobs)):
            self.advance(n)

    def early(self, first=0, last=None):
        for n, (steps, *_) in list(enumerate(self.plans))[first:last]:
            while self.at[n] < len(steps) - 1:
                self.advance(n)

    def finish(self):
        for step in range(max([len(steps) for steps, *_ in self.plans], default=0)):
            for n, (steps, *_) in enumerate(self.plans):
                if self.at[n] == step and step < len(steps):
                    self.advance(n)

    def spread(self, results):
        results = list(results)
        for chain, count in self.jobs:
            chain.step += count
            if not (self.sunk and chain.step == len(chain.steps)):
                chain.take(results)


def remote(exchange, number, vmem, always=False):
    if not (exchange.jobs or always):
        return pltpu.CompilerParams(vmem_limit_bytes=vmem << 20)
    return pltpu.CompilerParams(vmem_limit_bytes=vmem << 20, collective_id=number, has_side_effects=True)


MP_STEPS = [("mp", 1), ("mp", 2)]
MP_ORDER = [m for _, m in block_order(MP_STEPS)]


def gather_mp(own):
    far = swap(own, "mp", 2)
    return [own, far, swap(own, "mp", 1), swap(far, "mp", 1)]


def normalize(values):
    center = values - jnp.mean(values, axis=-1, keepdims=True)
    inverse = lax.rsqrt(jnp.mean(center * center, axis=-1, keepdims=True) + 1e-06)
    return center * inverse, inverse


def normalize_back(normal, inverse, grad):
    return inverse * (
        grad
        - jnp.mean(grad, axis=-1, keepdims=True)
        - normal * jnp.mean(grad * normal, axis=-1, keepdims=True)
    )


def forward_kernel(
    heads, base, shift_one, scale_one, gate_one, shift_two, scale_two, seg_col, seg_row, *refs
):
    weights, out_weights = refs[:4], refs[4:8]
    normed_out, qkv, attended, lse_out, attn_out, second_out = refs[8], refs[9:13], *refs[13:]
    span = heads * HEAD_DIM
    x = base[...].astype(F32)
    normed = (normalize(x)[0] * (1.0 + scale_one[...]) + shift_one[...]).astype(BF16)
    normed_out[...] = normed
    same = seg_col[0] == seg_row[0]
    lane = lax.broadcasted_iota(jnp.int32, (1, 128), 1)
    lse_all = jnp.zeros(lse_out.shape, F32)
    attn = jnp.zeros(x.shape, F32)
    for block in range(4):
        qkv[block][...] = nt(normed, weights[block][...]).astype(BF16)
        for head in range(heads):
            at = head * HEAD_DIM
            q = qkv[block][:, at : at + HEAD_DIM]
            k = qkv[block][:, span + at : span + at + HEAD_DIM]
            v = qkv[block][:, 2 * span + at : 2 * span + at + HEAD_DIM]
            scores = jnp.where(same, nt(q, k) * (HEAD_DIM**-0.5), -1000000000.0)
            top = jnp.max(scores, axis=-1, keepdims=True)
            expo = jnp.exp(scores - top)
            total = jnp.sum(expo, axis=-1, keepdims=True)
            light = (expo * (1.0 / total)).astype(BF16)
            start = block * span + at
            attended[:, start : start + HEAD_DIM] = nn(light, v).astype(BF16)
            lse_all = jnp.where(lane == block * heads + head, top + jnp.log(total), lse_all)
        attn += nn(attended[:, block * span : (block + 1) * span], out_weights[block][...])
    lse_out[...] = lse_all
    attn_out[...] = attn
    middle = x + gate_one[...] * attn
    second_out[...] = (normalize(middle)[0] * (1.0 + scale_two[...]) + shift_two[...]).astype(BF16)


def rows_of(owner, rows):
    return pl.multiple_of(flip(lax.axis_index("dp"), owner) * rows, 8)


def store_blocks(order, m, total, halves, rows, columns=slice(None)):
    half = len(order) // 2
    for place, owner in enumerate(order):
        if owner[1] == m:
            start = 0 if rows == total.shape[0] else rows_of(owner[0], rows)
            halves[place // half][place % half, :rows, :] = total[pl.ds(start, rows), columns].astype(BF16)


def row_block(seq, columns):
    return pl.BlockSpec((seq, columns), lambda i, *_: (i, 0))


def column_block(seq, width, number):
    return pl.BlockSpec((seq, width), lambda i, *_: (i, number))


def whole_block(array):
    return pl.BlockSpec(array.shape, lambda i, *_: (0,) * array.ndim, pipeline_mode=pl.Buffered(1))


def segment_blocks(seq):
    return [
        pl.BlockSpec((1, seq, 1), lambda i, *_: (i, 0, 0)),
        pl.BlockSpec((1, 1, seq), lambda i, *_: (i, 0, 0)),
    ]


def run_forward(patches, modulation, segments, qkv_parts, out_parts):
    rows, seq = segments.shape
    tokens, width = patches.shape
    columns = qkv_parts[0].shape[0]
    heads = columns // (3 * HEAD_DIM)
    work = rows * 4 * heads * seq * seq
    shapes = (
        [(width, BF16)] + [(columns, BF16)] * 4 + [(width, BF16), (128, F32), (width, F32), (width, BF16)]
    )
    return pl.pallas_call(
        functools.partial(forward_kernel, heads),
        grid=(rows,),
        in_specs=[row_block(seq, width)]
        + [column_block(seq, width, n) for n in range(5)]
        + segment_blocks(seq)
        + [whole_block(w) for w in qkv_parts + out_parts],
        out_specs=[row_block(seq, c) for c, _ in shapes],
        out_shape=[jax.ShapeDtypeStruct((tokens, c), t) for c, t in shapes],
        compiler_params=pltpu.CompilerParams(vmem_limit_bytes=62 << 20),
        cost_estimate=cost(
            flops=4 * work * HEAD_DIM + 8 * tokens * width * width,
            bytes_accessed=40 * tokens * width,
            transcendentals=work,
        ),
        name="attention_half",
    )(
        patches,
        *([modulation] * 5),
        segments[:, :, None],
        segments[:, None, :],
        *qkv_parts,
        *out_parts,
    )


def attention_back_kernel(
    heads,
    exchange,
    order,
    rows,
    base,
    scale_one,
    gate_one,
    scale_two,
    attn,
    cotangent,
    summed,
    normed,
    attended,
    lse,
    seg_col,
    seg_row,
    *refs,
):
    qkv, weights, out_weights = refs[:4], refs[4:8], refs[8:12]
    number = len(exchange.operands)
    moved, refs = refs[12 : 12 + number], refs[12 + number :]
    patches_grad, pieces, halves, refs = refs[0], refs[1], refs[2:4], refs[4:]
    number = len(exchange.shapes)
    moved_out, refs = refs[:number], refs[number:]
    totals, grad_qkv, refs = refs[:4], refs[4], refs[5:]
    step, last = pl.program_id(0), pl.num_programs(0) - 1
    exchange.bind(moved, moved_out, refs)

    @pl.when(step == 0)
    def _():
        exchange.begin()

    span = heads * HEAD_DIM
    width = base.shape[1]
    factor = HEAD_DIM**-0.5
    same = seg_col[0] == seg_row[0]
    grad, branch, gate = summed[...], attn[...], gate_one[...]
    normal, inverse = normalize(base[...].astype(F32) + gate * branch)
    middle_grad = cotangent[...].astype(F32) + normalize_back(
        normal, inverse, grad * (1.0 + scale_two[...])
    )
    patches_grad[...] = middle_grad
    pieces[:, 2 * width : 3 * width] = (middle_grad * branch).astype(BF16)
    pieces[:, 3 * width : 4 * width] = grad.astype(BF16)
    pieces[:, 4 * width :] = (grad * normal).astype(BF16)
    upper = (middle_grad * gate).astype(BF16)
    normed_grad = jnp.zeros(base.shape, F32)
    for block in range(4):
        if block == 0:

            @pl.when(step == last)
            def _():
                exchange.early(0, 1)

        if block == 2:

            @pl.when(step == last)
            def _():
                exchange.early(1)

        grad_heads = nt(upper, out_weights[block][...]).astype(BF16)
        for head in range(heads):
            at = head * HEAD_DIM
            n = block * heads + head
            q = qkv[block][:, at : at + HEAD_DIM]
            k = qkv[block][:, span + at : span + at + HEAD_DIM]
            v = qkv[block][:, 2 * span + at : 2 * span + at + HEAD_DIM]
            g = grad_heads[:, at : at + HEAD_DIM]
            scores = jnp.where(same, nt(q, k) * factor, -1000000000.0)
            probs = jnp.exp(scores - lse[:, n : n + 1])
            grad_probs = nt(g, v)
            term = jnp.sum(probs * grad_probs, axis=-1, keepdims=True)
            grad_scores = (probs * (grad_probs - term)).astype(BF16)
            grad_qkv[:, at : at + HEAD_DIM] = (nn(grad_scores, k) * factor).astype(BF16)
            grad_qkv[:, span + at : span + at + HEAD_DIM] = (tn(grad_scores, q) * factor).astype(BF16)
            grad_qkv[:, 2 * span + at : 2 * span + at + HEAD_DIM] = tn(
                probs.astype(BF16), g
            ).astype(BF16)
        made = grad_qkv[...]
        normed_grad += nn(made, weights[block][...])
        of_qkv = tn(normed[...], made)
        of_out = tn(upper, attended[:, block * span : (block + 1) * span])

        @pl.when(step == 0)
        def _():
            totals[block][:, : 3 * span] = of_qkv
            totals[block][:, 3 * span :] = of_out

        @pl.when(step > 0)
        def _():
            totals[block][:, : 3 * span] += of_qkv
            totals[block][:, 3 * span :] += of_out

        @pl.when(step == last)
        def _():
            store_blocks(order, MP_ORDER[block], totals[block], halves, rows)

    normal, inverse = normalize(base[...].astype(F32))
    patches_grad[...] += normalize_back(normal, inverse, normed_grad * (1.0 + scale_one[...]))
    pieces[:, :width] = normed_grad.astype(BF16)
    pieces[:, width : 2 * width] = (normed_grad * normal).astype(BF16)

    @pl.when(step == last)
    def _():
        exchange.finish()


def run_attention_back(
    patches,
    modulation,
    attn,
    cotangent,
    summed,
    normed,
    attended,
    lse,
    segments,
    qkv,
    qkv_parts,
    out_parts,
    order,
    rows,
    jobs,
    number,
):
    count, seq = segments.shape
    tokens, width = patches.shape
    columns = qkv[0].shape[1]
    heads = columns // (3 * HEAD_DIM)
    work = count * 4 * heads * seq * seq
    wide = row_block(seq, width)
    half = (len(order) // 2, rows, 4 * columns // 3)
    exchange = Exchange(jobs)
    results = pl.pallas_call(
        functools.partial(attention_back_kernel, heads, exchange, order, rows),
        grid_spec=pltpu.PrefetchScalarGridSpec(
            num_scalar_prefetch=0,
            grid=(count,),
            in_specs=[wide]
            + [column_block(seq, width, n) for n in (1, 2, 4)]
            + [wide] * 5
            + [row_block(seq, 128)]
            + segment_blocks(seq)
            + [row_block(seq, columns)] * 4
            + [whole_block(w) for w in qkv_parts + out_parts]
            + exchange.in_specs,
            out_specs=[wide, row_block(seq, 5 * width)]
            + [pl.BlockSpec(half, lambda i, *_: (0, 0, 0))] * 2
            + exchange.out_specs,
            scratch_shapes=[pltpu.VMEM((width, 4 * columns // 3), F32)] * 4
            + [pltpu.VMEM((seq, columns), BF16)]
            + exchange.scratch,
        ),
        out_shape=[
            jax.ShapeDtypeStruct((tokens, width), F32),
            jax.ShapeDtypeStruct((tokens, 5 * width), BF16),
        ]
        + [jax.ShapeDtypeStruct(half, BF16)] * 2
        + exchange.shapes,
        compiler_params=remote(exchange, number, 62),
        cost_estimate=cost(
            flops=10 * work * HEAD_DIM + 16 * tokens * width * width,
            bytes_accessed=60 * tokens * width,
            transcendentals=work,
        ),
        name="attention_back",
    )(
        patches,
        *([modulation] * 3),
        attn,
        cotangent,
        summed,
        normed,
        attended,
        lse,
        segments[:, :, None],
        segments[:, None, :],
        *qkv,
        *qkv_parts,
        *out_parts,
        *exchange.operands,
    )
    exchange.spread(results[4:])
    return results[:4]


BIAS_ROWS = 16


def tail_kernel(
    orders,
    rows,
    exchange,
    cond,
    silu_cond,
    base,
    attn,
    gate_one,
    gate_two,
    cotangent,
    mlp,
    pieces,
    weight,
    *refs,
):
    number = len(exchange.operands)
    moved, refs = refs[:number], refs[number:]
    cond_grad, output, qkv_grad, out_grad, ada_grad, bias_grad, refs = *refs[:6], refs[6:]
    number = len(exchange.jobs) - 3
    late, refs = refs[:number], refs[number:]
    modulation_grad, weight_here, total, load_sems, refs = *refs[:4], refs[4:]
    exchange.bind(moved, (), refs)
    tokens, width = base.shape
    pieces_load = pltpu.make_async_copy(
        pieces, modulation_grad.at[:, pl.ds(0, pieces.shape[1])], load_sems.at[0]
    )
    weight_load = pltpu.make_async_copy(weight, weight_here, load_sems.at[1])
    pieces_load.start()
    weight_load.start()
    exchange.begin()
    grad_out, branch = cotangent[...].astype(F32), mlp[...]
    modulation_grad[:, 5 * width :] = (grad_out * branch).astype(BF16)
    middle = base[...].astype(F32) + gate_one[...] * attn[...]
    output[...] = (middle + gate_two[...] * branch).astype(BF16)
    pieces_load.wait()

    columns = modulation_grad.shape[1] // 4
    split = columns // 2
    heads = qkv_grad.shape[1]
    mp = lax.axis_index("mp")

    def keep_heads(value):
        qkv_grad[...] = value[:, :heads]
        out_grad[...] = value[:, heads:]

    def keep_low(value):
        ada_grad[:, :split] = value[:rows]
        bias_grad[...] = value[rows:]

    def keep_high(value):
        ada_grad[:, split:] = value

    def keep_late(target, value):
        target[...] = value

    exchange.sinks = {0: keep_low, 1: keep_high, 2: keep_heads}
    for n, target in enumerate(late):
        exchange.sinks[3 + n] = functools.partial(keep_late, target)
    bias = jnp.sum(modulation_grad[...].astype(F32), axis=0, keepdims=True).astype(BF16)
    lines = [bias[:, n * split : (n + 1) * split] for n in range(8)]
    lines = jnp.concatenate(lines + [jnp.zeros_like(lines[0])] * (BIAS_ROWS - 8), axis=0)
    for place in range(len(orders[0])):
        half = len(orders[0]) // 2
        exchange.halves(0)[place // half][place % half, rows:, :] = lines
    exchange.advance(2)
    half = MP_ORDER[len(MP_ORDER) // 2 :]
    for m in half + [m for m in MP_ORDER if m not in half]:
        first = pl.multiple_of(flip(mp, m) * columns, 128)
        total[...] = tn(silu_cond[...], modulation_grad[:, pl.ds(first, columns)])
        for part, order in enumerate(orders):
            own = slice(part * split, (part + 1) * split)
            store_blocks(order, m, total, exchange.halves(part), rows, own)
        if m == half[-1]:
            exchange.start(0)
            exchange.start(1)
            for n in range(len(late)):
                exchange.advance(3 + n)
    exchange.advance(0)
    exchange.advance(1)
    weight_load.wait()
    value = cond[...].astype(F32)
    gate = 1.0 / (1.0 + jnp.exp(-value))
    cond_grad[...] = nt(modulation_grad[...], weight_here[...]) * (gate * (1.0 + value * (1.0 - gate)))
    for n in [2] + [3 + n for n in range(len(late))] + [0, 1, 0, 2, 1, 2, 0, 1]:
        if n > 2 or exchange.left(n) > 1:
            exchange.advance(n)
    exchange.finish()


def run_tail(
    conditioning, silu_cond, patches, attn, modulation, cotangent, mlp, pieces, ada_weight, orders, rows, jobs, number
):
    tokens, width = silu_cond.shape
    exchange = Exchange(jobs, True)
    anywhere = pl.BlockSpec(memory_space=pl.ANY)
    columns = ada_weight.shape[1] // 4
    heads = jobs[2][0].shape[2]
    whole = lambda columns: pl.BlockSpec((tokens, columns), lambda i: (0, 0), pipeline_mode=pl.Buffered(1))
    gate = lambda n: pl.BlockSpec((tokens, width), lambda i: (0, n), pipeline_mode=pl.Buffered(1))
    shapes = [
        jax.ShapeDtypeStruct((tokens, width), F32),
        jax.ShapeDtypeStruct((tokens, width), BF16),
        jax.ShapeDtypeStruct((rows, heads * 3 // 4), F32),
        jax.ShapeDtypeStruct((rows, heads // 4), F32),
        jax.ShapeDtypeStruct((rows, columns), F32),
        jax.ShapeDtypeStruct((BIAS_ROWS, columns // 2), F32),
    ]
    shapes += [jax.ShapeDtypeStruct(chain.shape[1:], F32) for chain, _ in jobs[3:]]
    return pl.pallas_call(
        functools.partial(tail_kernel, orders, rows, exchange),
        grid=(1,),
        in_specs=[whole(width)] * 4
        + [gate(2), gate(5)]
        + [whole(width)] * 2
        + [anywhere] * 2
        + exchange.in_specs,
        out_specs=[constant_block(shape) for shape in shapes],
        out_shape=shapes,
        scratch_shapes=[
            pltpu.VMEM((tokens, ada_weight.shape[1]), BF16),
            pltpu.VMEM(ada_weight.shape, BF16),
            pltpu.VMEM((width, columns), F32),
            pltpu.SemaphoreType.DMA((2,)),
        ]
        + exchange.scratch,
        compiler_params=remote(exchange, number, 63),
        cost_estimate=cost(
            flops=16 * tokens * width * ada_weight.shape[1], bytes_accessed=100 * width * width, transcendentals=0
        ),
        name="tail",
    )(
        conditioning,
        silu_cond,
        patches,
        attn,
        modulation,
        modulation,
        cotangent,
        mlp,
        pieces,
        ada_weight,
        *exchange.operands,
    )


def finish_kernel(moves, rows, *refs):
    parts, refs = refs[: len(moves)], refs[len(moves) :]
    half = (len(refs) - 4) // 2
    plain, outs, experts = refs[:half], refs[half : 2 * half], refs[2 * half :]
    for source, target in zip(plain, outs):
        target[...] = source[...]
    for part, (expert, first, last) in zip(parts, moves):
        for kind in range(2):
            value = part[0, kind * rows : (kind + 1) * rows, :]
            if expert is None:
                experts[2 + kind][:, first:last] = value
            else:
                experts[kind][expert, :, first:last] = value


def run_finish(moves, plain, experts, rows, width):
    def block(array, index):
        return pl.BlockSpec((1,) + array.shape[1:], lambda i: (index, 0, 0), pipeline_mode=pl.Buffered(1))

    shapes = [jax.ShapeDtypeStruct(a.shape, a.dtype) for a in plain]
    shapes += [jax.ShapeDtypeStruct((experts, rows, width), F32)] * 2
    shapes += [jax.ShapeDtypeStruct((rows, width), F32)] * 2
    return pl.pallas_call(
        functools.partial(finish_kernel, [move[2:] for move in moves], rows),
        grid=(1,),
        in_specs=[block(array, index) for array, index, *_ in moves] + [whole_block(a) for a in plain],
        out_specs=[constant_block(shape) for shape in shapes],
        out_shape=shapes,
        compiler_params=pltpu.CompilerParams(vmem_limit_bytes=60 << 20),
        name="finish",
    )(*[move[0] for move in moves], *plain)


def gelu_and_slope(values):
    square = values * values
    bent = jnp.tanh(values * (GELU_A + (GELU_A * GELU_B) * square))
    half = 0.5 * (1.0 + bent)
    active = values * half
    return active, half + active * (1.0 - bent) * (GELU_A + (3.0 * GELU_A * GELU_B) * square)


class Gather:
    def __init__(self, own, far, held, send_sems, recv_sems):
        self.own, self.far, self.held, self.send_sems, self.recv_sems = own, far, held, send_sems, recv_sems

    def copy(self, place):
        far = self.held.at[1] if self.far is None else self.far
        return pltpu.make_async_remote_copy(
            src_ref=far if place == 2 else self.own,
            dst_ref=self.held.at[place],
            send_sem=self.send_sems.at[place],
            recv_sem=self.recv_sems.at[place],
            device_id=Exchange.partner("mp", 2 if place == 1 else 1),
            device_id_type=pl.DeviceIdType.MESH,
        )

    def begin(self):
        if self.far is None:
            self.copy(1).start()
            self.copy(0).start()
        else:
            self.copy(0).start()
            self.copy(2).start()
            self.held[1] = self.far[...]
        self.held[3] = self.own[...]

    def tile(self, step):
        @pl.when(step == 1)
        def _():
            self.copy(0).wait()

        if self.far is None:

            @pl.when(step == 2)
            def _():
                self.copy(1).wait()
                self.copy(2).start()

        @pl.when(step == 3)
        def _():
            self.copy(2).wait()

        return self.held[(step + 3) % 4]


def gather_barrier():
    barrier = pltpu.get_barrier_semaphore()
    for mask in (1, 2):
        pl.semaphore_signal(
            barrier, inc=1, device_id=Exchange.partner("mp", mask), device_id_type=pl.DeviceIdType.MESH
        )
    pl.semaphore_wait(barrier, 2)


def expert_kernel(columns, gathers, first, last, grad_later, exchange, units, rows, *refs):
    count = len(columns)
    gates, tokens, grads, refs = *refs[:3], refs[3:]
    if gathers:
        grads_far, refs = refs[0], refs[1:]
    ups, downs, refs = refs[:count], refs[count : 2 * count], refs[2 * count :]
    if not first:
        old_out, old_back, refs = refs[0], refs[1], refs[2:]
    number = len(exchange.operands)
    moved, refs = refs[:number], refs[number:]
    number = 2 * count if grad_later else sum(2 * len(own) for own in units)
    halves, refs = refs[:number], refs[number:]
    number = 4 if last else 2
    made, refs = refs[:number], refs[number:]
    number = len(exchange.shapes)
    moved_out, refs = refs[:number], refs[number:]
    if gathers:
        gathered, refs = refs[:2], refs[2:]
    number = 0 if grad_later else 2 * count
    sums, refs = refs[:number], refs[number:]
    step, final = pl.program_id(0), pl.num_programs(0) - 1
    if gathers:
        gather = [Gather(tokens, None, *refs[:3]), Gather(grads, grads_far, *refs[3:6])]
        refs = refs[6:]
    exchange.bind(moved, moved_out, refs)

    @pl.when(step == 0)
    def _():
        exchange.begin()

    @pl.when(step == 2)
    def _():
        exchange.early()

    if not grad_later:
        start_sums(step, sums)
    if gathers:

        @pl.when(step == 0)
        def _():
            gather_barrier()
            for one in gather:
                one.begin()

        x, own_grads = [one.tile(step) for one in gather]
        gathered[0][...] = x
        gathered[1][...] = own_grads
    else:
        x, own_grads = tokens[...], grads[...]
    g32 = own_grads.astype(F32)
    routed = None if first else old_out[...]
    returned = None if first else old_back[...]
    for n, column in enumerate(columns):
        gate = gates[:, column : column + 1]
        slot_grad = (gate * g32).astype(BF16)
        hidden, grad_pre, one, two = expert_pass(x, slot_grad, gate, ups[n][0], downs[n][0])
        routed = one if routed is None else routed + one
        returned = two if returned is None else returned + two
        if grad_later:
            halves[2 * n][...] = hidden
            halves[2 * n + 1][...] = grad_pre
        else:
            sums[2 * n][...] += tn(x, grad_pre)
            sums[2 * n + 1][...] += tn(slot_grad, hidden)
    if last:
        for value, (kept, sent) in ((routed, made[:2]), (returned, made[2:])):

            @pl.when(step < 2)
            def _():
                kept[0] = value.astype(BF16)

            @pl.when(step >= 2)
            def _():
                sent[0] = value.astype(BF16)

    else:
        made[0][...] = routed
        made[1][...] = returned
    if not grad_later:
        store_halves(step, units, sums, halves, rows)

    @pl.when(step == final)
    def _():
        exchange.finish()


def start_sums(step, sums):
    @pl.when(step == 0)
    def _():
        for total in sums:
            total[...] = jnp.zeros_like(total)


def store_units(units, sums, targets, rows):
    for (columns, order), halves in zip(units, targets):
        half = len(order) // 2
        for place, owner in enumerate(order):
            start = place * rows if half == 1 else rows_of(owner, rows)
            for part, total in enumerate(sums):
                halves[place // half][place % half, part * rows : (part + 1) * rows, :] = total[
                    pl.ds(start, rows), columns
                ].astype(BF16)


def store_halves(step, units, sums, halves, rows):
    @pl.when(step == pl.num_programs(0) - 1)
    def _():
        start = 0
        for n, own in enumerate(units):
            pairs = [halves[start + 2 * u : start + 2 * u + 2] for u in range(len(own))]
            start += 2 * len(own)
            store_units(own, sums[2 * n : 2 * n + 2], pairs, rows)


def unit_shapes(units, rows, width):
    shapes = []
    for columns, order in units:
        number = len(range(*columns.indices(width)))
        shapes += [jax.ShapeDtypeStruct((len(order) // 2, 2 * rows, number), BF16)] * 2
    return shapes


def constant_block(shape):
    return pl.BlockSpec(shape.shape, lambda *_: (0,) * len(shape.shape))


def expert_pass(x, slot_grad, gate, up, down):
    pre = nn(x, up)
    grad_hidden = nt(slot_grad, down)
    hidden, slope = gelu_and_slope(pre)
    hidden = hidden.astype(BF16)
    grad_pre = (grad_hidden * slope).astype(BF16)
    return hidden, grad_pre, gate * nn(hidden, down), nt(grad_pre, up)


TILE = 512


def token_tiles(columns):
    return pl.BlockSpec((TILE, columns), lambda t: (t, 0))


def run_experts(
    columns, weights, units, rows, gates, tokens, grads, sums, last, grad_later, jobs, number, gathers=False
):
    count = len(columns)
    total, width = gates.shape[0], tokens.shape[1]
    hidden = weights[0][0].shape[2]
    steps = total // TILE
    first = sums is None
    exchange = Exchange(jobs)

    def weight(index, shape):
        return pl.BlockSpec((1,) + shape, lambda t: (index, 0, 0), pipeline_mode=pl.Buffered(1))

    def tiles(columns):
        return pl.BlockSpec((TILE, columns), lambda t: ((t % 2) * 2 + t // 2 if gathers else t, 0))

    in_specs = (
        [tiles(gates.shape[1])]
        + ([pl.BlockSpec((TILE, width), lambda t: (0, 0))] * 3 if gathers else [tiles(width)] * 2)
        + [weight(i, (width, hidden)) for _, _, i in weights]
        + [weight(i, (hidden, width)) for _, _, i in weights]
        + ([] if first else [token_tiles(width), token_tiles(width)])
    )
    given = len(in_specs)
    if grad_later:
        shapes = [jax.ShapeDtypeStruct((total, hidden), BF16)] * (2 * count)
        specs = [token_tiles(hidden)] * (2 * count)
    else:
        shapes = [shape for own in units for shape in unit_shapes(own, rows, hidden)]
        specs = [constant_block(shape) for shape in shapes]
    made = len(shapes)
    if last:
        block = (1, TILE, width)
        sum_specs = [
            pl.BlockSpec(block, lambda t: (jnp.minimum(t, 1), 0, 0)),
            pl.BlockSpec(block, lambda t: (jnp.maximum(t - 2, 0), 0, 0)),
        ] * 2
        sum_shapes = [jax.ShapeDtypeStruct((2, TILE, width), BF16)] * 4
    else:
        sum_specs = [tiles(width)] * 2
        sum_shapes = [jax.ShapeDtypeStruct((total, width), F32)] * 2
    gather_scratch, gather_shapes = [], []
    if gathers:
        gather_scratch = ([pltpu.VMEM((4, TILE, width), BF16)] + [pltpu.SemaphoreType.DMA((3,))] * 2) * 2
        gather_shapes = [jax.ShapeDtypeStruct((total, width), BF16)] * 2
    aliases = {} if first or last else {given - 2: made, given - 1: made + 1}
    results = pl.pallas_call(
        functools.partial(expert_kernel, columns, gathers, first, last, grad_later, exchange, units, rows),
        grid_spec=pltpu.PrefetchScalarGridSpec(
            num_scalar_prefetch=0,
            grid=(steps,),
            in_specs=in_specs + exchange.in_specs,
            out_specs=specs + sum_specs + exchange.out_specs + [tiles(width)] * (2 * gathers),
            scratch_shapes=([] if grad_later else [pltpu.VMEM((width, hidden), F32)] * (2 * count))
            + gather_scratch
            + exchange.scratch,
        ),
        out_shape=shapes + sum_shapes + exchange.shapes + gather_shapes,
        input_output_aliases=aliases,
        compiler_params=remote(exchange, number, 60, gathers),
        cost_estimate=cost(
            flops=(8 if grad_later else 12) * count * total * width * hidden,
            bytes_accessed=20 * total * width + 8 * count * width * hidden,
            transcendentals=count * total * hidden,
        ),
        name=f"experts_{count}",
    )(
        gates,
        tokens,
        *(grads if gathers else [grads]),
        *[up for up, _, _ in weights],
        *[down for _, down, _ in weights],
        *(() if first else sums),
        *exchange.operands,
    )
    number = made + len(sum_shapes)
    if gathers:
        return results[:made], results[made:number], results[number:]
    exchange.spread(results[number:])
    return results[:made], results[made:number]


SLOTS = 3


def long_kernel(count, exchange, units, unit_steps, rows, gates, tokens, grads, up, down, *refs):
    old = refs[:2]
    number = len(exchange.operands)
    moved, refs = refs[2 : 2 + number], refs[2 + number :]
    new, finals, last_final, refs = refs[:2], refs[2], refs[3], refs[4:]
    number = 2 * len(units)
    half_done, raw, refs = refs[:number], refs[number : 2 * number], refs[2 * number :]
    number = len(exchange.shapes)
    moved_out, refs = refs[:number], refs[number:]
    sums, totals, send, work, gots = refs[:2], refs[2:4], refs[4], refs[5], refs[6:9]
    send_sems, recv_sems, load_sems, store_sems, refs = *refs[9:13], refs[13:]
    exchange.bind(moved, moved_out, refs)
    e, t = pl.program_id(0), pl.program_id(1)
    tiles = 4

    def copy(chain, step, unit):
        slot = chain % SLOTS
        blocks = 4 >> step
        columns = units[unit][0]
        place = pl.ds(columns.start, columns.stop - columns.start)
        source = send if step == 0 else work
        first = 0 if step == 0 else blocks
        return pltpu.make_async_remote_copy(
            src_ref=source.at[slot, pl.ds(first, blocks), :, place],
            dst_ref=gots[step].at[slot, :, :, place],
            send_sem=send_sems.at[slot, step, unit],
            recv_sem=recv_sems.at[slot, step, unit],
            device_id=exchange.partner(*unit_steps[unit][step]),
            device_id_type=pl.DeviceIdType.MESH,
        )

    def launch(chain, step):
        for unit in range(len(units)):
            copy(chain, step, unit).start()

    def arrive(chain, step):
        for unit in range(len(units)):
            copy(chain, step, unit).wait()

    def add(chain, step):
        slot = chain % SLOTS

        def one(i, carry):
            total = work[slot, i].astype(F32) + gots[step][slot, i].astype(F32)
            work[slot, i] = total.astype(BF16)
            return carry

        lax.fori_loop(0, 4 >> step, one, 0)

    def close(chain, target):
        arrive(chain, 2)
        slot = chain % SLOTS
        target[0] = work[slot, 0].astype(F32) + gots[2][slot, 0].astype(F32)

    def loads(n, tile):
        return pltpu.make_async_copy(
            old[n].at[pl.ds(tile * TILE, TILE), :], totals[n].at[tile], load_sems.at[n, tile]
        )

    def stores(n, tile):
        return pltpu.make_async_copy(
            totals[n].at[tile], new[n].at[pl.ds(tile * TILE, TILE), :], store_sems.at[n, tile]
        )

    @pl.when((e == 0) & (t == 0))
    def _():
        for tile in range(tiles):
            for n in range(2):
                loads(n, tile).start()
        exchange.begin(sorted({step for steps in unit_steps for step in steps}))

    for tile in range(tiles):

        @pl.when((e == 0) & (t == tile))
        def _():
            for n in range(2):
                loads(n, tile).wait()

    @pl.when((e == 1) & (t == 0))
    def _():
        exchange.all_once()

    @pl.when((e == 1) & (t == 2))
    def _():
        exchange.all_once()

    @pl.when((e == 2) & (t == 0))
    def _():
        exchange.finish()

    @pl.when((e >= 2) & (t == 0))
    def _():
        arrive(e - 2, 0)
        add(e - 2, 0)
        launch(e - 2, 1)

    @pl.when((e >= 1) & (t == 0))
    def _():
        launch(e - 1, 0)

    @pl.when((e >= 3) & (t == 2))
    def _():
        close(e - 3, finals)

    @pl.when((e >= 2) & (t == 2))
    def _():
        arrive(e - 2, 1)
        add(e - 2, 1)
        launch(e - 2, 2)

    @pl.when(t == 0)
    def _():
        for total in sums:
            total[...] = jnp.zeros_like(total)

    lane = lax.broadcasted_iota(jnp.int32, (1, gates.shape[1]), 1)
    gate = jnp.sum(jnp.where(lane == e, gates[...], 0.0), axis=1, keepdims=True)
    x = tokens[...]
    slot_grad = (gate * grads[...].astype(F32)).astype(BF16)
    hidden, grad_pre, one, two = expert_pass(x, slot_grad, gate, up[0], down[0])
    totals[0][t] += one
    totals[1][t] += two
    sums[0][...] += tn(x, grad_pre)
    sums[1][...] += tn(slot_grad, hidden)

    for tile in range(tiles):

        @pl.when((e == count - 1) & (t == tile))
        def _():
            for n in range(2):
                stores(n, tile).start()

    @pl.when((t == tiles - 1) & (e < count - 1))
    def _():
        slot = e % SLOTS
        pairs = [
            (work.at[slot, :, :, pl.ds(c.start, c.stop - c.start)], send.at[slot, :, :, pl.ds(c.start, c.stop - c.start)])
            for c, _ in units
        ]
        store_units(units, sums, pairs, rows)

    @pl.when((t == tiles - 1) & (e == count - 1))
    def _():
        store_units(units, sums, [raw[2 * u : 2 * u + 2] for u in range(len(units))], rows)
        close(count - 3, last_final)
        arrive(count - 2, 0)
        add(count - 2, 0)
        slot = (count - 2) % SLOTS
        for u, (c, _) in enumerate(units):
            half_done[2 * u][...] = work[slot, 0:2, :, c]
            half_done[2 * u + 1][...] = work[slot, 2:4, :, c]
        for tile in range(tiles):
            for n in range(2):
                stores(n, tile).wait()


def run_long(count, units, unit_steps, rows, gates, tokens, grads, expert_up, expert_down, sums, jobs, number):
    total, width = tokens.shape
    hidden = expert_up.shape[2]
    exchange = Exchange(jobs)
    steps = total // TILE
    tile = lambda columns: pl.BlockSpec((TILE, columns), lambda e, t: (t, 0))
    weight = lambda shape: pl.BlockSpec((1,) + shape, lambda e, t: (e, 0, 0))
    anywhere = pl.BlockSpec(memory_space=pl.ANY)
    raw = unit_shapes(units, rows, hidden)
    half_done = [jax.ShapeDtypeStruct((s.shape[0] // 2,) + s.shape[1:], BF16) for s in raw]
    final = (1, 2 * rows, hidden)
    results = pl.pallas_call(
        functools.partial(long_kernel, count, exchange, units, unit_steps, rows),
        grid=(count, steps),
        in_specs=[
            tile(gates.shape[1]),
            tile(width),
            tile(width),
            weight((width, hidden)),
            weight((hidden, width)),
            anywhere,
            anywhere,
        ]
        + exchange.in_specs,
        out_specs=[anywhere, anywhere]
        + [pl.BlockSpec(final, lambda e, t: (jnp.maximum(e - 3, 0), 0, 0)), pl.BlockSpec(final, lambda e, t: (0, 0, 0))]
        + [constant_block(shape) for shape in half_done + raw]
        + exchange.out_specs,
        out_shape=[jax.ShapeDtypeStruct((total, width), F32)] * 2
        + [jax.ShapeDtypeStruct((count - 3,) + final[1:], F32), jax.ShapeDtypeStruct(final, F32)]
        + half_done
        + raw
        + exchange.shapes,
        scratch_shapes=[pltpu.VMEM((width, hidden), F32)] * 2
        + [pltpu.VMEM((steps, TILE, width), F32)] * 2
        + [pltpu.VMEM((SLOTS, 4, 2 * rows, hidden), BF16)] * 2
        + [pltpu.VMEM((SLOTS, 4 >> n, 2 * rows, hidden), BF16) for n in range(3)]
        + [pltpu.SemaphoreType.DMA((SLOTS, 3, len(units)))] * 2
        + [pltpu.SemaphoreType.DMA((2, steps))] * 2
        + exchange.scratch,
        compiler_params=remote(exchange, number, 62),
        cost_estimate=cost(
            flops=12 * count * total * width * hidden,
            bytes_accessed=8 * count * total * width,
            transcendentals=count * total * hidden,
        ),
        name="experts_long",
    )(gates, tokens, grads, expert_up, expert_down, *sums, *exchange.operands)
    made = len(raw)
    exchange.spread(results[4 + 2 * made :])
    finished = [(results[2], n) for n in range(count - 3)] + [(results[3], 0)]
    return results[:2], finished, results[4 : 4 + made], results[4 + made : 4 + 2 * made]


def expert_grads_kernel(columns, exchange, units, rows, *refs):
    count = len(columns)
    gates, tokens, grads = refs[:3]
    saved, refs = refs[3 : 3 + 2 * count], refs[3 + 2 * count :]
    number = len(exchange.operands)
    moved, refs = refs[:number], refs[number:]
    number = sum(2 * len(own) for own in units)
    halves, refs = refs[:number], refs[number:]
    number = len(exchange.shapes)
    moved_out, refs = refs[:number], refs[number:]
    sums, refs = refs[: 2 * count], refs[2 * count :]
    step, final = pl.program_id(0), pl.num_programs(0) - 1
    exchange.bind(moved, moved_out, refs)

    @pl.when(step == 0)
    def _():
        exchange.begin()

    @pl.when(step == 1)
    def _():
        exchange.early(0, 1)

    @pl.when(step == 2)
    def _():
        exchange.early(1)

    start_sums(step, sums)
    x = tokens[...]
    g32 = grads[...].astype(F32)
    for n, column in enumerate(columns):
        slot_grad = (gates[:, column : column + 1] * g32).astype(BF16)
        sums[2 * n][...] += tn(x, saved[2 * n + 1][...])
        sums[2 * n + 1][...] += tn(slot_grad, saved[2 * n][...])
    store_halves(step, units, sums, halves, rows)

    @pl.when(step == final)
    def _():
        exchange.finish()


def run_expert_grads(columns, saved, units, rows, gates, tokens, grads, jobs, number):
    count = len(columns)
    total, width = tokens.shape
    hidden = saved[0].shape[1]
    steps = total // TILE
    shapes = [shape for own in units for shape in unit_shapes(own, rows, hidden)]
    exchange = Exchange(jobs)
    results = pl.pallas_call(
        functools.partial(expert_grads_kernel, columns, exchange, units, rows),
        grid_spec=pltpu.PrefetchScalarGridSpec(
            num_scalar_prefetch=0,
            grid=(steps,),
            in_specs=[token_tiles(gates.shape[1]), token_tiles(width), token_tiles(width)]
            + [token_tiles(hidden)] * (2 * count)
            + exchange.in_specs,
            out_specs=[constant_block(shape) for shape in shapes] + exchange.out_specs,
            scratch_shapes=[pltpu.VMEM((width, hidden), F32)] * (2 * count) + exchange.scratch,
        ),
        out_shape=shapes + exchange.shapes,
        compiler_params=remote(exchange, number, 60),
        cost_estimate=cost(
            flops=4 * count * total * width * hidden,
            bytes_accessed=(4 + 4 * count) * total * width,
            transcendentals=0,
        ),
        name="expert_grads",
    )(gates, tokens, grads, *saved, *exchange.operands)
    exchange.spread(results[len(shapes) :])
    return results[: len(shapes)]


def local(
    patches,
    conditioning,
    cotangent,
    segments,
    routes,
    gate_values,
    ada_weight,
    ada_bias,
    qkv_weight,
    out_weight,
    shared_up,
    shared_down,
    expert_up,
    expert_down,
):
    tokens, width = patches.shape
    group = routes.shape[0]
    experts = expert_up.shape[0]
    seq = segments.shape[1]
    n_dp, n_mp = lax.axis_size("dp"), lax.axis_size("mp")
    dp, mp = lax.axis_index("dp"), lax.axis_index("mp")
    rows = width // n_dp

    qkv_parts = gather_mp(jnp.transpose(qkv_weight, (1, 2, 0)).reshape(-1, width))
    out_parts = gather_mp(out_weight)

    silu_cond = jax.nn.silu(conditioning.astype(F32)).astype(BF16)
    modulation = jnp.dot(silu_cond, ada_weight, preferred_element_type=F32) + ada_bias[None, :]
    gate_two = modulation[:, 5 * width :]
    grad_mlp = (cotangent.astype(F32) * gate_two).astype(BF16)
    own_rows = tokens // seq
    own_segments = lax.dynamic_slice_in_dim(segments, mp * own_rows, own_rows, axis=0)
    number = jnp.arange(16, dtype=jnp.int32)[None, :]
    gates = jnp.sum(
        jnp.where(routes[:, :, None] == number[:, None, :], gate_values[:, :, None], 0.0), axis=1
    )
    gates = jnp.where(number == experts, 1.0, gates)
    gates = jnp.concatenate(
        [lax.dynamic_slice_in_dim(gates, (mp ^ m) * tokens, tokens, axis=0) for m in MP_ORDER],
        axis=0,
    )
    grad_mlp, qkv_parts[1], out_parts[1], gates, own_segments, silu_cond = lax.optimization_barrier(
        (grad_mlp, qkv_parts[1], out_parts[1], gates, own_segments, silu_cond)
    )
    grad_far = swap(grad_mlp, "mp", 2)

    results = run_forward(patches, modulation, own_segments, qkv_parts, out_parts)
    normed_one, qkv, attended, lse, attn_out, normed_two = results[0], results[1:5], *results[5:]

    shared = (shared_up[None], shared_down[None], 0)
    weights = {e: (expert_up, expert_down, e) for e in range(experts)}
    weights[experts] = shared
    even = halves_evenly(n_dp, rows)
    step = rows if even else width // 2
    reduced, chains, wholes = {}, {}, {}
    if even:
        near_step, far_step, *rest = dp_steps(n_dp)
        hidden = expert_up.shape[2]
        cut = hidden * 2 // 3
        unit_steps = [[near_step, far_step] + rest, [far_step, near_step] + rest]
        parts = [(slice(0, cut), unit_steps[0]), (slice(cut, hidden), unit_steps[1])]
        kinds = {c: parts for c in weights}
        kinds[experts - 2] = [(slice(0, hidden), unit_steps[1])]
        kinds[experts - 1] = [(slice(0, hidden), unit_steps[0])]
        units = {
            c: [(columns, [d for d, _ in block_order(steps)]) for columns, steps in kind]
            for c, kind in kinds.items()
        }
    else:
        units = {c: [(slice(0, expert_up.shape[2]), [0, 1])] for c in weights}

    def take_halves(columns, halves, done=0):
        halves = list(halves)
        for column in columns:
            own = [halves.pop(0) for _ in range(2 * len(units[column]))]
            if even:
                chains[column] = [
                    Chain(own[2 * u], own[2 * u + 1], steps, done)
                    for u, (_, steps) in enumerate(kinds[column])
                ]
            else:
                wholes[column] = own

    def jobs(**counts):
        if not even:
            return []
        return [(c, int(count[1:])) for count, columns in counts.items() for x in columns for c in chains[x]]

    def call(columns, sums, last, moves, number):
        return run_experts(
            columns,
            [weights[c] for c in columns],
            [units[c] for c in columns],
            step,
            gates,
            all_tokens,
            all_grads,
            sums,
            last,
            last,
            moves,
            number,
        )

    halves, sums, (all_tokens, all_grads) = run_experts(
        (experts,),
        [weights[experts]],
        [units[experts]],
        step,
        gates,
        normed_two,
        [grad_mlp, grad_far],
        None,
        False,
        False,
        [],
        0,
        True,
    )
    take_halves((experts,), halves)
    late = (experts - 2, experts - 1)
    if even:
        sums, finished, half_done, raw = run_long(
            experts - 2,
            units[0],
            unit_steps,
            rows,
            gates,
            all_tokens,
            all_grads,
            expert_up,
            expert_down,
            sums,
            jobs(n3=(experts,)),
            1,
        )
        take_halves((experts - 4,), half_done, 1)
        take_halves((experts - 3,), raw)
    else:
        for e in range(0, experts - 2, 2):
            halves, sums = call((e, e + 1), sums, False, [], 1 + e // 2)
            take_halves((e, e + 1), halves)
    saved, sums = call(late, sums, True, jobs(n1=(experts - 4, experts - 3)), 4)
    out_chain, back_chain = Chain(*sums[:2], MP_STEPS), Chain(*sums[2:], MP_STEPS)
    halves = run_expert_grads(
        late,
        saved,
        [units[c] for c in late],
        step,
        gates,
        all_tokens,
        all_grads,
        [(back_chain, 2)] + jobs(n1=(experts - 4, experts - 3)),
        5,
    )
    take_halves(late, halves)
    tail_steps = [MP_STEPS] * 3
    if even:
        y, z, rest = dp_steps(n_dp)[0], dp_steps(n_dp)[1], dp_steps(n_dp)[2:]
        core, x = MP_STEPS
        tail_steps = [[core, x, y, z] + rest, [core, y, x, z] + rest, [core, z, x, y] + rest]
    tail_orders = [block_order(steps) for steps in tail_steps]

    tail_rows = rows if even else width
    results = run_attention_back(
        patches,
        modulation,
        attn_out,
        cotangent,
        back_chain.result,
        normed_one,
        attended,
        lse,
        own_segments,
        qkv,
        qkv_parts,
        out_parts,
        tail_orders[0],
        tail_rows,
        [(out_chain, 2)] + jobs(n1=late + (experts - 3,)),
        6,
    )
    patches_grad, pieces, heads_halves = results[0], results[1], results[2:4]
    heads_chain = Chain(*heads_halves, tail_steps[0])
    split = ada_weight.shape[1] // n_mp // 2
    half = len(tail_orders[1]) // 2
    ada_chains = [
        Chain.inside((half, tail_rows + BIAS_ROWS, split), tail_steps[1]),
        Chain.inside((half, tail_rows, split), tail_steps[2]),
    ]
    number = len(tail_steps[0])
    results = run_tail(
        conditioning,
        silu_cond,
        patches,
        attn_out,
        modulation,
        cotangent,
        out_chain.result,
        pieces,
        ada_weight,
        tail_orders[1:],
        tail_rows,
        [(c, number) for c in ada_chains] + [(heads_chain, number)] + jobs(n2=late),
        7,
    )
    conditioning_grad, output, qkv_sum, out_total, ada_sum, bias_all = results[:6]
    bias_all = bias_all[: 2 * n_mp].reshape(-1)
    if even:
        moves = [(array, index, e, 0, hidden) for e, (array, index) in enumerate(finished)]
        moves += [(array[None], 0, column, 0, hidden) for column, array in zip(late, results[6:])]
        for column, own in chains.items():
            if column not in late:
                for chain, (columns, _) in zip(own, kinds[column]):
                    place = None if column == experts else column
                    moves.append((chain.result[None], 0, place, columns.start, columns.stop))
        results = run_finish(
            moves, [output, patches_grad, conditioning_grad, ada_sum], experts, rows, hidden
        )
        output, patches_grad, conditioning_grad, ada_sum = results[:4]
        expert_up_sum, expert_down_sum, up_sum, down_sum = results[4:]
    else:
        for column, (first, second) in wholes.items():
            whole = jnp.stack([first[0], second[0]]).reshape(2, 2, step, -1)
            whole = jnp.swapaxes(whole, 0, 1).reshape(2, width, -1)
            part = lax.psum_scatter(whole, "dp", scatter_dimension=1, tiled=True).astype(F32)
            reduced[column] = part[0], part[1]
        up_sum, down_sum = reduced[experts]
        expert_up_sum, expert_down_sum = [
            jnp.stack([reduced[e][part] for e in range(experts)]) for part in range(2)
        ]
        qkv_sum, out_total, ada_sum = [
            lax.psum_scatter(a.astype(BF16), "dp", scatter_dimension=0, tiled=True).astype(F32)
            for a in (qkv_sum, out_total, ada_sum)
        ]
        bias_all = lax.psum(bias_all, "dp")
    share = bias_all.shape[0] // (n_dp * n_mp)
    return (
        output,
        patches_grad,
        conditioning_grad,
        ada_sum,
        lax.dynamic_slice_in_dim(bias_all, (dp * n_mp + mp) * share, share),
        qkv_sum.reshape(rows, 3, -1),
        out_total.T,
        up_sum,
        down_sum.T,
        expert_up_sum,
        jnp.swapaxes(expert_down_sum, 1, 2),
    )


def solution(mesh):
    in_specs = (
        P(("dp", "mp"), None),
        P(("dp", "mp"), None),
        P(("dp", "mp"), None),
        P("dp", None),
        P("dp", None),
        P("dp", None),
        P(),
        P(),
        P(None, None, "mp"),
        P("mp", None),
        P(None, "mp"),
        P("mp", None),
        P(None, None, "mp"),
        P(None, "mp", None),
    )
    out_specs = (
        P(("dp", "mp"), None),
        P(("dp", "mp"), None),
        P(("dp", "mp"), None),
        P("dp", "mp"),
        P(("dp", "mp")),
        P("dp", None, "mp"),
        P("mp", "dp"),
        P("dp", "mp"),
        P("mp", "dp"),
        P(None, "dp", "mp"),
        P(None, "mp", "dp"),
    )
    return jax.shard_map(local, mesh=mesh, in_specs=in_specs, out_specs=out_specs, check_vma=False)
```
